512 devices in a mesh: dp: 16 (over y, x_hi, core), loop: 32 (over x_lo, z).
Axes of the slice: x: 4 (x_hi: 2, x_lo: 2; x = x_hi * 2 + x_lo), y: 4, z: 16, core: 2. Of those that a mesh axis runs over, the one named last changes fastest.
Arguments:
- netlist: bfloat16 [16, 16384, 512], P('dp', 'loop'), may hold values from -9 to 9
- rtl: bfloat16 [16, 16384, 512], P('dp', 'loop'), may hold values from -9 to 9
- hard_target: int32 [16, 32, 16, 1], P('dp', 'loop'), may hold values from 0 to 15; in each aligned block of 16 rows (0 to 15, 16 to 31, ..., all dimensions but the last counted through in order) at most 2 rows name the same one
- hard_block: int32 [16, 32, 16], P('dp', 'loop'), may hold values from 0 to 3
Outputs:
- row_loss: float32 [16, 16384], P('dp', 'loop')
- netlist_grad: float32 [16, 16384, 512], P('dp', 'loop')
- rtl_grad: float32 [16, 16384, 512], P('dp', 'loop')
The draws below stay inside these ranges and needn't reach their ends.
Inputs may be any that keep to these rules, and one draw needn't show every extreme that they name: `hard_target`: among the 16 entries of one tile, no group is named more than 2 times, a bound that some block reaches.
All inputs are finite; a program needn't handle non-finite values.
Results may differ from the reference program's by a relative error of at most 0.0018.
Values may be sent and summed in bfloat16 or wider, within the bound.
No kernel may reach another device: no remote copies, remote signals or barrier semaphores. Data moves between devices by JAX's collectives and lax.ppermute only.
A program may use at most 64 MiB of HBM per device.

```python
import math
import jax
import jax.numpy as jnp
import numpy as np
from jax import lax

E = 512
BLOCK = 128
BLK_DEV = 4
STEPS = 2
CAP = 2
Q = 512
PAIRS = 16384
HS = 16
N_DP = 16
N_LOOP = 32


def draw_netlist(key, part):
    noise_key = jax.random.fold_in(key, 21)
    noise = jnp.clip(jax.random.normal(noise_key, (N_DP, PAIRS, E), jnp.float32), -6.0, 6.0)
    return noise.astype(jnp.bfloat16)


def draw_rtl(key, part):
    noise_key = jax.random.fold_in(key, 37)
    noise = jnp.clip(jax.random.normal(noise_key, (N_DP, PAIRS, E), jnp.float32), -6.0, 6.0)
    return noise.astype(jnp.bfloat16)


def touch_ends(result, stream_key, smallest, largest):
    spot = [jax.random.randint(jax.random.fold_in(stream_key, axis), (), 0, length) for axis, length in enumerate(result.shape)]
    longest = result.shape.index(max(result.shape))
    neighbour = spot[:longest] + [(spot[longest] + 1) % result.shape[longest]] + spot[longest + 1:]
    return result.at[tuple(spot)].set(smallest).at[tuple(neighbour)].set(largest)


def routed_block(key, own, number, rows, amount, top, bound, slope):
    order = jax.random.permutation(key, amount)
    heavy_load, usual = portions_of(amount, rows * top, bound, slope, True), portions_of(amount, rows * top, bound, slope, False)
    places = jnp.arange(amount)

    def named(lengths, turn):
        used = int((lengths > 0).sum())
        fixed = max(1, used // 4)
        shifted = fixed + (places - fixed + turn * (used - fixed)) % max(1, amount - fixed)
        return jnp.zeros((amount,), jnp.int32).at[order[jnp.where(places < fixed, places, shifted)]].set(jnp.asarray(lengths, jnp.int32))

    lengths = jnp.where(number % 4 == 0, named(heavy_load, number // 4), named(usual, number - number // 4 - 1))
    mixed = jax.random.permutation(jax.random.fold_in(own, 3), amount)
    source_of, taker = mixed[0:amount // 2 * 2:2], mixed[1:amount // 2 * 2:2]
    room = jnp.minimum(lengths[source_of] - 1, bound - lengths[taker]) // 2
    room = jnp.where((source_of == order[0]) | (taker == order[0]) | (lengths[taker] == 0), 0, jnp.maximum(room, 0))
    shifted = jax.random.randint(jax.random.fold_in(own, 4), (amount // 2,), 0, 1 << 20) % (room + 1)
    lengths = lengths.at[source_of].add(-shifted).at[taker].add(shifted)
    labels = jnp.searchsorted(jnp.cumsum(lengths), jnp.arange(rows * top), side="right").astype(jnp.int32)
    listing = labels.reshape(top, rows).T
    listing = listing[jax.random.permutation(jax.random.fold_in(own, 1), rows)]
    turn = jax.random.randint(jax.random.fold_in(own, 2), (rows, 1), 0, top)
    return jnp.take_along_axis(listing, (jnp.arange(top)[None, :] + turn) % top, axis=1)


def portions_of(amount, total, bound, skew, full):
    weights = [(1 << 20) // math.isqrt(standing ** skew) + 1 for standing in range(1, amount + 1)]
    largest = bound if full else min(bound, max(-(-total // amount), total * weights[0] // sum(weights)))
    least = 1 if total - largest >= amount - 1 else 0
    counts, spare = [largest] + [least] * (amount - 1), total - largest - least * (amount - 1)
    while spare > 0:
        free = [i for i in range(1, amount) if counts[i] < largest] or [i for i in range(1, amount) if counts[i] < bound]
        whole, budget = sum([weights[i] for i in free]), spare
        for i in free:
            addition = min(bound - counts[i], max(1, budget * weights[i] // whole), spare)
            counts[i] = counts[i] + addition
            spare = spare - addition
    return np.array(counts)


def setup_inputs(seed: int = 0) -> dict:
    streams_of = jax.random.split(jax.random.key(seed), 5)
    netlist = draw_netlist(jax.random.fold_in(streams_of[4], 71), 0)
    rtl = draw_rtl(jax.random.fold_in(streams_of[4], 71), 0)
    hard_target_keys = jax.random.split(jax.random.fold_in(streams_of[2], 1), N_DP * N_LOOP * HS // HS)
    hard_target_turns = jax.random.permutation(jax.random.fold_in(streams_of[2], 3), N_DP * N_LOOP * HS // HS)
    hard_target = jax.vmap(lambda own, number: routed_block(jax.random.fold_in(streams_of[2], 2), own, number, HS, N_DP, 1, CAP, 2))(hard_target_keys, hard_target_turns).reshape((N_DP, N_LOOP, HS, 1))
    hard_block = touch_ends(jax.random.randint(streams_of[3], (N_DP, N_LOOP, HS), 0, BLK_DEV), jax.random.fold_in(streams_of[3], 1), 0, BLK_DEV - 1).astype(jnp.int32)
    return dict(netlist=netlist, rtl=rtl, hard_target=hard_target, hard_block=hard_block)


def slot_ranks(targets):
    count = targets.shape[-1]
    same = targets[..., :, None] == targets[..., None, :]
    earlier = jnp.arange(count)[None, :] < jnp.arange(count)[:, None]
    return lax.optimization_barrier(jnp.sum((same & earlier).astype(jnp.int32), axis=-1))

def hard_for_reader(reader, targets, ranks, picks, blocks):
    slot_ids = jnp.arange(CAP, dtype=jnp.int32)
    select = ((targets == reader)[:, :, None, :] & (ranks[:, :, None, :] == slot_ids[None, None, :, None])).astype(jnp.int32)
    chosen = lax.optimization_barrier(jnp.sum(select * picks[:, :, None, :], axis=-1))
    slot_live = lax.optimization_barrier(jnp.sum(select, axis=-1))
    hard_keys = jnp.zeros((N_DP, N_LOOP, CAP, BLOCK, E), blocks.dtype)
    for which in range(BLK_DEV):
        hard_keys = jnp.where((chosen == which)[:, :, :, None, None], blocks[:, :, which][:, :, None], hard_keys)
    hard_keys = jnp.transpose(hard_keys, (1, 0, 2, 3, 4)).reshape(N_LOOP, N_DP * CAP * BLOCK, E)
    live_rows = jnp.transpose(slot_live, (1, 0, 2))[:, :, :, None] > 0
    live_rows = jnp.broadcast_to(live_rows, (N_LOOP, N_DP, CAP, BLOCK)).reshape(N_LOOP, N_DP * CAP * BLOCK)
    return (hard_keys, live_rows)

def group_terms(queries, own_keys, hard_keys, live_rows):
    logit_scale = 3.0 / math.sqrt(E)
    cycle_keys = jnp.stack([jnp.roll(own_keys, offset, axis=0) for offset in range(STEPS + 1)], axis=1)
    cycle_keys = cycle_keys.reshape(N_LOOP, (STEPS + 1) * Q, E)
    query_wide = queries.astype(jnp.float32)
    cycle_wide = cycle_keys.astype(jnp.float32)
    hard_wide = hard_keys.astype(jnp.float32)
    cycle_scores = jnp.einsum('lqe,lke->lqk', query_wide, cycle_wide) * logit_scale
    hard_scores = jnp.einsum('lqe,lke->lqk', query_wide, hard_wide) * logit_scale
    hard_scores = jnp.where(live_rows[:, None, :], hard_scores, -jnp.inf)
    row_max = jnp.maximum(lax.optimization_barrier(jnp.max(cycle_scores, axis=-1)), lax.optimization_barrier(jnp.max(hard_scores, axis=-1)))
    cycle_exp = jnp.exp(cycle_scores - row_max[..., None])
    hard_exp = jnp.exp(hard_scores - row_max[..., None])
    row_total = lax.optimization_barrier(jnp.sum(cycle_exp, axis=-1)) + lax.optimization_barrier(jnp.sum(hard_exp, axis=-1))
    positive = lax.optimization_barrier(jnp.sum(query_wide * own_keys.astype(jnp.float32), axis=-1)) * logit_scale
    losses = row_max + jnp.log(row_total) - positive
    cycle_weight = cycle_exp / row_total[..., None]
    cycle_weight = cycle_weight.at[:, :, :Q].add(-jnp.eye(Q, dtype=jnp.float32)[None])
    cycle_weight = cycle_weight.astype(jnp.bfloat16).astype(jnp.float32)
    hard_weight = (hard_exp / row_total[..., None]).astype(jnp.bfloat16).astype(jnp.float32)
    query_grad = (jnp.einsum('lqk,lke->lqe', cycle_weight, cycle_wide) + jnp.einsum('lqk,lke->lqe', hard_weight, hard_wide)) * logit_scale
    key_grad = jnp.einsum('lqk,lqe->lke', cycle_weight, query_wide) * logit_scale
    key_grad = key_grad.reshape(N_LOOP, STEPS + 1, Q, E)
    rtl_grad = key_grad[:, 0]
    for offset in range(1, STEPS + 1):
        rtl_grad = rtl_grad + jnp.roll(key_grad[:, offset], -offset, axis=0)
    return (losses, query_grad, rtl_grad)

def reference(netlist, rtl, hard_target, hard_block):
    targets = hard_target[..., 0]
    ranks = slot_ranks(targets)
    blocks = rtl.reshape(N_DP, N_LOOP, BLK_DEV, BLOCK, E)

    def one_group(group):
        queries = lax.dynamic_index_in_dim(netlist, group, 0, keepdims=False).reshape(N_LOOP, Q, E)
        own_keys = lax.dynamic_index_in_dim(rtl, group, 0, keepdims=False).reshape(N_LOOP, Q, E)
        hard_keys, live_rows = hard_for_reader(group, targets, ranks, hard_block, blocks)
        losses, query_grad, key_grad = group_terms(queries, own_keys, hard_keys, live_rows)
        return (losses.reshape(PAIRS), query_grad.reshape(PAIRS, E), key_grad.reshape(PAIRS, E))
    row_loss, netlist_grad, rtl_grad = lax.map(one_group, jnp.arange(N_DP, dtype=jnp.int32))
    return (row_loss, netlist_grad, rtl_grad)
```

```python
import functools
import math

import jax
import jax.numpy as jnp
from jax import lax
from jax.experimental import pallas as pl
from jax.experimental.pallas import tpu as pltpu
from jax.sharding import PartitionSpec as P

BLOCK = 128
CAP = 2
CHUNK = 256
VMEM_LIMIT = 56 * 1024 * 1024


def passed_along(block, axis, distance):
    devices = range(lax.axis_size(axis))
    route = [((i - distance) % len(devices), i) for i in devices]
    return lax.ppermute(block, axis, route)


def nt_dot(a, b):
    return lax.dot_general(a, b, (((1,), (1,)), ((), ())), preferred_element_type=jnp.float32)


def whole(space=pltpu.VMEM):
    return pl.BlockSpec(memory_space=space)


def pack_kernel(entries, targets, picks, tile, out, rank_of, sems):
    for j in range(entries):
        t = targets[j]
        rank = jnp.int32(0)
        for j2 in range(j):
            rank += (targets[j2] == t).astype(jnp.int32)
        rank_of[j] = t * CAP + jnp.minimum(rank, CAP - 1)
        pltpu.make_async_copy(tile.at[picks[j]], out.at[rank_of[j]], sems.at[j]).start()
    for j in range(entries):
        pltpu.make_async_copy(tile.at[picks[j]], out.at[rank_of[j]], sems.at[j]).wait()


def pack(targets, picks, tile, groups):
    entries = targets.shape[0]
    blocks, rows, feature = tile.shape
    return pl.pallas_call(
        functools.partial(pack_kernel, entries),
        out_shape=jax.ShapeDtypeStruct((groups * CAP, rows, feature), tile.dtype),
        in_specs=[whole(pltpu.SMEM), whole(pltpu.SMEM), whole()],
        out_specs=whole(pl.ANY),
        scratch_shapes=[pltpu.SMEM((entries,), jnp.int32), pltpu.SemaphoreType.DMA((entries,))],
        name="pack",
    )(targets, picks, tile)


def cycle_kernel(scale, q_ref, k0_ref, k1_ref, k2_ref, m_ref, l_ref, pos_ref, num_ref):
    q = q_ref[...]
    rows = q.shape[0]
    first = pl.multiple_of(pl.program_id(0) * rows, rows)
    keys = [k0_ref[...], k1_ref[...], k2_ref[...]]
    scores = [nt_dot(q, k) * scale for k in keys]
    m = jnp.max(jnp.maximum(jnp.maximum(scores[0], scores[1]), scores[2]), axis=1, keepdims=True)
    exps = [jnp.exp(s - m) for s in scores]
    m_ref[...] = m
    l_ref[...] = jnp.sum(exps[0] + exps[1] + exps[2], axis=1, keepdims=True)
    num = jnp.zeros((rows, q.shape[1]), jnp.float32)
    for e, k in zip(exps, keys):
        num += jnp.dot(e.astype(jnp.bfloat16), k, preferred_element_type=jnp.float32)
    num_ref[...] = num
    own = k0_ref[pl.ds(first, rows), :].astype(jnp.float32)
    pos_ref[...] = jnp.sum(q.astype(jnp.float32) * own, axis=1, keepdims=True) * scale


def cycle_part(scale, q, k0, k1, k2, rows=256):
    n, feature = q.shape
    block = pl.BlockSpec((rows, feature), lambda i: (i, 0))
    column = pl.BlockSpec((rows, 1), lambda i: (i, 0))
    full = pl.BlockSpec((n, feature), lambda i: (0, 0))
    col = jax.ShapeDtypeStruct((n, 1), jnp.float32)
    return pl.pallas_call(
        functools.partial(cycle_kernel, scale),
        grid=(n // rows,),
        out_shape=(col, col, col, jax.ShapeDtypeStruct((n, feature), jnp.float32)),
        in_specs=[block, full, full, full],
        out_specs=(column, column, column, block),
        compiler_params=pltpu.CompilerParams(vmem_limit_bytes=VMEM_LIMIT),
        cost_estimate=pl.CostEstimate(flops=4 * n * 3 * n * feature, bytes_accessed=4 * n * feature * 2 + n * feature * 4, transcendentals=3 * n * n),
        name="cycle",
    )(q, k0, k1, k2)


def hard_kernel(scale, sources, slots, counts, q_ref, k0_ref, m_ref, l_ref, pos_ref, num_ref, blocks,
                grad_ref, loss_ref, stats_ref, keys, scores, where, sems):
    n, feature = q_ref.shape
    live = jnp.int32(0)
    per = CHUNK // BLOCK
    for g in range(sources):
        for c in range(slots):
            @pl.when(counts[g] > c)
            def _(live=live, g=g, c=c):
                pltpu.make_async_copy(blocks.at[g * slots + c], keys.at[pl.ds(live * BLOCK, BLOCK)], sems.at[live]).start()
            live += (counts[g] > c).astype(jnp.int32)
    chunks = (live + per - 1) // per

    @pl.when(live < chunks * per)
    def _():
        keys[pl.ds(pl.multiple_of(live * BLOCK, BLOCK), BLOCK), :] = jnp.zeros((BLOCK, feature), keys.dtype)

    q = q_ref[...]

    def score(i, m):
        for p in range(per):
            @pl.when(i * per + p < live)
            def _(p=p):
                pltpu.make_async_copy(blocks.at[0], keys.at[pl.ds((i * per + p) * BLOCK, BLOCK)], sems.at[i * per + p]).wait()
        k = keys[pl.ds(pl.multiple_of(i * CHUNK, CHUNK), CHUNK), :]
        s = nt_dot(q, k) * scale
        lane = lax.broadcasted_iota(jnp.int32, (n, CHUNK), 1) + i * CHUNK
        s = jnp.where(lane < live * BLOCK, s, -jnp.inf)
        scores[i] = s
        return jnp.maximum(m, jnp.maximum(s[:, :BLOCK], s[:, BLOCK:]))

    old = m_ref[...]
    wide = lax.fori_loop(0, chunks, score, jnp.broadcast_to(old, (n, BLOCK)))
    m = jnp.max(wide, axis=1, keepdims=True)
    shrink = jnp.exp(old - m)
    grad_ref[...] = num_ref[...] * shrink

    def weigh(i, l):
        e = jnp.exp(scores[i] - m)
        k = keys[pl.ds(pl.multiple_of(i * CHUNK, CHUNK), CHUNK), :]
        grad_ref[...] += jnp.dot(e.astype(jnp.bfloat16), k, preferred_element_type=jnp.float32)
        return l + (e[:, :BLOCK] + e[:, BLOCK:])

    l = lax.fori_loop(0, chunks, weigh, jnp.zeros((n, BLOCK), jnp.float32))
    total = jnp.sum(l, axis=1, keepdims=True) + l_ref[...] * shrink
    inverse = 1.0 / total
    grad_ref[...] = (grad_ref[...] * inverse - k0_ref[...].astype(jnp.float32)) * scale
    loss = m + jnp.log(total) - pos_ref[...]
    lane = lax.broadcasted_iota(jnp.int32, (n, BLOCK), 1)
    table = jnp.where(lane == 0, m, jnp.where(lane == 1, inverse, loss))
    flipped = table.T
    stats_ref[...] = flipped[:8]
    loss_ref[...] = flipped[2:3]


def hard_part(scale, counts, q, k0, m, l, pos, num, blocks):
    n, feature = q.shape
    sources = counts.shape[0]
    total = sources * CAP
    f32 = jnp.float32
    return pl.pallas_call(
        functools.partial(hard_kernel, scale, sources, CAP),
        out_shape=(jax.ShapeDtypeStruct((n, feature), f32), jax.ShapeDtypeStruct((1, n), f32), jax.ShapeDtypeStruct((8, n), f32)),
        in_specs=[whole(pltpu.SMEM)] + [whole()] * 6 + [whole(pl.ANY)],
        out_specs=(whole(), whole(), whole()),
        scratch_shapes=[
            pltpu.VMEM((total * BLOCK, feature), jnp.bfloat16),
            pltpu.VMEM((total * BLOCK // CHUNK, n, CHUNK), f32),
            pltpu.SMEM((total,), jnp.int32),
            pltpu.SemaphoreType.DMA((total,)),
        ],
        compiler_params=pltpu.CompilerParams(vmem_limit_bytes=VMEM_LIMIT),
        cost_estimate=pl.CostEstimate(flops=2 * n * total * BLOCK * feature, bytes_accessed=total * BLOCK * feature, transcendentals=n * total * BLOCK // 2),
        name="hard",
    )(counts, q, k0, m, l, pos, num, blocks)


def rtl_kernel(scale, k_ref, n0_ref, n1_ref, n2_ref, s0_ref, s1_ref, s2_ref, out_ref):
    k = k_ref[...]
    total = jnp.zeros(out_ref.shape, jnp.float32)
    for n_ref, s_ref in ((n0_ref, s0_ref), (n1_ref, s1_ref), (n2_ref, s2_ref)):
        rows = n_ref[...]
        s = nt_dot(k, rows) * scale
        w = jnp.exp(s - s_ref[0:1, :]) * s_ref[1:2, :]
        total += jnp.dot(w.astype(jnp.bfloat16), rows, preferred_element_type=jnp.float32)
    first = pl.multiple_of(pl.program_id(0) * k.shape[0], k.shape[0])
    own = n0_ref[pl.ds(first, k.shape[0]), :].astype(jnp.float32)
    out_ref[...] = (total - own) * scale


def rtl_part(scale, k, n0, n1, n2, s0, s1, s2, rows=256):
    n, feature = k.shape
    block = pl.BlockSpec((rows, feature), lambda i: (i, 0))
    full = pl.BlockSpec((n, feature), lambda i: (0, 0))
    stat = pl.BlockSpec((8, n), lambda i: (0, 0))
    return pl.pallas_call(
        functools.partial(rtl_kernel, scale),
        grid=(n // rows,),
        out_shape=jax.ShapeDtypeStruct((n, feature), jnp.float32),
        in_specs=[block, full, full, full, stat, stat, stat],
        out_specs=block,
        compiler_params=pltpu.CompilerParams(vmem_limit_bytes=VMEM_LIMIT),
        cost_estimate=pl.CostEstimate(flops=4 * n * 3 * n * feature, bytes_accessed=4 * n * feature * 2 + n * feature * 4, transcendentals=3 * n * n),
        name="rtl",
    )(k, n0, n1, n2, s0, s1, s2)


def body(netlist, rtl, hard_target, hard_block):
    queries = netlist[0]
    own_keys = rtl[0]
    row_count, feature = queries.shape
    scale = 3.0 / math.sqrt(feature)
    groups = lax.axis_size("dp")
    targets = hard_target[0, 0, :, 0]
    picks = hard_block[0, 0]

    packed = pack(targets, picks, own_keys.reshape(-1, BLOCK, feature), groups)
    arrived = lax.all_to_all(packed, "dp", split_axis=0, concat_axis=0, tiled=True)
    named = jnp.sum((targets[None, :] == jnp.arange(groups, dtype=jnp.int32)[:, None]).astype(jnp.int32), axis=1)
    counts = lax.all_to_all(named, "dp", split_axis=0, concat_axis=0, tiled=True)

    rtl1 = passed_along(own_keys, "loop", 1)
    net1 = passed_along(queries, "loop", -1)
    rtl2 = passed_along(rtl1, "loop", 1)
    net2 = passed_along(net1, "loop", -1)

    m, l, pos, num = cycle_part(scale, queries, own_keys, rtl1, rtl2)
    grad, loss, stats = hard_part(scale, counts, queries, own_keys, m, l, pos, num, arrived)
    stats1 = passed_along(stats, "loop", -1)
    stats2 = passed_along(stats, "loop", -2)
    rtl_grad = rtl_part(scale, own_keys, queries, net1, net2, stats, stats1, stats2)
    return (loss, grad[None], rtl_grad[None])


def solution(mesh):
    return jax.shard_map(
        body,
        mesh=mesh,
        in_specs=(
            P("dp", "loop", None),
            P("dp", "loop", None),
            P("dp", "loop", None, None),
            P("dp", "loop", None),
        ),
        out_specs=(P("dp", "loop"), P("dp", "loop", None), P("dp", "loop", None)),
        check_vma=False,
    )
```

```python
import functools
import math

import jax
import jax.numpy as jnp
from jax import lax
from jax.experimental import pallas as pl
from jax.experimental.pallas import tpu as pltpu
from jax.sharding import PartitionSpec as P

BLOCK = 128
CAP = 2
CHUNK = 256
VMEM_LIMIT = 28 * 1024 * 1024
ABSENT = 1024.0


def passed_along(block, axis, distance):
    devices = range(lax.axis_size(axis))
    route = [((i - distance) % len(devices), i) for i in devices]
    return lax.ppermute(block, axis, route)


def nt_dot(a, b):
    return lax.dot_general(a, b, (((1,), (1,)), ((), ())), preferred_element_type=jnp.float32)


def whole(space=pltpu.VMEM):
    return pl.BlockSpec(memory_space=space)


def pack_kernel(entries, me, targets, picks, tile, out, place, used, mark, sems, mark_sems):
    column = (me[0] >> 1) & 1
    slots = out.shape[0]
    mark[...] = jnp.full(mark.shape, ABSENT, mark.dtype)
    for s in range(slots):
        used[s] = 0
    for j in range(entries):
        t = targets[j]
        rank = jnp.int32(0)
        for j2 in range(j):
            rank += (targets[j2] == t).astype(jnp.int32)
        slot = ((t >> 2) * 2 + (t & 1)) * CAP + jnp.minimum(rank, CAP - 1)
        place[j] = jnp.where(((t >> 1) & 1) == column, slot, -1)

        @pl.when(place[j] >= 0)
        def _(j=j):
            used[place[j]] = 1
            pltpu.make_async_copy(tile.at[picks[j]], out.at[place[j]], sems.at[j]).start()

    rows, lanes = mark.shape
    for s in range(slots):
        @pl.when(used[s] == 0)
        def _(s=s):
            pltpu.make_async_copy(mark, out.at[s, pl.ds(0, rows), pl.ds(0, lanes)], mark_sems.at[s]).start()

    for j in range(entries):
        @pl.when(place[j] >= 0)
        def _(j=j):
            pltpu.make_async_copy(tile.at[picks[j]], out.at[place[j]], sems.at[j]).wait()

    for s in range(slots):
        @pl.when(used[s] == 0)
        def _(s=s):
            pltpu.make_async_copy(mark, out.at[s, pl.ds(0, rows), pl.ds(0, lanes)], mark_sems.at[s]).wait()


def pack(me, targets, picks, tile, places):
    entries = targets.shape[0]
    blocks, rows, feature = tile.shape
    slots = places * CAP
    return pl.pallas_call(
        functools.partial(pack_kernel, entries),
        out_shape=jax.ShapeDtypeStruct((slots, rows, feature), tile.dtype),
        in_specs=[whole(pltpu.SMEM)] * 3 + [whole()],
        out_specs=whole(pl.ANY),
        scratch_shapes=[
            pltpu.SMEM((entries,), jnp.int32),
            pltpu.SMEM((slots,), jnp.int32),
            pltpu.VMEM((16, 128), tile.dtype),
            pltpu.SemaphoreType.DMA((entries,)),
            pltpu.SemaphoreType.DMA((slots,)),
        ],
        compiler_params=pltpu.CompilerParams(vmem_limit_bytes=4 * 1024 * 1024),
        name="pack",
    )(me, targets, picks, tile)


def cycle_kernel(rate, q_ref, k0_ref, k1_ref, k2_ref, m_ref, l_ref, num_ref):
    q = q_ref[...]
    rows = q.shape[0]
    keys = [k0_ref[...], k1_ref[...], k2_ref[...]]
    scores = [nt_dot(q, k) for k in keys]
    m = jnp.max(jnp.maximum(jnp.maximum(scores[0], scores[1]), scores[2]), axis=1, keepdims=True)
    exps = [jnp.exp2((s - m) * rate) for s in scores]
    m_ref[...] = m
    l_ref[...] = jnp.sum(exps[0] + exps[1] + exps[2], axis=1, keepdims=True)
    num = jnp.zeros((rows, q.shape[1]), jnp.float32)
    for e, k in zip(exps, keys):
        num += jnp.dot(e.astype(jnp.bfloat16), k, preferred_element_type=jnp.float32)
    num_ref[...] = num


def cycle_part(rate, q, k0, k1, k2, rows=256):
    n, feature = q.shape
    block = pl.BlockSpec((rows, feature), lambda i: (i, 0))
    column = pl.BlockSpec((rows, 1), lambda i: (i, 0))
    full = pl.BlockSpec((n, feature), lambda i: (0, 0))
    col = jax.ShapeDtypeStruct((n, 1), jnp.float32)
    return pl.pallas_call(
        functools.partial(cycle_kernel, rate),
        grid=(n // rows,),
        out_shape=(col, col, jax.ShapeDtypeStruct((n, feature), jnp.float32)),
        in_specs=[block, full, full, full],
        out_specs=(column, column, block),
        compiler_params=pltpu.CompilerParams(vmem_limit_bytes=VMEM_LIMIT),
        cost_estimate=pl.CostEstimate(flops=4 * n * 3 * n * feature, bytes_accessed=4 * n * feature * 2 + n * feature * 4, transcendentals=3 * n * n),
        name="cycle",
    )(q, k0, k1, k2)


def hard_kernel(rate, scale, last, q_ref, k0_ref, m_ref, l_ref, num_ref, blocks, *rest):
    if last:
        num_out, loss_ref, stats_ref, scores, order = rest
    else:
        num_out, m_out, l_out, scores, order = rest
    n, feature = q_ref.shape
    slots = blocks.shape[0]
    per = CHUNK // BLOCK
    order[0] = 0
    live = jnp.int32(0)
    for s in range(slots):
        there = jnp.max(blocks[s, :16, :128].astype(jnp.float32)) < ABSENT / 2
        order[live] = s
        live += there.astype(jnp.int32)
    odd = (live & 1) == 1
    chunks = (live + 1) >> 1

    @pl.when(odd)
    def _():
        order[live] = order[live - 1]

    q = q_ref[...]

    def chunk_keys(i):
        return jnp.concatenate([blocks[order[i * per + p]] for p in range(per)], axis=0)

    def score(i, m):
        s = nt_dot(q, chunk_keys(i))
        scores[i] = s
        return jnp.maximum(m, jnp.maximum(s[:, :BLOCK], s[:, BLOCK:]))

    old = m_ref[...]
    wide = lax.fori_loop(0, chunks, score, jnp.broadcast_to(old, (n, BLOCK)))
    m = jnp.max(wide, axis=1, keepdims=True)
    shrink = jnp.exp2((old - m) * rate)
    num_out[...] = num_ref[...] * shrink

    @pl.when(odd)
    def _():
        scores[chunks - 1, :, BLOCK:] = jnp.full((n, BLOCK), -jnp.inf, jnp.float32)

    def weigh(i, l):
        e = jnp.exp2((scores[i] - m) * rate)
        num_out[...] += jnp.dot(e.astype(jnp.bfloat16), chunk_keys(i), preferred_element_type=jnp.float32)
        return l + (e[:, :BLOCK] + e[:, BLOCK:])

    l = lax.fori_loop(0, chunks, weigh, jnp.zeros((n, BLOCK), jnp.float32))
    total = jnp.sum(l, axis=1, keepdims=True) + l_ref[...] * shrink
    if not last:
        m_out[...] = m
        l_out[...] = total
        return
    inverse = 1.0 / total
    own = k0_ref[...].astype(jnp.float32)
    num_out[...] = (num_out[...] * inverse - own) * scale
    positive = jnp.sum(q.astype(jnp.float32) * own, axis=1, keepdims=True)
    loss = (m - positive) * scale + jnp.log(total)
    lane = lax.broadcasted_iota(jnp.int32, (n, BLOCK), 1)
    table = jnp.where(lane == 0, m, jnp.where(lane == 1, inverse, loss))
    flipped = table.T
    stats_ref[...] = flipped[:8]
    loss_ref[...] = flipped[2:3]


def hard_part(rate, scale, last, q, k0, m, l, num, blocks):
    n, feature = q.shape
    slots = blocks.shape[0]
    f32 = jnp.float32
    col = jax.ShapeDtypeStruct((n, 1), f32)
    ends = (jax.ShapeDtypeStruct((1, n), f32), jax.ShapeDtypeStruct((8, n), f32)) if last else (col, col)
    keys = slots * BLOCK
    return pl.pallas_call(
        functools.partial(hard_kernel, rate, scale, last),
        out_shape=(jax.ShapeDtypeStruct((n, feature), f32),) + ends,
        in_specs=[whole()] * 6,
        out_specs=(whole(), whole(), whole()),
        scratch_shapes=[pltpu.VMEM((keys // CHUNK, n, CHUNK), f32), pltpu.SMEM((slots + 1,), jnp.int32)],
        compiler_params=pltpu.CompilerParams(vmem_limit_bytes=VMEM_LIMIT),
        cost_estimate=pl.CostEstimate(flops=2 * n * keys * feature, bytes_accessed=2 * keys * feature, transcendentals=n * keys // 2),
        name="hard_last" if last else "hard_first",
    )(q, k0, m, l, num, blocks)


def rtl_kernel(rate, scale, k_ref, n0_ref, n1_ref, n2_ref, s0_ref, s1_ref, s2_ref, out_ref):
    k = k_ref[...]
    total = jnp.zeros(out_ref.shape, jnp.float32)
    for n_ref, s_ref in ((n0_ref, s0_ref), (n1_ref, s1_ref), (n2_ref, s2_ref)):
        rows = n_ref[...]
        s = nt_dot(k, rows)
        w = jnp.exp2((s - s_ref[0:1, :]) * rate) * s_ref[1:2, :]
        total += jnp.dot(w.astype(jnp.bfloat16), rows, preferred_element_type=jnp.float32)
    first = pl.multiple_of(pl.program_id(0) * k.shape[0], k.shape[0])
    own = n0_ref[pl.ds(first, k.shape[0]), :].astype(jnp.float32)
    out_ref[...] = (total - own) * scale


def rtl_part(rate, scale, k, n0, n1, n2, s0, s1, s2, rows=256):
    n, feature = k.shape
    block = pl.BlockSpec((rows, feature), lambda i: (i, 0))
    full = pl.BlockSpec((n, feature), lambda i: (0, 0))
    stat = pl.BlockSpec((8, n), lambda i: (0, 0))
    return pl.pallas_call(
        functools.partial(rtl_kernel, rate, scale),
        grid=(n // rows,),
        out_shape=jax.ShapeDtypeStruct((n, feature), jnp.float32),
        in_specs=[block, full, full, full, stat, stat, stat],
        out_specs=block,
        compiler_params=pltpu.CompilerParams(vmem_limit_bytes=VMEM_LIMIT),
        cost_estimate=pl.CostEstimate(flops=4 * n * 3 * n * feature, bytes_accessed=4 * n * feature * 2 + n * feature * 4, transcendentals=3 * n * n),
        name="rtl",
    )(k, n0, n1, n2, s0, s1, s2)


def body(netlist, rtl, hard_target, hard_block):
    queries = netlist[0]
    own_keys = rtl[0]
    row_count, feature = queries.shape
    scale = 3.0 / math.sqrt(feature)
    rate = scale * math.log2(math.e)
    groups = lax.axis_size("dp")
    me = lax.axis_index("dp")
    targets = hard_target[0, 0, :, 0]
    picks = hard_block[0, 0]
    entries = targets.shape[0]
    columns = [[g for g in range(groups) if (g // 2) % 2 == x] for x in range(2)]
    places = groups // 2

    def spread(packed):
        return lax.all_to_all(packed, "dp", split_axis=0, concat_axis=0, axis_index_groups=columns, tiled=True)

    at = jnp.full((1,), me, jnp.int32)
    swap = [(g, g ^ 2) for g in range(groups)]
    packed = pack(at, targets, picks, own_keys.reshape(-1, BLOCK, feature), places)
    first = spread(packed)
    partner = lax.ppermute(own_keys, "dp", swap)
    theirs = lax.ppermute(jnp.concatenate([targets, picks]), "dp", swap)
    rtl1 = passed_along(own_keys, "loop", 1)
    net1 = passed_along(queries, "loop", -1)
    partner, theirs, rtl1, net1 = lax.optimization_barrier((partner, theirs, rtl1, net1))
    second = spread(pack(at, theirs[:entries], theirs[entries:], partner.reshape(-1, BLOCK, feature), places))
    rtl2 = passed_along(rtl1, "loop", 1)
    net2 = passed_along(net1, "loop", -1)

    m, l, num = cycle_part(rate, queries, own_keys, rtl1, rtl2)
    num, m, l = hard_part(rate, scale, False, queries, own_keys, m, l, num, first)
    grad, loss, stats = hard_part(rate, scale, True, queries, own_keys, m, l, num, second)
    stats1 = passed_along(stats, "loop", -1)
    stats2 = passed_along(stats, "loop", -2)
    rtl_grad = rtl_part(rate, scale, own_keys, queries, net1, net2, stats, stats1, stats2)
    return (loss, grad[None], rtl_grad[None])


def solution(mesh):
    return jax.shard_map(
        body,
        mesh=mesh,
        in_specs=(
            P("dp", "loop", None),
            P("dp", "loop", None),
            P("dp", "loop", None, None),
            P("dp", "loop", None),
        ),
        out_specs=(P("dp", "loop"), P("dp", "loop", None), P("dp", "loop", None)),
        check_vma=False,
    )
```

```python
import functools
import math

import jax
import jax.numpy as jnp
from jax import lax
from jax.experimental import pallas as pl
from jax.experimental.pallas import tpu as pltpu
from jax.sharding import PartitionSpec as P

BLOCK = 128
CAP = 2
CHUNK = 256
VMEM_LIMIT = 28 * 1024 * 1024
BIG_GRANT = 60 * 1024 * 1024
ABSENT = 1024.0
LANES = 128


def passed_along(block, axis, distance):
    devices = range(lax.axis_size(axis))
    route = [((i - distance) % len(devices), i) for i in devices]
    return lax.ppermute(block, axis, route)


def nt_dot(a, b):
    return lax.dot_general(a, b, (((1,), (1,)), ((), ())), preferred_element_type=jnp.float32)


def whole(space=pltpu.VMEM):
    return pl.BlockSpec(memory_space=space)


def shared(slots, entries, out, tile, place, used, seen, mark, sems, mark_sems, column, target_of, pick_of):
    mark[...] = jnp.full(mark.shape, ABSENT, mark.dtype)
    for s in range(slots):
        used[s] = 0
        seen[s] = 0
    for j in range(entries):
        t = target_of(j)
        rank = seen[t]
        seen[t] = rank + 1
        slot = ((t >> 2) * 2 + (t & 1)) * CAP + jnp.minimum(rank, CAP - 1)
        place[j] = jnp.where(((t >> 1) & 1) == column, slot, -1)

        @pl.when(place[j] >= 0)
        def _(j=j):
            used[place[j]] = 1
            pltpu.make_async_copy(tile.at[pick_of(j)], out.at[place[j]], sems.at[j]).start()

    rows, lanes = mark.shape
    for s in range(slots):
        @pl.when(used[s] == 0)
        def _(s=s):
            pltpu.make_async_copy(mark, out.at[s, pl.ds(0, rows), pl.ds(0, lanes)], mark_sems.at[s]).start()

    def finish():
        for j in range(entries):
            @pl.when(place[j] >= 0)
            def _(j=j):
                pltpu.make_async_copy(tile.at[pick_of(j)], out.at[place[j]], sems.at[j]).wait()

        for s in range(slots):
            @pl.when(used[s] == 0)
            def _(s=s):
                pltpu.make_async_copy(mark, out.at[s, pl.ds(0, rows), pl.ds(0, lanes)], mark_sems.at[s]).wait()

    return finish


def own_kernel(entries, me, targets, picks, rtl, out, mail, target_s, pick_s, tile, head, place, used, seen, mark, sems, mark_sems, in_sems):
    lists = [pltpu.make_async_copy(targets, target_s, in_sems.at[0]), pltpu.make_async_copy(picks, pick_s, in_sems.at[1])]
    load = pltpu.make_async_copy(rtl, tile, in_sems.at[2])
    for copy in lists + [load]:
        copy.start()
    for copy in lists:
        copy.wait()
    load.wait()
    blocks = tile.shape[0]
    store = pltpu.make_async_copy(tile, mail.at[pl.ds(0, blocks)], in_sems.at[3])
    store.start()
    column = (me[0] >> 1) & 1
    finish = shared(out.shape[0], entries, out, tile, place, used, seen, mark, sems, mark_sems, column, lambda j: target_s[j], lambda j: pick_s[j])
    lane = lax.broadcasted_iota(jnp.int32, head.shape, 1)
    line = jnp.zeros(head.shape, jnp.int32)
    for j in range(entries):
        line = jnp.where(lane == j, target_s[j], line)
        line = jnp.where(lane == entries + j, pick_s[j], line)
    head[...] = line.astype(jnp.float32).astype(head.dtype)
    rows, lanes = head.shape
    note = pltpu.make_async_copy(head, mail.at[blocks, pl.ds(0, rows), pl.ds(0, lanes)], in_sems.at[4])
    note.start()
    finish()
    store.wait()
    note.wait()


def pack_own(me, targets, picks, tile, places):
    entries = targets.shape[0]
    blocks, rows, feature = tile.shape
    slots = places * CAP
    hbm = whole(pltpu.HBM)
    return pl.pallas_call(
        functools.partial(own_kernel, entries),
        out_shape=(jax.ShapeDtypeStruct((slots, rows, feature), tile.dtype), jax.ShapeDtypeStruct((blocks + 1, rows, feature), tile.dtype)),
        in_specs=[whole(pltpu.SMEM), hbm, hbm, hbm],
        out_specs=(hbm, hbm),
        scratch_shapes=[
            pltpu.SMEM((entries,), jnp.int32),
            pltpu.SMEM((entries,), jnp.int32),
            pltpu.VMEM(tile.shape, tile.dtype),
            pltpu.VMEM((16, 128), tile.dtype),
            pltpu.SMEM((entries,), jnp.int32),
            pltpu.SMEM((slots,), jnp.int32),
            pltpu.SMEM((slots,), jnp.int32),
            pltpu.VMEM((16, 128), tile.dtype),
            pltpu.SemaphoreType.DMA((entries,)),
            pltpu.SemaphoreType.DMA((slots,)),
            pltpu.SemaphoreType.DMA((5,)),
        ],
        compiler_params=pltpu.CompilerParams(vmem_limit_bytes=BIG_GRANT),
        name="pack_own",
    )(me, targets, picks, tile)


def far_kernel(entries, me, mail, out, list_v, list_s, tile, head, place, used, seen, mark, sems, mark_sems, in_sems):
    blocks = tile.shape[0]
    rows, lanes = head.shape
    note = pltpu.make_async_copy(mail.at[blocks, pl.ds(0, rows), pl.ds(0, lanes)], head, in_sems.at[0])
    load = pltpu.make_async_copy(mail.at[pl.ds(0, blocks)], tile, in_sems.at[1])
    note.start()
    load.start()
    note.wait()
    list_v[...] = head[...].astype(jnp.float32)[:8].astype(jnp.int32)
    down = pltpu.make_async_copy(list_v, list_s, in_sems.at[2])
    down.start()
    down.wait()
    load.wait()
    column = (me[0] >> 1) & 1
    shared(out.shape[0], entries, out, tile, place, used, seen, mark, sems, mark_sems, column, lambda j: list_s[0, j], lambda j: list_s[0, entries + j])()


def pack_far(me, mail, places, entries):
    blocks, rows, feature = mail.shape
    slots = places * CAP
    hbm = whole(pltpu.HBM)
    return pl.pallas_call(
        functools.partial(far_kernel, entries),
        out_shape=jax.ShapeDtypeStruct((slots, rows, feature), mail.dtype),
        in_specs=[whole(pltpu.SMEM), hbm],
        out_specs=hbm,
        scratch_shapes=[
            pltpu.VMEM((8, 128), jnp.int32),
            pltpu.SMEM((8, 128), jnp.int32),
            pltpu.VMEM((blocks - 1, rows, feature), mail.dtype),
            pltpu.VMEM((16, 128), mail.dtype),
            pltpu.SMEM((entries,), jnp.int32),
            pltpu.SMEM((slots,), jnp.int32),
            pltpu.SMEM((slots,), jnp.int32),
            pltpu.VMEM((16, 128), mail.dtype),
            pltpu.SemaphoreType.DMA((entries,)),
            pltpu.SemaphoreType.DMA((slots,)),
            pltpu.SemaphoreType.DMA((3,)),
        ],
        compiler_params=pltpu.CompilerParams(vmem_limit_bytes=BIG_GRANT),
        name="pack_far",
    )(me, mail)


def cycle_kernel(rate, tiles, q_ref, *refs):
    q = q_ref[...]
    rows, feature = q.shape
    keys = [ref[...] for ref in refs[:tiles]]
    state_in, state_ref = (None, refs[tiles]) if len(refs) == tiles + 1 else refs[tiles:]
    scores = [nt_dot(q, k) for k in keys]
    m = jnp.max(functools.reduce(jnp.maximum, scores), axis=1, keepdims=True)
    if state_in is not None:
        old = state_in[:, feature : feature + 1]
        m = jnp.maximum(m, old)
    exps = [jnp.exp2((s - m) * rate) for s in scores]
    l = jnp.sum(functools.reduce(jnp.add, exps), axis=1, keepdims=True)
    num = jnp.zeros((rows, feature), jnp.float32)
    if state_in is not None:
        shrink = jnp.exp2((old - m) * rate)
        l += state_in[:, feature + 1 : feature + 2] * shrink
        num = state_in[:, :feature] * shrink
    for e, k in zip(exps, keys):
        num += jnp.dot(e.astype(jnp.bfloat16), k, preferred_element_type=jnp.float32)
    state_ref[:, :feature] = num
    lane = lax.broadcasted_iota(jnp.int32, (rows, LANES), 1)
    state_ref[:, feature:] = jnp.where(lane == 0, m, l)


def cycle_part(rate, q, keys, states, rows=256):
    n, feature = q.shape
    tiles = len(keys)
    block = pl.BlockSpec((rows, feature), lambda i: (i, 0))
    wide = pl.BlockSpec((rows, feature + LANES), lambda i: (i, 0))
    full = pl.BlockSpec((n, feature), lambda i: (0, 0))
    return pl.pallas_call(
        functools.partial(cycle_kernel, rate, tiles),
        grid=(n // rows,),
        out_shape=jax.ShapeDtypeStruct((n, feature + LANES), jnp.float32),
        in_specs=[block] + [full] * tiles + [wide] * len(states),
        out_specs=wide,
        compiler_params=pltpu.CompilerParams(vmem_limit_bytes=VMEM_LIMIT),
        cost_estimate=pl.CostEstimate(flops=4 * n * tiles * n * feature, bytes_accessed=(tiles + 3) * n * feature * 2, transcendentals=tiles * n * n),
        name="cycle_more" if states else "cycle",
    )(q, *keys, *states)


def hard_kernel(rate, scale, last, q_ref, k0_ref, state_in, blocks, *rest):
    if last:
        num, loss_ref, stats_ref, state, keys, scores, order, sems, state_sem = rest
    else:
        state_out, state, keys, scores, order, sems, state_sem = rest
    n, feature = q_ref.shape
    slots = blocks.shape[0]
    loads = [pltpu.make_async_copy(blocks.at[s], keys.at[s], sems.at[s]) for s in range(slots)]
    for load in loads:
        load.start()
    restore = pltpu.make_async_copy(state_in, state, state_sem.at[0])
    restore.start()
    live = jnp.int32(0)
    for s in range(slots):
        loads[s].wait()
        there = jnp.max(keys[s, :16, :128].astype(jnp.float32)) < ABSENT / 2
        order[live] = s
        live += there.astype(jnp.int32)
    odd = (live & 1) == 1
    pairs = (live + 1) >> 1
    fours = pairs >> 1
    single = (pairs & 1) == 1

    @pl.when(odd)
    def _():
        order[live] = order[live - 1]

    q = q_ref[...]

    def some_keys(pair, count):
        return jnp.concatenate([keys[order[pair * 2 + p]] for p in range(2 * count)], axis=0)

    def score(pair, count, m):
        s = nt_dot(q, some_keys(pair, count))
        for c in range(count):
            scores[pair + c] = s[:, c * CHUNK : (c + 1) * CHUNK]
        for c in range(2 * count):
            m = jnp.maximum(m, s[:, c * BLOCK : (c + 1) * BLOCK])
        return m

    wide = lax.fori_loop(0, fours, lambda i, m: score(2 * i, 2, m), jnp.full((n, BLOCK), -jnp.inf, jnp.float32))
    wide = lax.fori_loop(2 * fours, pairs, lambda i, m: score(i, 1, m), wide)
    restore.wait()
    old = state[:, feature : feature + 1]
    m = jnp.maximum(jnp.max(wide, axis=1, keepdims=True), old)
    shrink = jnp.exp2((old - m) * rate)
    kept = state[:, feature + 1 : feature + 2] * shrink
    if not last:
        num = state.at[:, pl.ds(0, feature)]
    num[...] = state[:, :feature] * shrink

    @pl.when(odd)
    def _():
        scores[pairs - 1, :, BLOCK:] = jnp.full((n, BLOCK), -jnp.inf, jnp.float32)

    def weigh(pair, count, l):
        parts = [jnp.exp2((scores[pair + c] - m) * rate) for c in range(count)]
        e = parts[0] if count == 1 else jnp.concatenate(parts, axis=1)
        num[...] += jnp.dot(e.astype(jnp.bfloat16), some_keys(pair, count), preferred_element_type=jnp.float32)
        for part in parts:
            l = l + (part[:, :BLOCK] + part[:, BLOCK:])
        return l

    l = lax.fori_loop(0, fours, lambda i, l: weigh(2 * i, 2, l), jnp.zeros((n, BLOCK), jnp.float32))
    l = lax.fori_loop(2 * fours, pairs, lambda i, l: weigh(i, 1, l), l)
    total = jnp.sum(l, axis=1, keepdims=True) + kept
    lane = lax.broadcasted_iota(jnp.int32, (n, LANES), 1)
    if not last:
        state[:, feature:] = jnp.where(lane == 0, m, total)
        save = pltpu.make_async_copy(state, state_out, state_sem.at[0])
        save.start()
        save.wait()
        return
    inverse = 1.0 / total
    own = k0_ref[...].astype(jnp.float32)
    num[...] = (num[...] * inverse - own) * scale
    positive = jnp.sum(q.astype(jnp.float32) * own, axis=1, keepdims=True)
    loss = (m - positive) * scale + jnp.log(total)
    table = jnp.where(lane == 0, m, jnp.where(lane == 1, inverse, loss))
    flipped = table.T
    stats_ref[...] = flipped[:8]
    loss_ref[...] = flipped[2:3]


def hard_part(rate, scale, last, q, k0, state, blocks):
    n, feature = q.shape
    slots = blocks.shape[0]
    f32 = jnp.float32
    shapes = [jax.ShapeDtypeStruct(state.shape, f32)]
    specs = [whole(pltpu.HBM)]
    if last:
        shapes = [jax.ShapeDtypeStruct((n, feature), f32), jax.ShapeDtypeStruct((1, n), f32), jax.ShapeDtypeStruct((8, n), f32)]
        specs = [whole()] * 3
    keys = slots * BLOCK
    return pl.pallas_call(
        functools.partial(hard_kernel, rate, scale, last),
        out_shape=shapes,
        in_specs=[whole(), whole(), whole(pl.ANY), whole(pl.ANY)],
        out_specs=specs,
        scratch_shapes=[
            pltpu.VMEM(state.shape, f32),
            pltpu.VMEM(blocks.shape, blocks.dtype),
            pltpu.VMEM((keys // CHUNK, n, CHUNK), f32),
            pltpu.SMEM((slots + 1,), jnp.int32),
            pltpu.SemaphoreType.DMA((slots,)),
            pltpu.SemaphoreType.DMA((1,)),
        ],
        compiler_params=pltpu.CompilerParams(vmem_limit_bytes=BIG_GRANT),
        cost_estimate=pl.CostEstimate(flops=2 * n * keys * feature, bytes_accessed=2 * keys * feature, transcendentals=n * keys // 2),
        name="hard_last" if last else "hard_first",
    )(q, k0, state, blocks)


def rtl_kernel(rate, scale, tiles, k_ref, *refs):
    n_refs, s_refs = refs[:tiles], refs[tiles : 2 * tiles]
    base_ref, out_ref = refs[2 * tiles :]
    k = k_ref[...]
    total = -base_ref[...].astype(jnp.float32) if tiles == 1 else base_ref[...]
    for n_ref, s_ref in zip(n_refs, s_refs):
        rows = n_ref[...]
        s = nt_dot(k, rows)
        w = jnp.exp2((s - s_ref[0:1, :]) * rate) * s_ref[1:2, :]
        total += jnp.dot(w.astype(jnp.bfloat16), rows, preferred_element_type=jnp.float32)
    out_ref[...] = total if tiles == 1 else total * scale


def rtl_part(rate, scale, k, nets, stats, base, rows=256):
    n, feature = k.shape
    tiles = len(nets)
    block = pl.BlockSpec((rows, feature), lambda i: (i, 0))
    full = pl.BlockSpec((n, feature), lambda i: (0, 0))
    stat = pl.BlockSpec((8, n), lambda i: (0, 0))
    return pl.pallas_call(
        functools.partial(rtl_kernel, rate, scale, tiles),
        grid=(n // rows,),
        out_shape=jax.ShapeDtypeStruct((n, feature), jnp.float32),
        in_specs=[block] + [full] * tiles + [stat] * tiles + [block],
        out_specs=block,
        compiler_params=pltpu.CompilerParams(vmem_limit_bytes=VMEM_LIMIT),
        cost_estimate=pl.CostEstimate(flops=4 * n * tiles * n * feature, bytes_accessed=(tiles + 3) * n * feature * 2, transcendentals=tiles * n * n),
        name="rtl_own" if tiles == 1 else "rtl_others",
    )(k, *nets, *stats, base)


def body(netlist, rtl, hard_target, hard_block):
    queries = netlist[0]
    own_keys = rtl[0]
    feature = queries.shape[1]
    scale = 3.0 / math.sqrt(feature)
    rate = scale * math.log2(math.e)
    groups = lax.axis_size("dp")
    targets = hard_target[0, 0, :, 0]
    picks = hard_block[0, 0]
    columns = [[g for g in range(groups) if (g // 2) % 2 == x] for x in range(2)]
    places = groups // 2

    def spread(packed):
        return lax.all_to_all(packed, "dp", split_axis=0, concat_axis=0, axis_index_groups=columns, tiled=True)

    at = jnp.full((1,), lax.axis_index("dp"), jnp.int32)
    packed, mail = pack_own(at, targets, picks, own_keys.reshape(-1, BLOCK, feature), places)
    first = spread(packed)
    mail = lax.ppermute(mail, "dp", [(g, g ^ 2) for g in range(groups)])
    rtl1 = passed_along(own_keys, "loop", 1)
    net1 = passed_along(queries, "loop", -1)
    rtl2 = passed_along(own_keys, "loop", 2)
    net2 = passed_along(queries, "loop", -2)
    mail, rtl1, net1 = lax.optimization_barrier((mail, rtl1, net1))
    second = spread(pack_far(at, mail, places, targets.shape[0]))

    state = cycle_part(rate, queries, [own_keys, rtl1], [])
    (state,) = hard_part(rate, scale, False, queries, own_keys, state, first)
    state = cycle_part(rate, queries, [rtl2], [state])
    grad, loss, stats = hard_part(rate, scale, True, queries, own_keys, state, second)
    stats1 = passed_along(stats, "loop", -1)
    stats2 = passed_along(stats, "loop", -2)
    begun = rtl_part(rate, scale, own_keys, [queries], [stats], queries)
    rtl_grad = rtl_part(rate, scale, own_keys, [net1, net2], [stats1, stats2], begun)
    return (loss, grad[None], rtl_grad[None])


def solution(mesh):
    return jax.shard_map(
        body,
        mesh=mesh,
        in_specs=(
            P("dp", "loop", None),
            P("dp", "loop", None),
            P("dp", "loop", None, None),
            P("dp", "loop", None),
        ),
        out_specs=(P("dp", "loop"), P("dp", "loop", None), P("dp", "loop", None)),
        check_vma=False,
    )
```

```python
import functools
import math

import jax
import jax.numpy as jnp
from jax import lax
from jax.experimental import pallas as pl
from jax.experimental.pallas import tpu as pltpu
from jax.sharding import PartitionSpec as P

BLOCK = 128
CAP = 2
CHUNK = 512
VMEM_LIMIT = 28 * 1024 * 1024
BIG_GRANT = 60 * 1024 * 1024
ABSENT = 1024.0
LANES = 128


def passed_along(block, axis, distance):
    devices = range(lax.axis_size(axis))
    route = [((i - distance) % len(devices), i) for i in devices]
    return lax.ppermute(block, axis, route)


def nt_dot(a, b):
    return lax.dot_general(a, b, (((1,), (1,)), ((), ())), preferred_element_type=jnp.float32)


def whole(space=pltpu.VMEM):
    return pl.BlockSpec(memory_space=space)


def shared(slots, entries, out, tile, place, used, seen, mark, sems, mark_sems, column, target_of, pick_of):
    mark[...] = jnp.full(mark.shape, ABSENT, mark.dtype)
    for s in range(slots):
        used[s] = 0
        seen[s] = 0
    for j in range(entries):
        t = target_of(j)
        rank = seen[t]
        seen[t] = rank + 1
        slot = ((t >> 2) * 2 + (t & 1)) * CAP + jnp.minimum(rank, CAP - 1)
        place[j] = jnp.where(((t >> 1) & 1) == column, slot, -1)

        @pl.when(place[j] >= 0)
        def _(j=j):
            used[place[j]] = 1
            pltpu.make_async_copy(tile.at[pick_of(j)], out.at[place[j]], sems.at[j]).start()

    rows, lanes = mark.shape
    for s in range(slots):
        @pl.when(used[s] == 0)
        def _(s=s):
            pltpu.make_async_copy(mark, out.at[s, pl.ds(0, rows), pl.ds(0, lanes)], mark_sems.at[s]).start()

    def finish():
        for j in range(entries):
            @pl.when(place[j] >= 0)
            def _(j=j):
                pltpu.make_async_copy(tile.at[pick_of(j)], out.at[place[j]], sems.at[j]).wait()

        for s in range(slots):
            @pl.when(used[s] == 0)
            def _(s=s):
                pltpu.make_async_copy(mark, out.at[s, pl.ds(0, rows), pl.ds(0, lanes)], mark_sems.at[s]).wait()

    return finish


def own_kernel(entries, me, targets, picks, rtl, out, mail, target_s, pick_s, tile, head, place, used, seen, mark, sems, mark_sems, in_sems):
    lists = [pltpu.make_async_copy(targets, target_s, in_sems.at[0]), pltpu.make_async_copy(picks, pick_s, in_sems.at[1])]
    load = pltpu.make_async_copy(rtl, tile, in_sems.at[2])
    for copy in lists + [load]:
        copy.start()
    for copy in lists:
        copy.wait()
    load.wait()
    blocks = tile.shape[0]
    store = pltpu.make_async_copy(tile, mail.at[pl.ds(0, blocks)], in_sems.at[3])
    store.start()
    column = (me[0] >> 1) & 1
    finish = shared(out.shape[0], entries, out, tile, place, used, seen, mark, sems, mark_sems, column, lambda j: target_s[j], lambda j: pick_s[j])
    lane = lax.broadcasted_iota(jnp.int32, head.shape, 1)
    line = jnp.zeros(head.shape, jnp.int32)
    for j in range(entries):
        line = jnp.where(lane == j, target_s[j], line)
        line = jnp.where(lane == entries + j, pick_s[j], line)
    head[...] = line.astype(jnp.float32).astype(head.dtype)
    rows, lanes = head.shape
    note = pltpu.make_async_copy(head, mail.at[blocks, pl.ds(0, rows), pl.ds(0, lanes)], in_sems.at[4])
    note.start()
    finish()
    store.wait()
    note.wait()


def pack_own(me, targets, picks, tile, places):
    entries = targets.shape[0]
    blocks, rows, feature = tile.shape
    slots = places * CAP
    hbm = whole(pltpu.HBM)
    return pl.pallas_call(
        functools.partial(own_kernel, entries),
        out_shape=(jax.ShapeDtypeStruct((slots, rows, feature), tile.dtype), jax.ShapeDtypeStruct((blocks + 1, rows, feature), tile.dtype)),
        in_specs=[whole(pltpu.SMEM), hbm, hbm, hbm],
        out_specs=(hbm, hbm),
        scratch_shapes=[
            pltpu.SMEM((entries,), jnp.int32),
            pltpu.SMEM((entries,), jnp.int32),
            pltpu.VMEM(tile.shape, tile.dtype),
            pltpu.VMEM((16, 128), tile.dtype),
            pltpu.SMEM((entries,), jnp.int32),
            pltpu.SMEM((slots,), jnp.int32),
            pltpu.SMEM((slots,), jnp.int32),
            pltpu.VMEM((16, 128), tile.dtype),
            pltpu.SemaphoreType.DMA((entries,)),
            pltpu.SemaphoreType.DMA((slots,)),
            pltpu.SemaphoreType.DMA((5,)),
        ],
        compiler_params=pltpu.CompilerParams(vmem_limit_bytes=BIG_GRANT),
        name="pack_own",
    )(me, targets, picks, tile)


def far_kernel(entries, me, mail, out, list_v, list_s, tile, head, place, used, seen, mark, sems, mark_sems, in_sems):
    blocks = tile.shape[0]
    rows, lanes = head.shape
    note = pltpu.make_async_copy(mail.at[blocks, pl.ds(0, rows), pl.ds(0, lanes)], head, in_sems.at[0])
    load = pltpu.make_async_copy(mail.at[pl.ds(0, blocks)], tile, in_sems.at[1])
    note.start()
    load.start()
    note.wait()
    list_v[...] = head[...].astype(jnp.float32)[:8].astype(jnp.int32)
    down = pltpu.make_async_copy(list_v, list_s, in_sems.at[2])
    down.start()
    down.wait()
    load.wait()
    column = (me[0] >> 1) & 1
    shared(out.shape[0], entries, out, tile, place, used, seen, mark, sems, mark_sems, column, lambda j: list_s[0, j], lambda j: list_s[0, entries + j])()


def pack_far(me, mail, places, entries):
    blocks, rows, feature = mail.shape
    slots = places * CAP
    hbm = whole(pltpu.HBM)
    return pl.pallas_call(
        functools.partial(far_kernel, entries),
        out_shape=jax.ShapeDtypeStruct((slots, rows, feature), mail.dtype),
        in_specs=[whole(pltpu.SMEM), hbm],
        out_specs=hbm,
        scratch_shapes=[
            pltpu.VMEM((8, 128), jnp.int32),
            pltpu.SMEM((8, 128), jnp.int32),
            pltpu.VMEM((blocks - 1, rows, feature), mail.dtype),
            pltpu.VMEM((16, 128), mail.dtype),
            pltpu.SMEM((entries,), jnp.int32),
            pltpu.SMEM((slots,), jnp.int32),
            pltpu.SMEM((slots,), jnp.int32),
            pltpu.VMEM((16, 128), mail.dtype),
            pltpu.SemaphoreType.DMA((entries,)),
            pltpu.SemaphoreType.DMA((slots,)),
            pltpu.SemaphoreType.DMA((3,)),
        ],
        compiler_params=pltpu.CompilerParams(vmem_limit_bytes=BIG_GRANT),
        name="pack_far",
    )(me, mail)


def cycle_kernel(rate, tiles, q_ref, *refs):
    q = q_ref[...]
    rows, feature = q.shape
    keys = [ref[...] for ref in refs[:tiles]]
    state_in, state_ref = (None, refs[tiles]) if len(refs) == tiles + 1 else refs[tiles:]
    scores = [nt_dot(q, k) for k in keys]
    m = jnp.max(functools.reduce(jnp.maximum, scores), axis=1, keepdims=True)
    if state_in is not None:
        old = state_in[:, feature : feature + 1]
        m = jnp.maximum(m, old)
    exps = [jnp.exp2((s - m) * rate) for s in scores]
    l = jnp.sum(functools.reduce(jnp.add, exps), axis=1, keepdims=True)
    num = jnp.zeros((rows, feature), jnp.float32)
    if state_in is not None:
        shrink = jnp.exp2((old - m) * rate)
        l += state_in[:, feature + 1 : feature + 2] * shrink
        num = state_in[:, :feature] * shrink
    for e, k in zip(exps, keys):
        num += jnp.dot(e.astype(jnp.bfloat16), k, preferred_element_type=jnp.float32)
    state_ref[:, :feature] = num
    lane = lax.broadcasted_iota(jnp.int32, (rows, LANES), 1)
    if state_in is not None:
        positive = state_in[:, feature + 2 : feature + 3]
    else:
        first = pl.multiple_of(pl.program_id(0) * rows, rows)
        own = refs[0][pl.ds(first, rows), :]
        positive = jnp.sum(q.astype(jnp.float32) * own.astype(jnp.float32), axis=1, keepdims=True)
    state_ref[:, feature:] = jnp.where(lane == 0, m, jnp.where(lane == 1, l, positive))


def cycle_part(rate, q, keys, states, rows=256):
    n, feature = q.shape
    tiles = len(keys)
    block = pl.BlockSpec((rows, feature), lambda i: (i, 0))
    wide = pl.BlockSpec((rows, feature + LANES), lambda i: (i, 0))
    full = pl.BlockSpec((n, feature), lambda i: (0, 0))
    return pl.pallas_call(
        functools.partial(cycle_kernel, rate, tiles),
        grid=(n // rows,),
        out_shape=jax.ShapeDtypeStruct((n, feature + LANES), jnp.float32),
        in_specs=[block] + [full] * tiles + [wide] * len(states),
        out_specs=wide,
        compiler_params=pltpu.CompilerParams(vmem_limit_bytes=VMEM_LIMIT),
        cost_estimate=pl.CostEstimate(flops=4 * n * tiles * n * feature, bytes_accessed=(tiles + 3) * n * feature * 2, transcendentals=tiles * n * n),
        name="cycle_more" if states else "cycle",
    )(q, *keys, *states)


def hard_kernel(rate, scale, last, q_hbm, k_hbm, state_in, blocks, *rest):
    if last:
        grad, loss_ref, stats_ref, q_ref, k_ref, state, keys, scores, order, sems, out_sems = rest
    else:
        state_out, q_ref, state, keys, scores, order, sems, out_sems = rest
    n, feature = q_ref.shape
    slots = blocks.shape[0]
    per = CHUNK // BLOCK
    load_keys = pltpu.make_async_copy(blocks, keys, sems.at[0])
    load_q = pltpu.make_async_copy(q_hbm, q_ref, sems.at[1])
    load_state = pltpu.make_async_copy(state_in, state, sems.at[2])
    load_keys.start()
    load_q.start()
    load_state.start()
    if last:
        load_own = pltpu.make_async_copy(k_hbm, k_ref, sems.at[3])
        load_own.start()
    load_keys.wait()
    there = [(jnp.max(keys[s, :16, :128].astype(jnp.float32)) < ABSENT / 2).astype(jnp.int32) for s in range(slots)]
    live = jnp.int32(0)
    for s in range(slots):
        order[live] = s
        live += there[s]
    chunks = (live + per - 1) // per
    tail = order[jnp.maximum(live - 1, 0)]
    for p in range(per - 1):
        order[live + p] = tail

    def chunk_keys(i):
        return jnp.concatenate([keys[order[i * per + p]] for p in range(per)], axis=0)

    load_q.wait()
    q = q_ref[...]

    def score(i, m):
        s = nt_dot(q, chunk_keys(i))
        scores[i] = s
        for c in range(per):
            m = jnp.maximum(m, s[:, c * BLOCK : (c + 1) * BLOCK])
        return m

    wide = lax.fori_loop(0, chunks, score, jnp.full((n, BLOCK), -jnp.inf, jnp.float32))
    load_state.wait()
    old = state[:, feature : feature + 1]
    m = jnp.maximum(jnp.max(wide, axis=1, keepdims=True), old)
    shrink = jnp.exp2((old - m) * rate)
    kept = state[:, feature + 1 : feature + 2] * shrink
    state[:, :feature] = state[:, :feature] * shrink
    for p in range(1, per):
        @pl.when(((chunks - 1) * per + p >= live) & (chunks > 0))
        def _(p=p):
            scores[chunks - 1, :, p * BLOCK : (p + 1) * BLOCK] = jnp.full((n, BLOCK), -jnp.inf, jnp.float32)

    def weigh(i, l):
        e = jnp.exp2((scores[i] - m) * rate)
        state[:, :feature] += jnp.dot(e.astype(jnp.bfloat16), chunk_keys(i), preferred_element_type=jnp.float32)
        for c in range(per):
            l = l + e[:, c * BLOCK : (c + 1) * BLOCK]
        return l

    l = lax.fori_loop(0, chunks, weigh, jnp.zeros((n, BLOCK), jnp.float32))
    total = jnp.sum(l, axis=1, keepdims=True) + kept
    lane = lax.broadcasted_iota(jnp.int32, (n, LANES), 1)
    if not last:
        state[:, feature:] = jnp.where(lane == 0, m, jnp.where(lane == 1, total, state[:, feature:]))
        save = pltpu.make_async_copy(state, state_out, out_sems.at[0])
        save.start()
        save.wait()
        return
    load_own.wait()
    inverse = 1.0 / total
    piece = n // out_sems.shape[0]
    saves = []
    for r in range(out_sems.shape[0]):
        part = pl.ds(r * piece, piece)
        gain = inverse[r * piece : (r + 1) * piece] * scale
        state[part, :feature] = state[part, :feature] * gain - k_ref[part, :].astype(jnp.float32) * scale
        saves.append(pltpu.make_async_copy(state.at[part, pl.ds(0, feature)], grad.at[part], out_sems.at[r]))
        saves[-1].start()
    positive = state[:, feature + 2 : feature + 3]
    loss = (m - positive) * scale + jnp.log(total)
    table = jnp.where(lane == 0, m, jnp.where(lane == 1, inverse, loss))
    flipped = table.T
    stats_ref[...] = flipped[:8]
    loss_ref[...] = flipped[2:3]
    for save in saves:
        save.wait()


def hard_part(rate, scale, last, q, k0, state, blocks):
    n, feature = q.shape
    slots = blocks.shape[0]
    f32 = jnp.float32
    keys = slots * BLOCK
    scratch = [pltpu.VMEM(q.shape, q.dtype)]
    shapes = [jax.ShapeDtypeStruct(state.shape, f32)]
    specs = [whole(pl.ANY)]
    if last:
        scratch += [pltpu.VMEM(k0.shape, k0.dtype)]
        shapes = [jax.ShapeDtypeStruct((n, feature), f32), jax.ShapeDtypeStruct((1, n), f32), jax.ShapeDtypeStruct((8, n), f32)]
        specs = [whole(pl.ANY), whole(), whole()]
    scratch += [
        pltpu.VMEM(state.shape, f32),
        pltpu.VMEM(blocks.shape, blocks.dtype),
        pltpu.VMEM((keys // CHUNK, n, CHUNK), f32),
        pltpu.SMEM((slots + CHUNK // BLOCK,), jnp.int32),
        pltpu.SemaphoreType.DMA((4,)),
        pltpu.SemaphoreType.DMA((4 if last else 1,)),
    ]
    return pl.pallas_call(
        functools.partial(hard_kernel, rate, scale, last),
        out_shape=shapes,
        in_specs=[whole(pl.ANY)] * 4,
        out_specs=specs,
        scratch_shapes=scratch,
        compiler_params=pltpu.CompilerParams(vmem_limit_bytes=BIG_GRANT),
        cost_estimate=pl.CostEstimate(flops=2 * n * keys * feature, bytes_accessed=2 * keys * feature, transcendentals=n * keys // 2),
        name="hard_last" if last else "hard_first",
    )(q, k0, state, blocks)


def rtl_kernel(rate, scale, k_ref, n0_ref, n1_ref, n2_ref, s0_ref, s1_ref, s2_ref, out_ref):
    k = k_ref[...]
    first = pl.multiple_of(pl.program_id(0) * k.shape[0], k.shape[0])
    total = -n0_ref[pl.ds(first, k.shape[0]), :].astype(jnp.float32)
    for n_ref, s_ref in ((n0_ref, s0_ref), (n1_ref, s1_ref), (n2_ref, s2_ref)):
        rows = n_ref[...]
        s = nt_dot(k, rows)
        w = jnp.exp2((s - s_ref[0:1, :]) * rate) * s_ref[1:2, :]
        total += jnp.dot(w.astype(jnp.bfloat16), rows, preferred_element_type=jnp.float32)
    out_ref[...] = total * scale


def rtl_part(rate, scale, k, n0, n1, n2, s0, s1, s2, rows=256):
    n, feature = k.shape
    block = pl.BlockSpec((rows, feature), lambda i: (i, 0))
    full = pl.BlockSpec((n, feature), lambda i: (0, 0), pipeline_mode=pl.Buffered(1))
    stat = pl.BlockSpec((8, n), lambda i: (0, 0), pipeline_mode=pl.Buffered(1))
    return pl.pallas_call(
        functools.partial(rtl_kernel, rate, scale),
        grid=(n // rows,),
        out_shape=jax.ShapeDtypeStruct((n, feature), jnp.float32),
        in_specs=[block, full, full, full, stat, stat, stat],
        out_specs=block,
        compiler_params=pltpu.CompilerParams(vmem_limit_bytes=VMEM_LIMIT),
        cost_estimate=pl.CostEstimate(flops=4 * n * 3 * n * feature, bytes_accessed=6 * n * feature * 2, transcendentals=3 * n * n),
        name="rtl",
    )(k, n0, n1, n2, s0, s1, s2)


def body(netlist, rtl, hard_target, hard_block):
    queries = netlist[0]
    own_keys = rtl[0]
    feature = queries.shape[1]
    scale = 3.0 / math.sqrt(feature)
    rate = scale * math.log2(math.e)
    groups = lax.axis_size("dp")
    targets = hard_target[0, 0, :, 0]
    picks = hard_block[0, 0]
    columns = [[g for g in range(groups) if (g // 2) % 2 == x] for x in range(2)]
    places = groups // 2

    def spread(packed):
        return lax.all_to_all(packed, "dp", split_axis=0, concat_axis=0, axis_index_groups=columns, tiled=True)

    at = jnp.full((1,), lax.axis_index("dp"), jnp.int32)
    packed, mail = pack_own(at, targets, picks, own_keys.reshape(-1, BLOCK, feature), places)
    first = spread(packed)
    mail = lax.ppermute(mail, "dp", [(g, g ^ 2) for g in range(groups)])
    mail, onward, back = lax.optimization_barrier((mail, own_keys, queries))
    rtl1 = passed_along(onward, "loop", 1)
    net1 = passed_along(back, "loop", -1)
    packed = pack_far(at, mail, places, targets.shape[0])
    packed, rtl1, net1 = lax.optimization_barrier((packed, rtl1, net1))
    second = spread(packed)
    rtl2 = passed_along(rtl1, "loop", 1)
    net2 = passed_along(net1, "loop", -1)

    state = cycle_part(rate, queries, [own_keys, rtl1], [])
    (state,) = hard_part(rate, scale, False, queries, own_keys, state, first)
    state = cycle_part(rate, queries, [rtl2], [state])
    grad, loss, stats = hard_part(rate, scale, True, queries, own_keys, state, second)
    stats1 = passed_along(stats, "loop", -1)
    stats2 = passed_along(stats, "loop", -2)
    rtl_grad = rtl_part(rate, scale, own_keys, queries, net1, net2, stats, stats1, stats2)
    return (loss, grad[None], rtl_grad[None])


def solution(mesh):
    return jax.shard_map(
        body,
        mesh=mesh,
        in_specs=(
            P("dp", "loop", None),
            P("dp", "loop", None),
            P("dp", "loop", None, None),
            P("dp", "loop", None),
        ),
        out_specs=(P("dp", "loop"), P("dp", "loop", None), P("dp", "loop", None)),
        check_vma=False,
    )
```

```python
import functools
import math

import jax
import jax.numpy as jnp
from jax import lax
from jax.experimental import pallas as pl
from jax.experimental.pallas import tpu as pltpu
from jax.sharding import PartitionSpec as P

BLOCK = 128
CAP = 2
CHUNK = 512
VMEM_LIMIT = 28 * 1024 * 1024
BIG_GRANT = 60 * 1024 * 1024
ABSENT = 1024.0
LANES = 128


def passed_along(block, axis, distance):
    devices = range(lax.axis_size(axis))
    route = [((i - distance) % len(devices), i) for i in devices]
    return lax.ppermute(block, axis, route)


def nt_dot(a, b):
    return lax.dot_general(a, b, (((1,), (1,)), ((), ())), preferred_element_type=jnp.float32)


def whole(space=pltpu.VMEM):
    return pl.BlockSpec(memory_space=space)


def shared(slots, entries, out, tile, place, used, seen, mark, sems, mark_sems, column, target_of, pick_of):
    mark[...] = jnp.full(mark.shape, ABSENT, mark.dtype)
    for s in range(slots):
        used[s] = 0
        seen[s] = 0
    for j in range(entries):
        t = target_of(j)
        rank = seen[t]
        seen[t] = rank + 1
        slot = ((t >> 2) * 2 + (t & 1)) * CAP + jnp.minimum(rank, CAP - 1)
        place[j] = jnp.where(((t >> 1) & 1) == column, slot, -1)

        @pl.when(place[j] >= 0)
        def _(j=j):
            used[place[j]] = 1
            pltpu.make_async_copy(tile.at[pl.ds(pl.multiple_of(pick_of(j) * BLOCK, BLOCK), BLOCK)], out.at[place[j]], sems.at[j]).start()

    rows, lanes = mark.shape
    for s in range(slots):
        @pl.when(used[s] == 0)
        def _(s=s):
            pltpu.make_async_copy(mark, out.at[s, pl.ds(0, rows), pl.ds(0, lanes)], mark_sems.at[s]).start()

    def finish():
        for j in range(entries):
            @pl.when(place[j] >= 0)
            def _(j=j):
                pltpu.make_async_copy(tile.at[pl.ds(pl.multiple_of(pick_of(j) * BLOCK, BLOCK), BLOCK)], out.at[place[j]], sems.at[j]).wait()

        for s in range(slots):
            @pl.when(used[s] == 0)
            def _(s=s):
                pltpu.make_async_copy(mark, out.at[s, pl.ds(0, rows), pl.ds(0, lanes)], mark_sems.at[s]).wait()

    return finish


def own_kernel(entries, me, targets, picks, rtl, out, mail, target_s, pick_s, tile, head, place, used, seen, mark, sems, mark_sems, in_sems):
    lists = [pltpu.make_async_copy(targets, target_s, in_sems.at[0]), pltpu.make_async_copy(picks, pick_s, in_sems.at[1])]
    load = pltpu.make_async_copy(rtl, tile, in_sems.at[2])
    for copy in lists + [load]:
        copy.start()
    for copy in lists:
        copy.wait()
    load.wait()
    size = tile.shape[0]
    store = pltpu.make_async_copy(tile, mail.at[pl.ds(0, size)], in_sems.at[3])
    store.start()
    column = (me[0] >> 1) & 1
    finish = shared(out.shape[0], entries, out, tile, place, used, seen, mark, sems, mark_sems, column, lambda j: target_s[j], lambda j: pick_s[j])
    lane = lax.broadcasted_iota(jnp.int32, head.shape, 1)
    line = jnp.zeros(head.shape, jnp.int32)
    for j in range(entries):
        line = jnp.where(lane == j, target_s[j], line)
        line = jnp.where(lane == entries + j, pick_s[j], line)
    head[...] = line.astype(jnp.float32).astype(head.dtype)
    rows, lanes = head.shape
    note = pltpu.make_async_copy(head, mail.at[pl.ds(size, rows), pl.ds(0, lanes)], in_sems.at[4])
    note.start()
    finish()
    store.wait()
    note.wait()


def pack_own(me, targets, picks, tile, places):
    entries = targets.shape[0]
    rows, feature = tile.shape
    slots = places * CAP
    hbm = whole(pltpu.HBM)
    return pl.pallas_call(
        functools.partial(own_kernel, entries),
        out_shape=(jax.ShapeDtypeStruct((slots, BLOCK, feature), tile.dtype), jax.ShapeDtypeStruct((rows + 16, feature), tile.dtype)),
        in_specs=[whole(pltpu.SMEM), hbm, hbm, hbm],
        out_specs=(hbm, hbm),
        scratch_shapes=[
            pltpu.SMEM((entries,), jnp.int32),
            pltpu.SMEM((entries,), jnp.int32),
            pltpu.VMEM(tile.shape, tile.dtype),
            pltpu.VMEM((16, 128), tile.dtype),
            pltpu.SMEM((entries,), jnp.int32),
            pltpu.SMEM((slots,), jnp.int32),
            pltpu.SMEM((slots,), jnp.int32),
            pltpu.VMEM((16, 128), tile.dtype),
            pltpu.SemaphoreType.DMA((entries,)),
            pltpu.SemaphoreType.DMA((slots,)),
            pltpu.SemaphoreType.DMA((5,)),
        ],
        compiler_params=pltpu.CompilerParams(vmem_limit_bytes=BIG_GRANT),
        name="pack_own",
    )(me, targets, picks, tile)


def far_kernel(entries, me, mail, out, list_v, list_s, tile, head, place, used, seen, mark, sems, mark_sems, in_sems):
    size = tile.shape[0]
    rows, lanes = head.shape
    note = pltpu.make_async_copy(mail.at[pl.ds(size, rows), pl.ds(0, lanes)], head, in_sems.at[0])
    load = pltpu.make_async_copy(mail.at[pl.ds(0, size)], tile, in_sems.at[1])
    note.start()
    load.start()
    note.wait()
    list_v[...] = head[...].astype(jnp.float32)[:8].astype(jnp.int32)
    down = pltpu.make_async_copy(list_v, list_s, in_sems.at[2])
    down.start()
    down.wait()
    load.wait()
    column = (me[0] >> 1) & 1
    shared(out.shape[0], entries, out, tile, place, used, seen, mark, sems, mark_sems, column, lambda j: list_s[0, j], lambda j: list_s[0, entries + j])()


def pack_far(me, mail, places, entries):
    rows, feature = mail.shape
    slots = places * CAP
    hbm = whole(pltpu.HBM)
    return pl.pallas_call(
        functools.partial(far_kernel, entries),
        out_shape=jax.ShapeDtypeStruct((slots, BLOCK, feature), mail.dtype),
        in_specs=[whole(pltpu.SMEM), hbm],
        out_specs=hbm,
        scratch_shapes=[
            pltpu.VMEM((8, 128), jnp.int32),
            pltpu.SMEM((8, 128), jnp.int32),
            pltpu.VMEM((rows - 16, feature), mail.dtype),
            pltpu.VMEM((16, 128), mail.dtype),
            pltpu.SMEM((entries,), jnp.int32),
            pltpu.SMEM((slots,), jnp.int32),
            pltpu.SMEM((slots,), jnp.int32),
            pltpu.VMEM((16, 128), mail.dtype),
            pltpu.SemaphoreType.DMA((entries,)),
            pltpu.SemaphoreType.DMA((slots,)),
            pltpu.SemaphoreType.DMA((3,)),
        ],
        compiler_params=pltpu.CompilerParams(vmem_limit_bytes=BIG_GRANT),
        name="pack_far",
    )(me, mail)


def cycle_kernel(rate, tiles, q_ref, *refs):
    q = q_ref[...]
    rows, feature = q.shape
    keys = [ref[...] for ref in refs[:tiles]]
    state_in, state_ref = (None, refs[tiles]) if len(refs) == tiles + 1 else refs[tiles:]
    scores = [nt_dot(q, k) for k in keys]
    m = jnp.max(functools.reduce(jnp.maximum, scores), axis=1, keepdims=True)
    if state_in is not None:
        old = state_in[:, feature : feature + 1]
        m = jnp.maximum(m, old)
    exps = [jnp.exp2((s - m) * rate) for s in scores]
    l = jnp.sum(functools.reduce(jnp.add, exps), axis=1, keepdims=True)
    num = jnp.zeros((rows, feature), jnp.float32)
    if state_in is not None:
        shrink = jnp.exp2((old - m) * rate)
        l += state_in[:, feature + 1 : feature + 2] * shrink
        num = state_in[:, :feature] * shrink
    for e, k in zip(exps, keys):
        num += jnp.dot(e.astype(jnp.bfloat16), k, preferred_element_type=jnp.float32)
    state_ref[:, :feature] = num
    lane = lax.broadcasted_iota(jnp.int32, (rows, LANES), 1)
    if state_in is not None:
        positive = state_in[:, feature + 2 : feature + 3]
    else:
        first = pl.multiple_of(pl.program_id(0) * rows, rows)
        own = refs[0][pl.ds(first, rows), :]
        positive = jnp.sum(q.astype(jnp.float32) * own.astype(jnp.float32), axis=1, keepdims=True)
    state_ref[:, feature:] = jnp.where(lane == 0, m, jnp.where(lane == 1, l, positive))


def cycle_part(rate, q, keys, states, rows=256):
    n, feature = q.shape
    tiles = len(keys)
    block = pl.BlockSpec((rows, feature), lambda i: (i, 0))
    wide = pl.BlockSpec((rows, feature + LANES), lambda i: (i, 0))
    full = pl.BlockSpec((n, feature), lambda i: (0, 0))
    return pl.pallas_call(
        functools.partial(cycle_kernel, rate, tiles),
        grid=(n // rows,),
        out_shape=jax.ShapeDtypeStruct((n, feature + LANES), jnp.float32),
        in_specs=[block] + [full] * tiles + [wide] * len(states),
        out_specs=wide,
        compiler_params=pltpu.CompilerParams(vmem_limit_bytes=VMEM_LIMIT),
        cost_estimate=pl.CostEstimate(flops=4 * n * tiles * n * feature, bytes_accessed=(tiles + 3) * n * feature * 2, transcendentals=tiles * n * n),
        name="cycle_more" if states else "cycle",
    )(q, *keys, *states)


def hard_kernel(rate, scale, last, q_hbm, k_hbm, state_in, blocks, *rest):
    if last:
        grad, loss_ref, stats_ref, q_ref, k_ref, state, keys, scores, order, sems, out_sems = rest
    else:
        state_out, q_ref, state, keys, scores, order, sems, out_sems = rest
    n, feature = q_ref.shape
    slots = blocks.shape[0]
    per = CHUNK // BLOCK
    load_keys = pltpu.make_async_copy(blocks, keys, sems.at[0])
    load_q = pltpu.make_async_copy(q_hbm, q_ref, sems.at[1])
    load_state = pltpu.make_async_copy(state_in, state, sems.at[2])
    load_keys.start()
    load_q.start()
    load_state.start()
    if last:
        load_own = pltpu.make_async_copy(k_hbm, k_ref, sems.at[3])
        load_own.start()
    load_keys.wait()
    there = [(jnp.max(keys[s, :16, :128].astype(jnp.float32)) < ABSENT / 2).astype(jnp.int32) for s in range(slots)]
    live = jnp.int32(0)
    for s in range(slots):
        order[live] = s
        live += there[s]
    chunks = (live + per - 1) // per
    tail = order[jnp.maximum(live - 1, 0)]
    for p in range(per - 1):
        order[live + p] = tail

    def chunk_keys(i):
        return jnp.concatenate([keys[order[i * per + p]] for p in range(per)], axis=0)

    load_q.wait()
    q = q_ref[...]

    def score(i, m):
        s = nt_dot(q, chunk_keys(i))
        scores[i] = s
        for c in range(per):
            m = jnp.maximum(m, s[:, c * BLOCK : (c + 1) * BLOCK])
        return m

    wide = lax.fori_loop(0, chunks, score, jnp.full((n, BLOCK), -jnp.inf, jnp.float32))
    load_state.wait()
    old = state[:, feature : feature + 1]
    m = jnp.maximum(jnp.max(wide, axis=1, keepdims=True), old)
    shrink = jnp.exp2((old - m) * rate)
    kept = state[:, feature + 1 : feature + 2] * shrink
    state[:, :feature] = state[:, :feature] * shrink
    for p in range(1, per):
        @pl.when(((chunks - 1) * per + p >= live) & (chunks > 0))
        def _(p=p):
            scores[chunks - 1, :, p * BLOCK : (p + 1) * BLOCK] = jnp.full((n, BLOCK), -jnp.inf, jnp.float32)

    def weigh(i, l):
        e = jnp.exp2((scores[i] - m) * rate)
        state[:, :feature] += jnp.dot(e.astype(jnp.bfloat16), chunk_keys(i), preferred_element_type=jnp.float32)
        for c in range(per):
            l = l + e[:, c * BLOCK : (c + 1) * BLOCK]
        return l

    l = lax.fori_loop(0, chunks, weigh, jnp.zeros((n, BLOCK), jnp.float32))
    total = jnp.sum(l, axis=1, keepdims=True) + kept
    lane = lax.broadcasted_iota(jnp.int32, (n, LANES), 1)
    if not last:
        state[:, feature:] = jnp.where(lane == 0, m, jnp.where(lane == 1, total, state[:, feature:]))
        save = pltpu.make_async_copy(state, state_out, out_sems.at[0])
        save.start()
        save.wait()
        return
    load_own.wait()
    inverse = 1.0 / total
    piece = n // out_sems.shape[0]
    saves = []
    for r in range(out_sems.shape[0]):
        part = pl.ds(r * piece, piece)
        gain = inverse[r * piece : (r + 1) * piece] * scale
        state[part, :feature] = state[part, :feature] * gain - k_ref[part, :].astype(jnp.float32) * scale
        saves.append(pltpu.make_async_copy(state.at[part, pl.ds(0, feature)], grad.at[part], out_sems.at[r]))
        saves[-1].start()
    positive = state[:, feature + 2 : feature + 3]
    loss = (m - positive) * scale + jnp.log(total)
    table = jnp.where(lane == 0, m, jnp.where(lane == 1, inverse, loss))
    flipped = table.T
    stats_ref[...] = flipped[:8]
    loss_ref[...] = flipped[2:3]
    for save in saves:
        save.wait()


def hard_part(rate, scale, last, q, k0, state, blocks):
    n, feature = q.shape
    slots = blocks.shape[0]
    f32 = jnp.float32
    keys = slots * BLOCK
    scratch = [pltpu.VMEM(q.shape, q.dtype)]
    shapes = [jax.ShapeDtypeStruct(state.shape, f32)]
    specs = [whole(pl.ANY)]
    if last:
        scratch += [pltpu.VMEM(k0.shape, k0.dtype)]
        shapes = [jax.ShapeDtypeStruct((n, feature), f32), jax.ShapeDtypeStruct((1, n), f32), jax.ShapeDtypeStruct((8, n), f32)]
        specs = [whole(pl.ANY), whole(), whole()]
    scratch += [
        pltpu.VMEM(state.shape, f32),
        pltpu.VMEM(blocks.shape, blocks.dtype),
        pltpu.VMEM((keys // CHUNK, n, CHUNK), f32),
        pltpu.SMEM((slots + CHUNK // BLOCK,), jnp.int32),
        pltpu.SemaphoreType.DMA((4,)),
        pltpu.SemaphoreType.DMA((4 if last else 1,)),
    ]
    return pl.pallas_call(
        functools.partial(hard_kernel, rate, scale, last),
        out_shape=shapes,
        in_specs=[whole(pl.ANY)] * 4,
        out_specs=specs,
        scratch_shapes=scratch,
        compiler_params=pltpu.CompilerParams(vmem_limit_bytes=BIG_GRANT),
        cost_estimate=pl.CostEstimate(flops=2 * n * keys * feature, bytes_accessed=2 * keys * feature, transcendentals=n * keys // 2),
        name="hard_last" if last else "hard_first",
    )(q, k0, state, blocks)


def rtl_kernel(rate, scale, k_ref, n0_ref, n1_ref, n2_ref, s0_ref, s1_ref, s2_ref, out_ref):
    k = k_ref[...]
    first = pl.multiple_of(pl.program_id(0) * k.shape[0], k.shape[0])
    total = -n0_ref[pl.ds(first, k.shape[0]), :].astype(jnp.float32)
    for n_ref, s_ref in ((n0_ref, s0_ref), (n1_ref, s1_ref), (n2_ref, s2_ref)):
        rows = n_ref[...]
        s = nt_dot(k, rows)
        w = jnp.exp2((s - s_ref[0:1, :]) * rate) * s_ref[1:2, :]
        total += jnp.dot(w.astype(jnp.bfloat16), rows, preferred_element_type=jnp.float32)
    out_ref[...] = total * scale


def rtl_part(rate, scale, k, n0, n1, n2, s0, s1, s2, rows=256):
    n, feature = k.shape
    block = pl.BlockSpec((rows, feature), lambda i: (i, 0))
    full = pl.BlockSpec((n, feature), lambda i: (0, 0), pipeline_mode=pl.Buffered(1))
    stat = pl.BlockSpec((8, n), lambda i: (0, 0), pipeline_mode=pl.Buffered(1))
    return pl.pallas_call(
        functools.partial(rtl_kernel, rate, scale),
        grid=(n // rows,),
        out_shape=jax.ShapeDtypeStruct((n, feature), jnp.float32),
        in_specs=[block, full, full, full, stat, stat, stat],
        out_specs=block,
        compiler_params=pltpu.CompilerParams(vmem_limit_bytes=VMEM_LIMIT),
        cost_estimate=pl.CostEstimate(flops=4 * n * 3 * n * feature, bytes_accessed=6 * n * feature * 2, transcendentals=3 * n * n),
        name="rtl",
    )(k, n0, n1, n2, s0, s1, s2)


def body(netlist, rtl, hard_target, hard_block):
    queries = netlist[0]
    own_keys = rtl[0]
    feature = queries.shape[1]
    scale = 3.0 / math.sqrt(feature)
    rate = scale * math.log2(math.e)
    groups = lax.axis_size("dp")
    targets = hard_target[0, 0, :, 0]
    picks = hard_block[0, 0]
    columns = [[g for g in range(groups) if (g // 2) % 2 == x] for x in range(2)]
    places = groups // 2

    def spread(packed):
        return lax.all_to_all(packed, "dp", split_axis=0, concat_axis=0, axis_index_groups=columns, tiled=True)

    at = jnp.full((1,), lax.axis_index("dp"), jnp.int32)
    packed, mail = pack_own(at, targets, picks, own_keys, places)
    first = spread(packed)
    mail = lax.ppermute(mail, "dp", [(g, g ^ 2) for g in range(groups)])
    rtl1 = passed_along(own_keys, "loop", 1)
    mail, rtl1, back = lax.optimization_barrier((mail, rtl1, queries))
    second = spread(pack_far(at, mail, places, targets.shape[0]))
    rtl2 = passed_along(rtl1, "loop", 1)
    net1 = passed_along(back, "loop", -1)

    state = cycle_part(rate, queries, [own_keys, rtl1], [])
    (state,) = hard_part(rate, scale, False, queries, own_keys, state, first)
    net1, state = lax.optimization_barrier((net1, state))
    net2 = passed_along(net1, "loop", -1)
    state = cycle_part(rate, queries, [rtl2], [state])
    grad, loss, stats = hard_part(rate, scale, True, queries, own_keys, state, second)
    stats1 = passed_along(stats, "loop", -1)
    stats2 = passed_along(stats, "loop", -2)
    rtl_grad = rtl_part(rate, scale, own_keys, queries, net1, net2, stats, stats1, stats2)
    return (loss, grad[None], rtl_grad[None])


def solution(mesh):
    return jax.shard_map(
        body,
        mesh=mesh,
        in_specs=(
            P("dp", "loop", None),
            P("dp", "loop", None),
            P("dp", "loop", None, None),
            P("dp", "loop", None),
        ),
        out_specs=(P("dp", "loop"), P("dp", "loop", None), P("dp", "loop", None)),
        check_vma=False,
    )
```

```python
import functools
import math

import jax
import jax.numpy as jnp
from jax import lax
from jax.experimental import pallas as pl
from jax.experimental.pallas import tpu as pltpu
from jax.sharding import PartitionSpec as P

BLOCK = 128
CAP = 2
CHUNK = 512
VMEM_LIMIT = 20 * 1024 * 1024
BIG_GRANT = 60 * 1024 * 1024
FAR_GRANT = 64_000_000
HARD_GRANT = 32 * 1024 * 1024
ABSENT = 1024.0
LANES = 128


def passed_along(block, axis, distance):
    devices = range(lax.axis_size(axis))
    route = [((i - distance) % len(devices), i) for i in devices]
    return lax.ppermute(block, axis, route)


def nt_dot(a, b):
    return lax.dot_general(a, b, (((1,), (1,)), ((), ())), preferred_element_type=jnp.float32)


def whole(space=pltpu.VMEM):
    return pl.BlockSpec(memory_space=space)


def shared(slots, entries, out, tile, place, used, seen, mark, sems, mark_sems, column, target_of, pick_of):
    mark[...] = jnp.full(mark.shape, ABSENT, mark.dtype)
    for s in range(slots):
        used[s] = 0
        seen[s] = 0
    for j in range(entries):
        t = target_of(j)
        rank = seen[t]
        seen[t] = rank + 1
        slot = ((t >> 2) * 2 + (t & 1)) * CAP + jnp.minimum(rank, CAP - 1)
        place[j] = jnp.where(((t >> 1) & 1) == column, slot, -1)

        @pl.when(place[j] >= 0)
        def _(j=j):
            used[place[j]] = 1
            pltpu.make_async_copy(tile.at[pl.ds(pl.multiple_of(pick_of(j) * BLOCK, BLOCK), BLOCK)], out.at[place[j]], sems.at[j]).start()

    rows, lanes = mark.shape
    for s in range(slots):
        @pl.when(used[s] == 0)
        def _(s=s):
            pltpu.make_async_copy(mark, out.at[s, pl.ds(0, rows), pl.ds(0, lanes)], mark_sems.at[s]).start()

    def finish():
        for j in range(entries):
            @pl.when(place[j] >= 0)
            def _(j=j):
                pltpu.make_async_copy(tile.at[pl.ds(pl.multiple_of(pick_of(j) * BLOCK, BLOCK), BLOCK)], out.at[place[j]], sems.at[j]).wait()

        for s in range(slots):
            @pl.when(used[s] == 0)
            def _(s=s):
                pltpu.make_async_copy(mark, out.at[s, pl.ds(0, rows), pl.ds(0, lanes)], mark_sems.at[s]).wait()

    return finish


def own_kernel(entries, me, targets, picks, rtl, out, mail, target_s, pick_s, tile, head, place, used, seen, mark, sems, mark_sems, in_sems):
    lists = [pltpu.make_async_copy(targets, target_s, in_sems.at[0]), pltpu.make_async_copy(picks, pick_s, in_sems.at[1])]
    load = pltpu.make_async_copy(rtl, tile, in_sems.at[2])
    for copy in lists + [load]:
        copy.start()
    for copy in lists:
        copy.wait()
    load.wait()
    size = tile.shape[0]
    store = pltpu.make_async_copy(tile, mail.at[pl.ds(0, size)], in_sems.at[3])
    store.start()
    column = (me[0] >> 1) & 1
    finish = shared(out.shape[0], entries, out, tile, place, used, seen, mark, sems, mark_sems, column, lambda j: target_s[j], lambda j: pick_s[j])
    lane = lax.broadcasted_iota(jnp.int32, head.shape, 1)
    line = jnp.zeros(head.shape, jnp.int32)
    for j in range(entries):
        line = jnp.where(lane == j, target_s[j], line)
        line = jnp.where(lane == entries + j, pick_s[j], line)
    head[...] = line.astype(jnp.float32).astype(head.dtype)
    rows, lanes = head.shape
    note = pltpu.make_async_copy(head, mail.at[pl.ds(size, rows), pl.ds(0, lanes)], in_sems.at[4])
    note.start()
    finish()
    store.wait()
    note.wait()


def pack_own(me, targets, picks, tile, places):
    entries = targets.shape[0]
    rows, feature = tile.shape
    slots = places * CAP
    hbm = whole(pltpu.HBM)
    return pl.pallas_call(
        functools.partial(own_kernel, entries),
        out_shape=(jax.ShapeDtypeStruct((slots, BLOCK, feature), tile.dtype), jax.ShapeDtypeStruct((rows + 16, feature), tile.dtype)),
        in_specs=[whole(pltpu.SMEM), hbm, hbm, hbm],
        out_specs=(hbm, hbm),
        scratch_shapes=[
            pltpu.SMEM((entries,), jnp.int32),
            pltpu.SMEM((entries,), jnp.int32),
            pltpu.VMEM(tile.shape, tile.dtype),
            pltpu.VMEM((16, 128), tile.dtype),
            pltpu.SMEM((entries,), jnp.int32),
            pltpu.SMEM((slots,), jnp.int32),
            pltpu.SMEM((slots,), jnp.int32),
            pltpu.VMEM((16, 128), tile.dtype),
            pltpu.SemaphoreType.DMA((entries,)),
            pltpu.SemaphoreType.DMA((slots,)),
            pltpu.SemaphoreType.DMA((5,)),
        ],
        compiler_params=pltpu.CompilerParams(vmem_limit_bytes=BIG_GRANT),
        name="pack_own",
    )(me, targets, picks, tile)


def far_kernel(entries, me, mail, out, list_v, list_s, tile, head, place, used, seen, mark, sems, mark_sems, in_sems):
    size = tile.shape[0]
    rows, lanes = head.shape
    note = pltpu.make_async_copy(mail.at[pl.ds(size, rows), pl.ds(0, lanes)], head, in_sems.at[0])
    load = pltpu.make_async_copy(mail.at[pl.ds(0, size)], tile, in_sems.at[1])
    note.start()
    load.start()
    note.wait()
    list_v[...] = head[...].astype(jnp.float32)[:8].astype(jnp.int32)
    down = pltpu.make_async_copy(list_v, list_s, in_sems.at[2])
    down.start()
    down.wait()
    load.wait()
    column = (me[0] >> 1) & 1
    shared(out.shape[0], entries, out, tile, place, used, seen, mark, sems, mark_sems, column, lambda j: list_s[0, j], lambda j: list_s[0, entries + j])()


def pack_far(me, mail, places, entries):
    rows, feature = mail.shape
    slots = places * CAP
    hbm = whole(pltpu.HBM)
    return pl.pallas_call(
        functools.partial(far_kernel, entries),
        out_shape=jax.ShapeDtypeStruct((slots, BLOCK, feature), mail.dtype),
        in_specs=[whole(pltpu.SMEM), hbm],
        out_specs=hbm,
        scratch_shapes=[
            pltpu.VMEM((8, 128), jnp.int32),
            pltpu.SMEM((8, 128), jnp.int32),
            pltpu.VMEM((rows - 16, feature), mail.dtype),
            pltpu.VMEM((16, 128), mail.dtype),
            pltpu.SMEM((entries,), jnp.int32),
            pltpu.SMEM((slots,), jnp.int32),
            pltpu.SMEM((slots,), jnp.int32),
            pltpu.VMEM((16, 128), mail.dtype),
            pltpu.SemaphoreType.DMA((entries,)),
            pltpu.SemaphoreType.DMA((slots,)),
            pltpu.SemaphoreType.DMA((3,)),
        ],
        compiler_params=pltpu.CompilerParams(vmem_limit_bytes=FAR_GRANT),
        name="pack_far",
    )(me, mail)


def cycle_kernel(rate, scale, start, end, q_ref, k_ref, *refs):
    q = q_ref[...]
    k = k_ref[...]
    rows, feature = q.shape
    s = nt_dot(q, k)
    m = jnp.max(s, axis=1, keepdims=True)
    if start:
        (state_ref,) = refs
        first = pl.multiple_of(pl.program_id(0) * rows, rows)
        own = k_ref[pl.ds(first, rows), :].astype(jnp.float32)
        positive = jnp.sum(q.astype(jnp.float32) * own, axis=1, keepdims=True)
    else:
        state_in = refs[0]
        old = state_in[:, feature : feature + 1]
        positive = state_in[:, feature + 2 : feature + 3]
        m = jnp.maximum(m, old)
    if end:
        others_ref = refs[1]
        m = jnp.maximum(m, others_ref[:, feature : feature + 1])
    e = jnp.exp2((s - m) * rate)
    l = jnp.sum(e, axis=1, keepdims=True)
    num = jnp.dot(e.astype(jnp.bfloat16), k, preferred_element_type=jnp.float32)
    if not start:
        shrink = jnp.exp2((old - m) * rate)
        l += state_in[:, feature + 1 : feature + 2] * shrink
        num += state_in[:, :feature] * shrink
    if end:
        shrink = jnp.exp2((others_ref[:, feature : feature + 1] - m) * rate)
        l += others_ref[:, feature + 1 : feature + 2] * shrink
        num += others_ref[:, :feature] * shrink
    lane = lax.broadcasted_iota(jnp.int32, (rows, LANES), 1)
    if not end:
        state_ref = refs[-1]
        state_ref[:, :feature] = num
        state_ref[:, feature:] = jnp.where(lane == 0, m, jnp.where(lane == 1, l, positive))
        return
    own_ref, grad_ref, loss_ref, stats_ref = refs[2:]
    inverse = 1.0 / l
    grad_ref[...] = (num * inverse - own_ref[...].astype(jnp.float32)) * scale
    loss = (m - positive) * scale + jnp.log(l)
    table = jnp.where(lane == 0, m, jnp.where(lane == 1, inverse, loss))
    flipped = table.T
    stats_ref[...] = flipped[:8]
    loss_ref[...] = flipped[2:3]


def cycle_part(rate, scale, q, k, state=None, rest=None, rows=256):
    n, feature = q.shape
    f32 = jnp.float32
    block = pl.BlockSpec((rows, feature), lambda i: (i, 0))
    wide = pl.BlockSpec((rows, feature + LANES), lambda i: (i, 0))
    full = pl.BlockSpec((n, feature), lambda i: (0, 0), pipeline_mode=pl.Buffered(1))
    start, end = state is None, rest is not None
    args, specs = [q, k], [block, full]
    if not start:
        args, specs = args + [state], specs + [wide]
    shapes, outs = jax.ShapeDtypeStruct((n, feature + LANES), f32), wide
    if end:
        args, specs = args + list(rest), specs + [wide, block]
        shapes = (jax.ShapeDtypeStruct((n, feature), f32), jax.ShapeDtypeStruct((1, n), f32), jax.ShapeDtypeStruct((8, n), f32))
        outs = (block, pl.BlockSpec((1, rows), lambda i: (0, i)), pl.BlockSpec((8, rows), lambda i: (0, i)))
    return pl.pallas_call(
        functools.partial(cycle_kernel, rate, scale, start, end),
        grid=(n // rows,),
        out_shape=shapes,
        in_specs=specs,
        out_specs=outs,
        compiler_params=pltpu.CompilerParams(vmem_limit_bytes=VMEM_LIMIT),
        cost_estimate=pl.CostEstimate(flops=4 * n * n * feature, bytes_accessed=8 * n * feature, transcendentals=n * n),
        name="cycle_own" if start else "cycle_last" if end else "cycle_more",
    )(*args)


def hard_kernel(rate, fresh, q_hbm, *refs):
    state_in = None if fresh else refs[0]
    blocks, state, q_ref, keys, scores, order, sems = refs[-7:]
    n, feature = q_ref.shape
    slots = blocks.shape[0]
    per = CHUNK // BLOCK
    load_keys = pltpu.make_async_copy(blocks, keys, sems.at[0])
    load_q = pltpu.make_async_copy(q_hbm, q_ref, sems.at[1])
    load_keys.start()
    load_q.start()
    if not fresh:
        load_state = pltpu.make_async_copy(state_in, state, sems.at[2])
        load_state.start()
    load_keys.wait()
    there = [(jnp.max(keys[s, :16, :128].astype(jnp.float32)) < ABSENT / 2).astype(jnp.int32) for s in range(slots)]
    live = jnp.int32(0)
    for s in range(slots):
        order[live] = s
        live += there[s]
    chunks = (live + per - 1) // per
    tail = order[jnp.maximum(live - 1, 0)]
    for p in range(per - 1):
        order[live + p] = tail

    def chunk_keys(i):
        return jnp.concatenate([keys[order[i * per + p]] for p in range(per)], axis=0)

    load_q.wait()
    q = q_ref[...]

    def score(i, m):
        s = nt_dot(q, chunk_keys(i))
        scores[i] = s
        for c in range(per):
            m = jnp.maximum(m, s[:, c * BLOCK : (c + 1) * BLOCK])
        return m

    wide = lax.fori_loop(0, chunks, score, jnp.full((n, BLOCK), -jnp.inf, jnp.float32))
    m = jnp.max(wide, axis=1, keepdims=True)
    if fresh:
        state[...] = jnp.zeros(state.shape, jnp.float32)
        kept = 0.0
    else:
        load_state.wait()
        old = state[:, feature : feature + 1]
        m = jnp.maximum(m, old)
        shrink = jnp.exp2((old - m) * rate)
        kept = state[:, feature + 1 : feature + 2] * shrink
        state[:, :feature] = state[:, :feature] * shrink
    for p in range(1, per):
        @pl.when(((chunks - 1) * per + p >= live) & (chunks > 0))
        def _(p=p):
            scores[chunks - 1, :, p * BLOCK : (p + 1) * BLOCK] = jnp.full((n, BLOCK), -jnp.inf, jnp.float32)

    def weigh(i, l):
        e = jnp.exp2((scores[i] - m) * rate)
        state[:, :feature] += jnp.dot(e.astype(jnp.bfloat16), chunk_keys(i), preferred_element_type=jnp.float32)
        for c in range(per):
            l = l + e[:, c * BLOCK : (c + 1) * BLOCK]
        return l

    l = lax.fori_loop(0, chunks, weigh, jnp.zeros((n, BLOCK), jnp.float32))
    total = jnp.sum(l, axis=1, keepdims=True) + kept
    lane = lax.broadcasted_iota(jnp.int32, (n, LANES), 1)
    state[:, feature:] = jnp.where(lane == 0, m, jnp.where(lane == 1, total, state[:, feature:]))


def hard_part(rate, q, states, blocks, name):
    n, feature = q.shape
    slots = blocks.shape[0]
    f32 = jnp.float32
    keys = slots * BLOCK
    return pl.pallas_call(
        functools.partial(hard_kernel, rate, not states),
        out_shape=jax.ShapeDtypeStruct((n, feature + LANES), f32),
        in_specs=[whole(pl.ANY)] * (2 + len(states)),
        out_specs=whole(),
        scratch_shapes=[
            pltpu.VMEM(q.shape, q.dtype),
            pltpu.VMEM(blocks.shape, blocks.dtype),
            pltpu.VMEM((keys // CHUNK, n, CHUNK), f32),
            pltpu.SMEM((slots + CHUNK // BLOCK,), jnp.int32),
            pltpu.SemaphoreType.DMA((3,)),
        ],
        compiler_params=pltpu.CompilerParams(vmem_limit_bytes=HARD_GRANT),
        cost_estimate=pl.CostEstimate(flops=2 * n * keys * feature, bytes_accessed=2 * keys * feature, transcendentals=n * keys // 2),
        name=name,
    )(q, *states, blocks)


def rtl_kernel(rate, scale, k_ref, n0_ref, n1_ref, n2_ref, s0_ref, s1_ref, s2_ref, out_ref):
    k = k_ref[...]
    first = pl.multiple_of(pl.program_id(0) * k.shape[0], k.shape[0])
    total = -n0_ref[pl.ds(first, k.shape[0]), :].astype(jnp.float32)
    for n_ref, s_ref in ((n0_ref, s0_ref), (n1_ref, s1_ref), (n2_ref, s2_ref)):
        rows = n_ref[...]
        s = nt_dot(k, rows)
        w = jnp.exp2((s - s_ref[0:1, :]) * rate) * s_ref[1:2, :]
        total += jnp.dot(w.astype(jnp.bfloat16), rows, preferred_element_type=jnp.float32)
    out_ref[...] = total * scale


def rtl_part(rate, scale, k, n0, n1, n2, s0, s1, s2, rows=256):
    n, feature = k.shape
    block = pl.BlockSpec((rows, feature), lambda i: (i, 0))
    full = pl.BlockSpec((n, feature), lambda i: (0, 0), pipeline_mode=pl.Buffered(1))
    stat = pl.BlockSpec((8, n), lambda i: (0, 0), pipeline_mode=pl.Buffered(1))
    return pl.pallas_call(
        functools.partial(rtl_kernel, rate, scale),
        grid=(n // rows,),
        out_shape=jax.ShapeDtypeStruct((n, feature), jnp.float32),
        in_specs=[block, full, full, full, stat, stat, stat],
        out_specs=block,
        compiler_params=pltpu.CompilerParams(vmem_limit_bytes=VMEM_LIMIT),
        cost_estimate=pl.CostEstimate(flops=4 * n * 3 * n * feature, bytes_accessed=6 * n * feature * 2, transcendentals=3 * n * n),
        name="rtl",
    )(k, n0, n1, n2, s0, s1, s2)


def body(netlist, rtl, hard_target, hard_block):
    queries = netlist[0]
    own_keys = rtl[0]
    feature = queries.shape[1]
    scale = 3.0 / math.sqrt(feature)
    rate = scale * math.log2(math.e)
    groups = lax.axis_size("dp")
    targets = hard_target[0, 0, :, 0]
    picks = hard_block[0, 0]
    columns = [[g for g in range(groups) if (g // 2) % 2 == x] for x in range(2)]
    places = groups // 2

    def spread(packed):
        return lax.all_to_all(packed, "dp", split_axis=0, concat_axis=0, axis_index_groups=columns, tiled=True)

    at = jnp.full((1,), lax.axis_index("dp"), jnp.int32)
    packed, mail = pack_own(at, targets, picks, own_keys, places)
    first = spread(packed)
    mail = lax.ppermute(mail, "dp", [(g, g ^ 2) for g in range(groups)])
    mail, onward, back = lax.optimization_barrier((mail, own_keys, queries))
    rtl1 = passed_along(onward, "loop", 1)
    net1 = passed_along(back, "loop", -1)
    second = spread(pack_far(at, mail, places, targets.shape[0]))

    state = cycle_part(rate, scale, queries, own_keys)
    state = hard_part(rate, queries, [state], first, "hard_first")
    rtl1, net1, state = lax.optimization_barrier((rtl1, net1, state))
    rtl2 = passed_along(rtl1, "loop", 1)
    net2 = passed_along(net1, "loop", -1)
    state = cycle_part(rate, scale, queries, rtl1, state)
    others = hard_part(rate, queries, [], second, "hard_second")
    grad, loss, stats = cycle_part(rate, scale, queries, rtl2, state, (others, own_keys))
    stats1 = passed_along(stats, "loop", -1)
    stats2 = passed_along(stats, "loop", -2)
    rtl_grad = rtl_part(rate, scale, own_keys, queries, net1, net2, stats, stats1, stats2)
    return (loss, grad[None], rtl_grad[None])


def solution(mesh):
    return jax.shard_map(
        body,
        mesh=mesh,
        in_specs=(
            P("dp", "loop", None),
            P("dp", "loop", None),
            P("dp", "loop", None, None),
            P("dp", "loop", None),
        ),
        out_specs=(P("dp", "loop"), P("dp", "loop", None), P("dp", "loop", None)),
        check_vma=False,
    )
```

```python
import functools
import math

import jax
import jax.numpy as jnp
from jax import lax
from jax.experimental import pallas as pl
from jax.experimental.pallas import tpu as pltpu
from jax.sharding import PartitionSpec as P

BLOCK = 128
CAP = 2
CHUNK = 512
VMEM_LIMIT = 20 * 1024 * 1024
BIG_GRANT = 60 * 1024 * 1024
FAR_GRANT = 64_000_000
HARD_GRANT = 32 * 1024 * 1024
ABSENT = 1024.0
LANES = 128


def passed_along(block, axis, distance):
    devices = range(lax.axis_size(axis))
    route = [((i - distance) % len(devices), i) for i in devices]
    return lax.ppermute(block, axis, route)


def nt_dot(a, b):
    return lax.dot_general(a, b, (((1,), (1,)), ((), ())), preferred_element_type=jnp.float32)


def whole(space=pltpu.VMEM):
    return pl.BlockSpec(memory_space=space)


def shared(slots, entries, out, tile, place, used, seen, mark, sems, mark_sems, column, target_of, pick_of):
    mark[...] = jnp.full(mark.shape, ABSENT, mark.dtype)
    for s in range(slots):
        used[s] = 0
        seen[s] = 0
    for j in range(entries):
        t = target_of(j)
        rank = seen[t]
        seen[t] = rank + 1
        slot = ((t >> 2) * 2 + (t & 1)) * CAP + jnp.minimum(rank, CAP - 1)
        place[j] = jnp.where(((t >> 1) & 1) == column, slot, -1)

        @pl.when(place[j] >= 0)
        def _(j=j):
            used[place[j]] = 1
            pltpu.make_async_copy(tile.at[pl.ds(pl.multiple_of(pick_of(j) * BLOCK, BLOCK), BLOCK)], out.at[place[j]], sems.at[j]).start()

    rows, lanes = mark.shape
    for s in range(slots):
        @pl.when(used[s] == 0)
        def _(s=s):
            pltpu.make_async_copy(mark, out.at[s, pl.ds(0, rows), pl.ds(0, lanes)], mark_sems.at[s]).start()

    def finish():
        for j in range(entries):
            @pl.when(place[j] >= 0)
            def _(j=j):
                pltpu.make_async_copy(tile.at[pl.ds(pl.multiple_of(pick_of(j) * BLOCK, BLOCK), BLOCK)], out.at[place[j]], sems.at[j]).wait()

        for s in range(slots):
            @pl.when(used[s] == 0)
            def _(s=s):
                pltpu.make_async_copy(mark, out.at[s, pl.ds(0, rows), pl.ds(0, lanes)], mark_sems.at[s]).wait()

    return finish


def own_kernel(entries, me, targets, picks, rtl, out, mail, target_s, pick_s, tile, head, place, used, seen, mark, sems, mark_sems, in_sems):
    lists = [pltpu.make_async_copy(targets, target_s, in_sems.at[0]), pltpu.make_async_copy(picks, pick_s, in_sems.at[1])]
    load = pltpu.make_async_copy(rtl, tile, in_sems.at[2])
    for copy in lists + [load]:
        copy.start()
    for copy in lists:
        copy.wait()
    load.wait()
    size = tile.shape[0]
    store = pltpu.make_async_copy(tile, mail.at[pl.ds(0, size)], in_sems.at[3])
    store.start()
    column = (me[0] >> 1) & 1
    finish = shared(out.shape[0], entries, out, tile, place, used, seen, mark, sems, mark_sems, column, lambda j: target_s[j], lambda j: pick_s[j])
    lane = lax.broadcasted_iota(jnp.int32, head.shape, 1)
    line = jnp.zeros(head.shape, jnp.int32)
    for j in range(entries):
        line = jnp.where(lane == j, target_s[j], line)
        line = jnp.where(lane == entries + j, pick_s[j], line)
    head[...] = line.astype(jnp.float32).astype(head.dtype)
    rows, lanes = head.shape
    note = pltpu.make_async_copy(head, mail.at[pl.ds(size, rows), pl.ds(0, lanes)], in_sems.at[4])
    note.start()
    finish()
    store.wait()
    note.wait()


def pack_own(me, targets, picks, tile, places):
    entries = targets.shape[0]
    rows, feature = tile.shape
    slots = places * CAP
    hbm = whole(pltpu.HBM)
    return pl.pallas_call(
        functools.partial(own_kernel, entries),
        out_shape=(jax.ShapeDtypeStruct((slots, BLOCK, feature), tile.dtype), jax.ShapeDtypeStruct((rows + 16, feature), tile.dtype)),
        in_specs=[whole(pltpu.SMEM), hbm, hbm, hbm],
        out_specs=(hbm, hbm),
        scratch_shapes=[
            pltpu.SMEM((entries,), jnp.int32),
            pltpu.SMEM((entries,), jnp.int32),
            pltpu.VMEM(tile.shape, tile.dtype),
            pltpu.VMEM((16, 128), tile.dtype),
            pltpu.SMEM((entries,), jnp.int32),
            pltpu.SMEM((slots,), jnp.int32),
            pltpu.SMEM((slots,), jnp.int32),
            pltpu.VMEM((16, 128), tile.dtype),
            pltpu.SemaphoreType.DMA((entries,)),
            pltpu.SemaphoreType.DMA((slots,)),
            pltpu.SemaphoreType.DMA((5,)),
        ],
        compiler_params=pltpu.CompilerParams(vmem_limit_bytes=BIG_GRANT),
        name="pack_own",
    )(me, targets, picks, tile)


def far_kernel(entries, me, mail, out, list_v, list_s, tile, head, place, used, seen, mark, sems, mark_sems, in_sems):
    size = tile.shape[0]
    rows, lanes = head.shape
    note = pltpu.make_async_copy(mail.at[pl.ds(size, rows), pl.ds(0, lanes)], head, in_sems.at[0])
    load = pltpu.make_async_copy(mail.at[pl.ds(0, size)], tile, in_sems.at[1])
    note.start()
    load.start()
    note.wait()
    list_v[...] = head[...].astype(jnp.float32)[:8].astype(jnp.int32)
    down = pltpu.make_async_copy(list_v, list_s, in_sems.at[2])
    down.start()
    down.wait()
    load.wait()
    column = (me[0] >> 1) & 1
    shared(out.shape[0], entries, out, tile, place, used, seen, mark, sems, mark_sems, column, lambda j: list_s[0, j], lambda j: list_s[0, entries + j])()


def pack_far(me, mail, places, entries):
    rows, feature = mail.shape
    slots = places * CAP
    hbm = whole(pltpu.HBM)
    return pl.pallas_call(
        functools.partial(far_kernel, entries),
        out_shape=jax.ShapeDtypeStruct((slots, BLOCK, feature), mail.dtype),
        in_specs=[whole(pltpu.SMEM), hbm],
        out_specs=hbm,
        scratch_shapes=[
            pltpu.VMEM((8, 128), jnp.int32),
            pltpu.SMEM((8, 128), jnp.int32),
            pltpu.VMEM((rows - 16, feature), mail.dtype),
            pltpu.VMEM((16, 128), mail.dtype),
            pltpu.SMEM((entries,), jnp.int32),
            pltpu.SMEM((slots,), jnp.int32),
            pltpu.SMEM((slots,), jnp.int32),
            pltpu.VMEM((16, 128), mail.dtype),
            pltpu.SemaphoreType.DMA((entries,)),
            pltpu.SemaphoreType.DMA((slots,)),
            pltpu.SemaphoreType.DMA((3,)),
        ],
        compiler_params=pltpu.CompilerParams(vmem_limit_bytes=FAR_GRANT),
        name="pack_far",
    )(me, mail)


def cycle_kernel(rate, scale, tiles, end, q_ref, *refs):
    q = q_ref[...]
    rows, feature = q.shape
    first = pl.multiple_of(pl.program_id(0) * rows, rows)
    keys = [ref[...] for ref in refs[:tiles]]
    scores = [nt_dot(q, k) for k in keys]
    m = jnp.max(functools.reduce(jnp.maximum, scores), axis=1, keepdims=True)
    states = refs[tiles : tiles + 2] if end else ()
    for state in states:
        m = jnp.maximum(m, state[:, feature : feature + 1])
    exps = [jnp.exp2((s - m) * rate) for s in scores]
    l = jnp.sum(functools.reduce(jnp.add, exps), axis=1, keepdims=True)
    num = jnp.dot(exps[0].astype(jnp.bfloat16), keys[0], preferred_element_type=jnp.float32)
    for e, k in zip(exps[1:], keys[1:]):
        num += jnp.dot(e.astype(jnp.bfloat16), k, preferred_element_type=jnp.float32)
    for state in states:
        shrink = jnp.exp2((state[:, feature : feature + 1] - m) * rate)
        l += state[:, feature + 1 : feature + 2] * shrink
        num += state[:, :feature] * shrink
    lane = lax.broadcasted_iota(jnp.int32, (rows, LANES), 1)
    if not end:
        state_ref = refs[-1]
        own = refs[0][pl.ds(first, rows), :].astype(jnp.float32)
        positive = jnp.sum(q.astype(jnp.float32) * own, axis=1, keepdims=True)
        state_ref[:, :feature] = num
        state_ref[:, feature:] = jnp.where(lane == 0, m, jnp.where(lane == 1, l, positive))
        return
    positive = states[0][:, feature + 2 : feature + 3]
    own_ref, grad_ref, loss_ref, stats_ref = refs[tiles + 2 :]
    inverse = 1.0 / l
    grad_ref[...] = (num * inverse - own_ref[...].astype(jnp.float32)) * scale
    loss = (m - positive) * scale + jnp.log(l)
    table = jnp.where(lane == 0, m, jnp.where(lane == 1, inverse, loss))
    flipped = table.T
    stats_ref[...] = flipped[:8]
    loss_ref[...] = flipped[2:3]


def cycle_part(rate, scale, q, keys, states=(), own=None, rows=256):
    n, feature = q.shape
    f32 = jnp.float32
    tiles = len(keys)
    block = pl.BlockSpec((rows, feature), lambda i: (i, 0))
    wide = pl.BlockSpec((rows, feature + LANES), lambda i: (i, 0))
    full = pl.BlockSpec((n, feature), lambda i: (0, 0), pipeline_mode=pl.Buffered(1))
    end = own is not None
    args, specs = [q, *keys, *states], [block] + [full] * tiles + [wide] * len(states)
    shapes, outs = jax.ShapeDtypeStruct((n, feature + LANES), f32), wide
    if end:
        args, specs = args + [own], specs + [block]
        shapes = (jax.ShapeDtypeStruct((n, feature), f32), jax.ShapeDtypeStruct((1, n), f32), jax.ShapeDtypeStruct((8, n), f32))
        outs = (block, pl.BlockSpec((1, rows), lambda i: (0, i)), pl.BlockSpec((8, rows), lambda i: (0, i)))
    return pl.pallas_call(
        functools.partial(cycle_kernel, rate, scale, tiles, end),
        grid=(n // rows,),
        out_shape=shapes,
        in_specs=specs,
        out_specs=outs,
        compiler_params=pltpu.CompilerParams(vmem_limit_bytes=VMEM_LIMIT),
        cost_estimate=pl.CostEstimate(flops=4 * n * tiles * n * feature, bytes_accessed=8 * n * feature, transcendentals=tiles * n * n),
        name="cycle_last" if end else "cycle_own",
    )(*args)


def hard_kernel(rate, fresh, q_hbm, *refs):
    state_in = None if fresh else refs[0]
    blocks, state, q_ref, keys, scores, order, sems = refs[-7:]
    n, feature = q_ref.shape
    slots = blocks.shape[0]
    per = CHUNK // BLOCK
    load_keys = pltpu.make_async_copy(blocks, keys, sems.at[0])
    load_q = pltpu.make_async_copy(q_hbm, q_ref, sems.at[1])
    load_keys.start()
    load_q.start()
    if not fresh:
        load_state = pltpu.make_async_copy(state_in, state, sems.at[2])
        load_state.start()
    load_keys.wait()
    there = [(jnp.max(keys[s, :16, :128].astype(jnp.float32)) < ABSENT / 2).astype(jnp.int32) for s in range(slots)]
    live = jnp.int32(0)
    for s in range(slots):
        order[live] = s
        live += there[s]
    chunks = (live + per - 1) // per
    tail = order[jnp.maximum(live - 1, 0)]
    for p in range(per - 1):
        order[live + p] = tail

    def chunk_keys(i):
        return jnp.concatenate([keys[order[i * per + p]] for p in range(per)], axis=0)

    load_q.wait()
    q = q_ref[...]

    def score(i, m):
        s = nt_dot(q, chunk_keys(i))
        scores[i] = s
        for c in range(per):
            m = jnp.maximum(m, s[:, c * BLOCK : (c + 1) * BLOCK])
        return m

    wide = lax.fori_loop(0, chunks, score, jnp.full((n, BLOCK), -jnp.inf, jnp.float32))
    m = jnp.max(wide, axis=1, keepdims=True)
    if fresh:
        state[...] = jnp.zeros(state.shape, jnp.float32)
        kept = 0.0
    else:
        load_state.wait()
        old = state[:, feature : feature + 1]
        m = jnp.maximum(m, old)
        shrink = jnp.exp2((old - m) * rate)
        kept = state[:, feature + 1 : feature + 2] * shrink
        state[:, :feature] = state[:, :feature] * shrink
    for p in range(1, per):
        @pl.when(((chunks - 1) * per + p >= live) & (chunks > 0))
        def _(p=p):
            scores[chunks - 1, :, p * BLOCK : (p + 1) * BLOCK] = jnp.full((n, BLOCK), -jnp.inf, jnp.float32)

    def weigh(i, l):
        e = jnp.exp2((scores[i] - m) * rate)
        state[:, :feature] += jnp.dot(e.astype(jnp.bfloat16), chunk_keys(i), preferred_element_type=jnp.float32)
        for c in range(per):
            l = l + e[:, c * BLOCK : (c + 1) * BLOCK]
        return l

    l = lax.fori_loop(0, chunks, weigh, jnp.zeros((n, BLOCK), jnp.float32))
    total = jnp.sum(l, axis=1, keepdims=True) + kept
    lane = lax.broadcasted_iota(jnp.int32, (n, LANES), 1)
    state[:, feature:] = jnp.where(lane == 0, m, jnp.where(lane == 1, total, state[:, feature:]))


def hard_part(rate, q, states, blocks, name):
    n, feature = q.shape
    slots = blocks.shape[0]
    f32 = jnp.float32
    keys = slots * BLOCK
    return pl.pallas_call(
        functools.partial(hard_kernel, rate, not states),
        out_shape=jax.ShapeDtypeStruct((n, feature + LANES), f32),
        in_specs=[whole(pl.ANY)] * (2 + len(states)),
        out_specs=whole(),
        scratch_shapes=[
            pltpu.VMEM(q.shape, q.dtype),
            pltpu.VMEM(blocks.shape, blocks.dtype),
            pltpu.VMEM((keys // CHUNK, n, CHUNK), f32),
            pltpu.SMEM((slots + CHUNK // BLOCK,), jnp.int32),
            pltpu.SemaphoreType.DMA((3,)),
        ],
        compiler_params=pltpu.CompilerParams(vmem_limit_bytes=HARD_GRANT),
        cost_estimate=pl.CostEstimate(flops=2 * n * keys * feature, bytes_accessed=2 * keys * feature, transcendentals=n * keys // 2),
        name=name,
    )(q, *states, blocks)


def rtl_kernel(rate, scale, k_ref, n0_ref, n1_ref, n2_ref, s0_ref, s1_ref, s2_ref, out_ref):
    k = k_ref[...]
    first = pl.multiple_of(pl.program_id(0) * k.shape[0], k.shape[0])
    total = -n0_ref[pl.ds(first, k.shape[0]), :].astype(jnp.float32)
    for n_ref, s_ref in ((n0_ref, s0_ref), (n1_ref, s1_ref), (n2_ref, s2_ref)):
        rows = n_ref[...]
        s = nt_dot(k, rows)
        w = jnp.exp2((s - s_ref[0:1, :]) * rate) * s_ref[1:2, :]
        total += jnp.dot(w.astype(jnp.bfloat16), rows, preferred_element_type=jnp.float32)
    out_ref[...] = total * scale


def rtl_part(rate, scale, k, n0, n1, n2, s0, s1, s2, rows=256):
    n, feature = k.shape
    block = pl.BlockSpec((rows, feature), lambda i: (i, 0))
    full = pl.BlockSpec((n, feature), lambda i: (0, 0), pipeline_mode=pl.Buffered(1))
    stat = pl.BlockSpec((8, n), lambda i: (0, 0), pipeline_mode=pl.Buffered(1))
    return pl.pallas_call(
        functools.partial(rtl_kernel, rate, scale),
        grid=(n // rows,),
        out_shape=jax.ShapeDtypeStruct((n, feature), jnp.float32),
        in_specs=[block, full, full, full, stat, stat, stat],
        out_specs=block,
        compiler_params=pltpu.CompilerParams(vmem_limit_bytes=VMEM_LIMIT),
        cost_estimate=pl.CostEstimate(flops=4 * n * 3 * n * feature, bytes_accessed=6 * n * feature * 2, transcendentals=3 * n * n),
        name="rtl",
    )(k, n0, n1, n2, s0, s1, s2)


def body(netlist, rtl, hard_target, hard_block):
    queries = netlist[0]
    own_keys = rtl[0]
    feature = queries.shape[1]
    scale = 3.0 / math.sqrt(feature)
    rate = scale * math.log2(math.e)
    groups = lax.axis_size("dp")
    targets = hard_target[0, 0, :, 0]
    picks = hard_block[0, 0]
    columns = [[g for g in range(groups) if (g // 2) % 2 == x] for x in range(2)]
    places = groups // 2

    def spread(packed):
        return lax.all_to_all(packed, "dp", split_axis=0, concat_axis=0, axis_index_groups=columns, tiled=True)

    at = jnp.full((1,), lax.axis_index("dp"), jnp.int32)
    packed, mail = pack_own(at, targets, picks, own_keys, places)
    first = spread(packed)
    mail = lax.ppermute(mail, "dp", [(g, g ^ 2) for g in range(groups)])
    size = lax.axis_size("loop")
    line = size // 2
    spot = lax.axis_index("loop") % line
    up = [(i, i + 1) for i in range(size) if i % line < line - 1]
    down = [(i, i - 1) for i in range(size) if i % line > 0]
    seam = [(i, (i + 1) % size) for i in range(line - 1, size, line)] + [(i, (i - 1) % size) for i in range(0, size, line)]
    rtl1 = lax.ppermute(own_keys, "loop", up)
    net1 = lax.ppermute(queries, "loop", down)
    edge = jnp.where(spot == 0, queries, own_keys)
    mail, rtl1, net1, edge = lax.optimization_barrier((mail, rtl1, net1, edge))
    edge = lax.ppermute(edge, "loop", seam)
    second = spread(pack_far(at, mail, places, targets.shape[0]))

    state = cycle_part(rate, scale, queries, [own_keys])
    state = hard_part(rate, queries, [state], first, "hard_first")
    edge, state = lax.optimization_barrier((edge, state))
    rtl1 = jnp.where(spot == 0, edge, rtl1)
    net1 = jnp.where(spot == line - 1, edge, net1)
    rtl2 = passed_along(rtl1, "loop", 1)
    net2 = passed_along(net1, "loop", -1)
    others = hard_part(rate, queries, [], second, "hard_second")
    grad, loss, stats = cycle_part(rate, scale, queries, [rtl1, rtl2], [state, others], own_keys)
    stats1 = passed_along(stats, "loop", -1)
    stats2 = passed_along(stats, "loop", -2)
    rtl_grad = rtl_part(rate, scale, own_keys, queries, net1, net2, stats, stats1, stats2)
    return (loss, grad[None], rtl_grad[None])


def solution(mesh):
    return jax.shard_map(
        body,
        mesh=mesh,
        in_specs=(
            P("dp", "loop", None),
            P("dp", "loop", None),
            P("dp", "loop", None, None),
            P("dp", "loop", None),
        ),
        out_specs=(P("dp", "loop"), P("dp", "loop", None), P("dp", "loop", None)),
        check_vma=False,
    )
```

```python
import functools
import math

import jax
import jax.numpy as jnp
from jax import lax
from jax.experimental import pallas as pl
from jax.experimental.pallas import tpu as pltpu
from jax.sharding import PartitionSpec as P

BLOCK = 128
CAP = 2
CHUNK = 512
VMEM_LIMIT = 20 * 1024 * 1024
BIG_GRANT = 60 * 1024 * 1024
FAR_GRANT = 64_000_000
HARD_GRANT = 32 * 1024 * 1024
ABSENT = 1024.0
LANES = 128


def passed_along(block, axis, distance):
    devices = range(lax.axis_size(axis))
    route = [((i - distance) % len(devices), i) for i in devices]
    return lax.ppermute(block, axis, route)


def nt_dot(a, b):
    return lax.dot_general(a, b, (((1,), (1,)), ((), ())), preferred_element_type=jnp.float32)


def whole(space=pltpu.VMEM):
    return pl.BlockSpec(memory_space=space)


def shared(slots, entries, out, tile, place, used, seen, mark, sems, mark_sems, column, target_of, pick_of):
    mark[...] = jnp.full(mark.shape, ABSENT, mark.dtype)
    for s in range(slots):
        used[s] = 0
        seen[s] = 0
    for j in range(entries):
        t = target_of(j)
        rank = seen[t]
        seen[t] = rank + 1
        slot = ((t >> 2) * 2 + (t & 1)) * CAP + jnp.minimum(rank, CAP - 1)
        place[j] = jnp.where(((t >> 1) & 1) == column, slot, -1)

        @pl.when(place[j] >= 0)
        def _(j=j):
            used[place[j]] = 1
            pltpu.make_async_copy(tile.at[pl.ds(pl.multiple_of(pick_of(j) * BLOCK, BLOCK), BLOCK)], out.at[place[j]], sems.at[j]).start()

    rows, lanes = mark.shape
    for s in range(slots):
        @pl.when(used[s] == 0)
        def _(s=s):
            pltpu.make_async_copy(mark, out.at[s, pl.ds(0, rows), pl.ds(0, lanes)], mark_sems.at[s]).start()

    def finish():
        for j in range(entries):
            @pl.when(place[j] >= 0)
            def _(j=j):
                pltpu.make_async_copy(tile.at[pl.ds(pl.multiple_of(pick_of(j) * BLOCK, BLOCK), BLOCK)], out.at[place[j]], sems.at[j]).wait()

        for s in range(slots):
            @pl.when(used[s] == 0)
            def _(s=s):
                pltpu.make_async_copy(mark, out.at[s, pl.ds(0, rows), pl.ds(0, lanes)], mark_sems.at[s]).wait()

    return finish


def own_kernel(entries, me, targets, picks, rtl, out, mail, target_s, pick_s, tile, head, place, used, seen, mark, sems, mark_sems, in_sems):
    lists = [pltpu.make_async_copy(targets, target_s, in_sems.at[0]), pltpu.make_async_copy(picks, pick_s, in_sems.at[1])]
    load = pltpu.make_async_copy(rtl, tile, in_sems.at[2])
    for copy in lists + [load]:
        copy.start()
    for copy in lists:
        copy.wait()
    load.wait()
    size = tile.shape[0]
    store = pltpu.make_async_copy(tile, mail.at[pl.ds(0, size)], in_sems.at[3])
    store.start()
    column = (me[0] >> 1) & 1
    finish = shared(out.shape[0], entries, out, tile, place, used, seen, mark, sems, mark_sems, column, lambda j: target_s[j], lambda j: pick_s[j])
    lane = lax.broadcasted_iota(jnp.int32, head.shape, 1)
    line = jnp.zeros(head.shape, jnp.int32)
    for j in range(entries):
        line = jnp.where(lane == j, target_s[j], line)
        line = jnp.where(lane == entries + j, pick_s[j], line)
    head[...] = line.astype(jnp.float32).astype(head.dtype)
    rows, lanes = head.shape
    note = pltpu.make_async_copy(head, mail.at[pl.ds(size, rows), pl.ds(0, lanes)], in_sems.at[4])
    note.start()
    finish()
    store.wait()
    note.wait()


def pack_own(me, targets, picks, tile, places):
    entries = targets.shape[0]
    rows, feature = tile.shape
    slots = places * CAP
    hbm = whole(pltpu.HBM)
    return pl.pallas_call(
        functools.partial(own_kernel, entries),
        out_shape=(jax.ShapeDtypeStruct((slots, BLOCK, feature), tile.dtype), jax.ShapeDtypeStruct((rows + 16, feature), tile.dtype)),
        in_specs=[whole(pltpu.SMEM), hbm, hbm, hbm],
        out_specs=(hbm, hbm),
        scratch_shapes=[
            pltpu.SMEM((entries,), jnp.int32),
            pltpu.SMEM((entries,), jnp.int32),
            pltpu.VMEM(tile.shape, tile.dtype),
            pltpu.VMEM((16, 128), tile.dtype),
            pltpu.SMEM((entries,), jnp.int32),
            pltpu.SMEM((slots,), jnp.int32),
            pltpu.SMEM((slots,), jnp.int32),
            pltpu.VMEM((16, 128), tile.dtype),
            pltpu.SemaphoreType.DMA((entries,)),
            pltpu.SemaphoreType.DMA((slots,)),
            pltpu.SemaphoreType.DMA((5,)),
        ],
        compiler_params=pltpu.CompilerParams(vmem_limit_bytes=BIG_GRANT),
        name="pack_own",
    )(me, targets, picks, tile)


def far_kernel(entries, me, mail, out, list_v, list_s, tile, head, place, used, seen, mark, sems, mark_sems, in_sems):
    size = tile.shape[0]
    rows, lanes = head.shape
    note = pltpu.make_async_copy(mail.at[pl.ds(size, rows), pl.ds(0, lanes)], head, in_sems.at[0])
    load = pltpu.make_async_copy(mail.at[pl.ds(0, size)], tile, in_sems.at[1])
    note.start()
    load.start()
    note.wait()
    list_v[...] = head[...].astype(jnp.float32)[:8].astype(jnp.int32)
    down = pltpu.make_async_copy(list_v, list_s, in_sems.at[2])
    down.start()
    down.wait()
    load.wait()
    column = (me[0] >> 1) & 1
    shared(out.shape[0], entries, out, tile, place, used, seen, mark, sems, mark_sems, column, lambda j: list_s[0, j], lambda j: list_s[0, entries + j])()


def pack_far(me, mail, places, entries):
    rows, feature = mail.shape
    slots = places * CAP
    hbm = whole(pltpu.HBM)
    return pl.pallas_call(
        functools.partial(far_kernel, entries),
        out_shape=jax.ShapeDtypeStruct((slots, BLOCK, feature), mail.dtype),
        in_specs=[whole(pltpu.SMEM), hbm],
        out_specs=hbm,
        scratch_shapes=[
            pltpu.VMEM((8, 128), jnp.int32),
            pltpu.SMEM((8, 128), jnp.int32),
            pltpu.VMEM((rows - 16, feature), mail.dtype),
            pltpu.VMEM((16, 128), mail.dtype),
            pltpu.SMEM((entries,), jnp.int32),
            pltpu.SMEM((slots,), jnp.int32),
            pltpu.SMEM((slots,), jnp.int32),
            pltpu.VMEM((16, 128), mail.dtype),
            pltpu.SemaphoreType.DMA((entries,)),
            pltpu.SemaphoreType.DMA((slots,)),
            pltpu.SemaphoreType.DMA((3,)),
        ],
        compiler_params=pltpu.CompilerParams(vmem_limit_bytes=FAR_GRANT),
        name="pack_far",
    )(me, mail)


def cycle_kernel(rate, scale, tiles, end, q_ref, *refs):
    q = q_ref[...]
    rows, feature = q.shape
    first = pl.multiple_of(pl.program_id(0) * rows, rows)
    keys = [ref[...] for ref in refs[:tiles]]
    scores = [nt_dot(q, k) for k in keys]
    m = jnp.max(functools.reduce(jnp.maximum, scores), axis=1, keepdims=True)
    states = refs[tiles : tiles + 2] if end else ()
    for state in states:
        m = jnp.maximum(m, state[:, feature : feature + 1])
    exps = [jnp.exp2((s - m) * rate) for s in scores]
    l = jnp.sum(functools.reduce(jnp.add, exps), axis=1, keepdims=True)
    num = jnp.dot(exps[0].astype(jnp.bfloat16), keys[0], preferred_element_type=jnp.float32)
    for e, k in zip(exps[1:], keys[1:]):
        num += jnp.dot(e.astype(jnp.bfloat16), k, preferred_element_type=jnp.float32)
    for state in states:
        shrink = jnp.exp2((state[:, feature : feature + 1] - m) * rate)
        l += state[:, feature + 1 : feature + 2] * shrink
        num += state[:, :feature] * shrink
    lane = lax.broadcasted_iota(jnp.int32, (rows, LANES), 1)
    if not end:
        state_ref = refs[-1]
        own = refs[0][pl.ds(first, rows), :].astype(jnp.float32)
        positive = jnp.sum(q.astype(jnp.float32) * own, axis=1, keepdims=True)
        state_ref[:, :feature] = num
        state_ref[:, feature:] = jnp.where(lane == 0, m, jnp.where(lane == 1, l, positive))
        return
    positive = states[0][:, feature + 2 : feature + 3]
    own_ref, grad_ref, loss_ref, stats_ref = refs[tiles + 2 :]
    inverse = 1.0 / l
    grad_ref[...] = (num * inverse - own_ref[...].astype(jnp.float32)) * scale
    loss = (m - positive) * scale + jnp.log(l)
    table = jnp.where(lane == 0, m, jnp.where(lane == 1, inverse, loss))
    flipped = table.T
    stats_ref[...] = flipped[:8]
    loss_ref[...] = flipped[2:3]


def cycle_part(rate, scale, q, keys, states=(), own=None, rows=256):
    n, feature = q.shape
    f32 = jnp.float32
    tiles = len(keys)
    block = pl.BlockSpec((rows, feature), lambda i: (i, 0))
    wide = pl.BlockSpec((rows, feature + LANES), lambda i: (i, 0))
    full = pl.BlockSpec((n, feature), lambda i: (0, 0), pipeline_mode=pl.Buffered(1))
    end = own is not None
    args, specs = [q, *keys, *states], [block] + [full] * tiles + [wide] * len(states)
    shapes, outs = jax.ShapeDtypeStruct((n, feature + LANES), f32), wide
    if end:
        args, specs = args + [own], specs + [block]
        shapes = (jax.ShapeDtypeStruct((n, feature), f32), jax.ShapeDtypeStruct((1, n), f32), jax.ShapeDtypeStruct((8, n), f32))
        outs = (block, pl.BlockSpec((1, rows), lambda i: (0, i)), pl.BlockSpec((8, rows), lambda i: (0, i)))
    return pl.pallas_call(
        functools.partial(cycle_kernel, rate, scale, tiles, end),
        grid=(n // rows,),
        out_shape=shapes,
        in_specs=specs,
        out_specs=outs,
        compiler_params=pltpu.CompilerParams(vmem_limit_bytes=VMEM_LIMIT),
        cost_estimate=pl.CostEstimate(flops=4 * n * tiles * n * feature, bytes_accessed=8 * n * feature, transcendentals=tiles * n * n),
        name="cycle_last" if end else "cycle_own",
    )(*args)


def hard_kernel(rate, fresh, q_hbm, *refs):
    state_in = None if fresh else refs[0]
    blocks, state, q_ref, keys, scores, order, sems = refs[-7:]
    n, feature = q_ref.shape
    slots = blocks.shape[0]
    per = CHUNK // BLOCK
    load_keys = pltpu.make_async_copy(blocks, keys, sems.at[0])
    load_q = pltpu.make_async_copy(q_hbm, q_ref, sems.at[1])
    load_keys.start()
    load_q.start()
    if not fresh:
        load_state = pltpu.make_async_copy(state_in, state, sems.at[2])
        load_state.start()
    load_keys.wait()
    there = [(jnp.max(keys[s, :16, :128].astype(jnp.float32)) < ABSENT / 2).astype(jnp.int32) for s in range(slots)]
    live = jnp.int32(0)
    for s in range(slots):
        order[live] = s
        live += there[s]
    chunks = (live + per - 1) // per
    tail = order[jnp.maximum(live - 1, 0)]
    for p in range(per - 1):
        order[live + p] = tail

    def chunk_keys(i):
        return jnp.concatenate([keys[order[i * per + p]] for p in range(per)], axis=0)

    load_q.wait()
    q = q_ref[...]

    def score(i, m):
        s = nt_dot(q, chunk_keys(i))
        scores[i] = s
        for c in range(per):
            m = jnp.maximum(m, s[:, c * BLOCK : (c + 1) * BLOCK])
        return m

    wide = lax.fori_loop(0, chunks, score, jnp.full((n, BLOCK), -jnp.inf, jnp.float32))
    m = jnp.max(wide, axis=1, keepdims=True)
    if fresh:
        state[...] = jnp.zeros(state.shape, jnp.float32)
        kept = 0.0
    else:
        load_state.wait()
        old = state[:, feature : feature + 1]
        m = jnp.maximum(m, old)
        shrink = jnp.exp2((old - m) * rate)
        kept = state[:, feature + 1 : feature + 2] * shrink
        state[:, :feature] = state[:, :feature] * shrink
    for p in range(1, per):
        @pl.when(((chunks - 1) * per + p >= live) & (chunks > 0))
        def _(p=p):
            scores[chunks - 1, :, p * BLOCK : (p + 1) * BLOCK] = jnp.full((n, BLOCK), -jnp.inf, jnp.float32)

    def weigh(i, l):
        e = jnp.exp2((scores[i] - m) * rate)
        state[:, :feature] += jnp.dot(e.astype(jnp.bfloat16), chunk_keys(i), preferred_element_type=jnp.float32)
        for c in range(per):
            l = l + e[:, c * BLOCK : (c + 1) * BLOCK]
        return l

    l = lax.fori_loop(0, chunks, weigh, jnp.zeros((n, BLOCK), jnp.float32))
    total = jnp.sum(l, axis=1, keepdims=True) + kept
    lane = lax.broadcasted_iota(jnp.int32, (n, LANES), 1)
    state[:, feature:] = jnp.where(lane == 0, m, jnp.where(lane == 1, total, state[:, feature:]))


def hard_part(rate, q, states, blocks, name):
    n, feature = q.shape
    slots = blocks.shape[0]
    f32 = jnp.float32
    keys = slots * BLOCK
    return pl.pallas_call(
        functools.partial(hard_kernel, rate, not states),
        out_shape=jax.ShapeDtypeStruct((n, feature + LANES), f32),
        in_specs=[whole(pl.ANY)] * (2 + len(states)),
        out_specs=whole(),
        scratch_shapes=[
            pltpu.VMEM(q.shape, q.dtype),
            pltpu.VMEM(blocks.shape, blocks.dtype),
            pltpu.VMEM((keys // CHUNK, n, CHUNK), f32),
            pltpu.SMEM((slots + CHUNK // BLOCK,), jnp.int32),
            pltpu.SemaphoreType.DMA((3,)),
        ],
        compiler_params=pltpu.CompilerParams(vmem_limit_bytes=HARD_GRANT),
        cost_estimate=pl.CostEstimate(flops=2 * n * keys * feature, bytes_accessed=2 * keys * feature, transcendentals=n * keys // 2),
        name=name,
    )(q, *states, blocks)


def rtl_kernel(rate, scale, k_ref, n0_ref, n1_ref, n2_ref, s0_ref, s1_ref, s2_ref, out_ref):
    k = k_ref[...]
    first = pl.multiple_of(pl.program_id(0) * k.shape[0], k.shape[0])
    total = -n0_ref[pl.ds(first, k.shape[0]), :].astype(jnp.float32)
    for n_ref, s_ref in ((n0_ref, s0_ref), (n1_ref, s1_ref), (n2_ref, s2_ref)):
        rows = n_ref[...]
        s = nt_dot(k, rows)
        w = jnp.exp2((s - s_ref[0:1, :]) * rate) * s_ref[1:2, :]
        total += jnp.dot(w.astype(jnp.bfloat16), rows, preferred_element_type=jnp.float32)
    out_ref[...] = total * scale


def rtl_part(rate, scale, k, n0, n1, n2, s0, s1, s2, rows=256):
    n, feature = k.shape
    block = pl.BlockSpec((rows, feature), lambda i: (i, 0))
    full = pl.BlockSpec((n, feature), lambda i: (0, 0), pipeline_mode=pl.Buffered(1))
    stat = pl.BlockSpec((8, n), lambda i: (0, 0), pipeline_mode=pl.Buffered(1))
    return pl.pallas_call(
        functools.partial(rtl_kernel, rate, scale),
        grid=(n // rows,),
        out_shape=jax.ShapeDtypeStruct((n, feature), jnp.float32),
        in_specs=[block, full, full, full, stat, stat, stat],
        out_specs=block,
        compiler_params=pltpu.CompilerParams(vmem_limit_bytes=VMEM_LIMIT),
        cost_estimate=pl.CostEstimate(flops=4 * n * 3 * n * feature, bytes_accessed=6 * n * feature * 2, transcendentals=3 * n * n),
        name="rtl",
    )(k, n0, n1, n2, s0, s1, s2)


def body(netlist, rtl, hard_target, hard_block):
    queries = netlist[0]
    own_keys = rtl[0]
    feature = queries.shape[1]
    scale = 3.0 / math.sqrt(feature)
    rate = scale * math.log2(math.e)
    groups = lax.axis_size("dp")
    targets = hard_target[0, 0, :, 0]
    picks = hard_block[0, 0]
    columns = [[g for g in range(groups) if (g // 2) % 2 == x] for x in range(2)]
    places = groups // 2

    def spread(packed):
        return lax.all_to_all(packed, "dp", split_axis=0, concat_axis=0, axis_index_groups=columns, tiled=True)

    at = jnp.full((1,), lax.axis_index("dp"), jnp.int32)
    packed, mail = pack_own(at, targets, picks, own_keys, places)
    first = spread(packed)
    mail = lax.ppermute(mail, "dp", [(g, g ^ 2) for g in range(groups)])
    rtl1 = passed_along(own_keys, "loop", 1)
    mail, rtl1, back = lax.optimization_barrier((mail, rtl1, queries))
    second = spread(pack_far(at, mail, places, targets.shape[0]))
    rtl2 = passed_along(rtl1, "loop", 1)
    net1 = passed_along(back, "loop", -1)

    state = cycle_part(rate, scale, queries, [own_keys, rtl1])
    state = hard_part(rate, queries, [state], first, "hard_first")
    net1, state = lax.optimization_barrier((net1, state))
    net2 = passed_along(net1, "loop", -1)
    others = hard_part(rate, queries, [], second, "hard_second")
    grad, loss, stats = cycle_part(rate, scale, queries, [rtl2], [state, others], own_keys)
    stats1 = passed_along(stats, "loop", -1)
    stats2 = passed_along(stats, "loop", -2)
    rtl_grad = rtl_part(rate, scale, own_keys, queries, net1, net2, stats, stats1, stats2)
    return (loss, grad[None], rtl_grad[None])


def solution(mesh):
    return jax.shard_map(
        body,
        mesh=mesh,
        in_specs=(
            P("dp", "loop", None),
            P("dp", "loop", None),
            P("dp", "loop", None, None),
            P("dp", "loop", None),
        ),
        out_specs=(P("dp", "loop"), P("dp", "loop", None), P("dp", "loop", None)),
        check_vma=False,
    )
```

```python
import functools
import math

import jax
import jax.numpy as jnp
from jax import lax
from jax.experimental import pallas as pl
from jax.experimental.pallas import tpu as pltpu
from jax.sharding import PartitionSpec as P

BLOCK = 128
CAP = 2
CHUNK = 512
VMEM_LIMIT = 20 * 1024 * 1024
BIG_GRANT = 60 * 1024 * 1024
FAR_GRANT = 64_000_000
HARD_GRANT = 32 * 1024 * 1024
ABSENT = 1024.0
LANES = 128


def passed_along(block, axis, distance):
    devices = range(lax.axis_size(axis))
    route = [((i - distance) % len(devices), i) for i in devices]
    return lax.ppermute(block, axis, route)


def nt_dot(a, b):
    return lax.dot_general(a, b, (((1,), (1,)), ((), ())), preferred_element_type=jnp.float32)


def whole(space=pltpu.VMEM):
    return pl.BlockSpec(memory_space=space)


def shared(slots, entries, out, tile, place, used, seen, mark, sems, mark_sems, column, target_of, pick_of):
    mark[...] = jnp.full(mark.shape, ABSENT, mark.dtype)
    for s in range(slots):
        used[s] = 0
        seen[s] = 0
    for j in range(entries):
        t = target_of(j)
        rank = seen[t]
        seen[t] = rank + 1
        slot = ((t >> 2) * 2 + (t & 1)) * CAP + jnp.minimum(rank, CAP - 1)
        place[j] = jnp.where(((t >> 1) & 1) == column, slot, -1)

        @pl.when(place[j] >= 0)
        def _(j=j):
            used[place[j]] = 1
            pltpu.make_async_copy(tile.at[pl.ds(pl.multiple_of(pick_of(j) * BLOCK, BLOCK), BLOCK)], out.at[place[j]], sems.at[j]).start()

    rows, lanes = mark.shape
    for s in range(slots):
        @pl.when(used[s] == 0)
        def _(s=s):
            pltpu.make_async_copy(mark, out.at[s, pl.ds(0, rows), pl.ds(0, lanes)], mark_sems.at[s]).start()

    def finish():
        for j in range(entries):
            @pl.when(place[j] >= 0)
            def _(j=j):
                pltpu.make_async_copy(tile.at[pl.ds(pl.multiple_of(pick_of(j) * BLOCK, BLOCK), BLOCK)], out.at[place[j]], sems.at[j]).wait()

        for s in range(slots):
            @pl.when(used[s] == 0)
            def _(s=s):
                pltpu.make_async_copy(mark, out.at[s, pl.ds(0, rows), pl.ds(0, lanes)], mark_sems.at[s]).wait()

    return finish


def own_kernel(entries, me, targets, picks, rtl, out, mail, target_s, pick_s, tile, head, place, used, seen, mark, sems, mark_sems, in_sems):
    lists = [pltpu.make_async_copy(targets, target_s, in_sems.at[0]), pltpu.make_async_copy(picks, pick_s, in_sems.at[1])]
    load = pltpu.make_async_copy(rtl, tile, in_sems.at[2])
    for copy in lists + [load]:
        copy.start()
    for copy in lists:
        copy.wait()
    load.wait()
    size = tile.shape[0]
    store = pltpu.make_async_copy(tile, mail.at[pl.ds(0, size)], in_sems.at[3])
    store.start()
    column = (me[0] >> 1) & 1
    finish = shared(out.shape[0], entries, out, tile, place, used, seen, mark, sems, mark_sems, column, lambda j: target_s[j], lambda j: pick_s[j])
    lane = lax.broadcasted_iota(jnp.int32, head.shape, 1)
    line = jnp.zeros(head.shape, jnp.int32)
    for j in range(entries):
        line = jnp.where(lane == j, target_s[j], line)
        line = jnp.where(lane == entries + j, pick_s[j], line)
    head[...] = line.astype(jnp.float32).astype(head.dtype)
    rows, lanes = head.shape
    note = pltpu.make_async_copy(head, mail.at[pl.ds(size, rows), pl.ds(0, lanes)], in_sems.at[4])
    note.start()
    finish()
    store.wait()
    note.wait()


def pack_own(me, targets, picks, tile, places):
    entries = targets.shape[0]
    rows, feature = tile.shape
    slots = places * CAP
    hbm = whole(pltpu.HBM)
    return pl.pallas_call(
        functools.partial(own_kernel, entries),
        out_shape=(jax.ShapeDtypeStruct((slots, BLOCK, feature), tile.dtype), jax.ShapeDtypeStruct((rows + 16, feature), tile.dtype)),
        in_specs=[whole(pltpu.SMEM), hbm, hbm, hbm],
        out_specs=(hbm, hbm),
        scratch_shapes=[
            pltpu.SMEM((entries,), jnp.int32),
            pltpu.SMEM((entries,), jnp.int32),
            pltpu.VMEM(tile.shape, tile.dtype),
            pltpu.VMEM((16, 128), tile.dtype),
            pltpu.SMEM((entries,), jnp.int32),
            pltpu.SMEM((slots,), jnp.int32),
            pltpu.SMEM((slots,), jnp.int32),
            pltpu.VMEM((16, 128), tile.dtype),
            pltpu.SemaphoreType.DMA((entries,)),
            pltpu.SemaphoreType.DMA((slots,)),
            pltpu.SemaphoreType.DMA((5,)),
        ],
        compiler_params=pltpu.CompilerParams(vmem_limit_bytes=BIG_GRANT),
        name="pack_own",
    )(me, targets, picks, tile)


def far_kernel(entries, me, mail, out, list_v, list_s, tile, head, place, used, seen, mark, sems, mark_sems, in_sems):
    size = tile.shape[0]
    rows, lanes = head.shape
    note = pltpu.make_async_copy(mail.at[pl.ds(size, rows), pl.ds(0, lanes)], head, in_sems.at[0])
    load = pltpu.make_async_copy(mail.at[pl.ds(0, size)], tile, in_sems.at[1])
    note.start()
    load.start()
    note.wait()
    list_v[...] = head[...].astype(jnp.float32)[:8].astype(jnp.int32)
    down = pltpu.make_async_copy(list_v, list_s, in_sems.at[2])
    down.start()
    down.wait()
    load.wait()
    column = (me[0] >> 1) & 1
    shared(out.shape[0], entries, out, tile, place, used, seen, mark, sems, mark_sems, column, lambda j: list_s[0, j], lambda j: list_s[0, entries + j])()


def pack_far(me, mail, places, entries):
    rows, feature = mail.shape
    slots = places * CAP
    hbm = whole(pltpu.HBM)
    return pl.pallas_call(
        functools.partial(far_kernel, entries),
        out_shape=jax.ShapeDtypeStruct((slots, BLOCK, feature), mail.dtype),
        in_specs=[whole(pltpu.SMEM), hbm],
        out_specs=hbm,
        scratch_shapes=[
            pltpu.VMEM((8, 128), jnp.int32),
            pltpu.SMEM((8, 128), jnp.int32),
            pltpu.VMEM((rows - 16, feature), mail.dtype),
            pltpu.VMEM((16, 128), mail.dtype),
            pltpu.SMEM((entries,), jnp.int32),
            pltpu.SMEM((slots,), jnp.int32),
            pltpu.SMEM((slots,), jnp.int32),
            pltpu.VMEM((16, 128), mail.dtype),
            pltpu.SemaphoreType.DMA((entries,)),
            pltpu.SemaphoreType.DMA((slots,)),
            pltpu.SemaphoreType.DMA((3,)),
        ],
        compiler_params=pltpu.CompilerParams(vmem_limit_bytes=FAR_GRANT),
        name="pack_far",
    )(me, mail)


def cycle_kernel(rate, scale, tiles, given, end, q_ref, *refs):
    q = q_ref[...]
    rows, feature = q.shape
    first = pl.multiple_of(pl.program_id(0) * rows, rows)
    keys = [ref[...] for ref in refs[:tiles]]
    scores = [nt_dot(q, k) for k in keys]
    states = refs[tiles : tiles + given]
    peaks = [jnp.max(s, axis=1, keepdims=True) for s in scores] + [state[:, feature : feature + 1] for state in states]
    m = functools.reduce(jnp.maximum, peaks)
    l = jnp.zeros((rows, 1), jnp.float32)
    num = jnp.zeros((rows, feature), jnp.float32)
    for s, k in zip(scores, keys):
        e = jnp.exp2((s - m) * rate)
        l += jnp.sum(e, axis=1, keepdims=True)
        num += jnp.dot(e.astype(jnp.bfloat16), k, preferred_element_type=jnp.float32)
    for state in states:
        shrink = jnp.exp2((state[:, feature : feature + 1] - m) * rate)
        l += state[:, feature + 1 : feature + 2] * shrink
        num += state[:, :feature] * shrink
    lane = lax.broadcasted_iota(jnp.int32, (rows, LANES), 1)
    if not end:
        state_ref = refs[-1]
        if given:
            positive = states[0][:, feature + 2 : feature + 3]
        else:
            own = refs[0][pl.ds(first, rows), :].astype(jnp.float32)
            positive = jnp.sum(q.astype(jnp.float32) * own, axis=1, keepdims=True)
        state_ref[:, :feature] = num
        state_ref[:, feature:] = jnp.where(lane == 0, m, jnp.where(lane == 1, l, positive))
        return
    positive = states[0][:, feature + 2 : feature + 3]
    own_ref, grad_ref, loss_ref, stats_ref = refs[tiles + given :]
    inverse = 1.0 / l
    grad_ref[...] = (num * inverse - own_ref[...].astype(jnp.float32)) * scale
    loss = (m - positive) * scale + jnp.log(l)
    table = jnp.where(lane == 0, m, jnp.where(lane == 1, inverse, loss))
    flipped = table.T
    stats_ref[...] = flipped[:8]
    loss_ref[...] = flipped[2:3]


def cycle_part(rate, scale, q, keys, states=(), own=None, rows=256):
    n, feature = q.shape
    f32 = jnp.float32
    tiles = len(keys)
    block = pl.BlockSpec((rows, feature), lambda i: (i, 0))
    wide = pl.BlockSpec((rows, feature + LANES), lambda i: (i, 0))
    full = pl.BlockSpec((n, feature), lambda i: (0, 0), pipeline_mode=pl.Buffered(1))
    end = own is not None
    args, specs = [q, *keys, *states], [block] + [full] * tiles + [wide] * len(states)
    shapes, outs = jax.ShapeDtypeStruct((n, feature + LANES), f32), wide
    if end:
        args, specs = args + [own], specs + [block]
        shapes = (jax.ShapeDtypeStruct((n, feature), f32), jax.ShapeDtypeStruct((1, n), f32), jax.ShapeDtypeStruct((8, n), f32))
        outs = (block, pl.BlockSpec((1, rows), lambda i: (0, i)), pl.BlockSpec((8, rows), lambda i: (0, i)))
    return pl.pallas_call(
        functools.partial(cycle_kernel, rate, scale, tiles, len(states), end),
        grid=(n // rows,),
        out_shape=shapes,
        in_specs=specs,
        out_specs=outs,
        compiler_params=pltpu.CompilerParams(vmem_limit_bytes=VMEM_LIMIT),
        cost_estimate=pl.CostEstimate(flops=4 * n * tiles * n * feature, bytes_accessed=8 * n * feature, transcendentals=tiles * n * n),
        name="cycle_last" if end else "cycle_more" if states else "cycle_own",
    )(*args)


def hard_kernel(rate, fresh, q_hbm, *refs):
    state_in = None if fresh else refs[0]
    blocks, state, q_ref, keys, scores, order, sems = refs[-7:]
    n, feature = q_ref.shape
    slots = blocks.shape[0]
    per = CHUNK // BLOCK
    load_keys = pltpu.make_async_copy(blocks, keys, sems.at[0])
    load_q = pltpu.make_async_copy(q_hbm, q_ref, sems.at[1])
    load_keys.start()
    load_q.start()
    if not fresh:
        load_state = pltpu.make_async_copy(state_in, state, sems.at[2])
        load_state.start()
    load_keys.wait()
    there = [(jnp.max(keys[s, :16, :128].astype(jnp.float32)) < ABSENT / 2).astype(jnp.int32) for s in range(slots)]
    live = jnp.int32(0)
    for s in range(slots):
        order[live] = s
        live += there[s]
    chunks = (live + per - 1) // per
    tail = order[jnp.maximum(live - 1, 0)]
    for p in range(per - 1):
        order[live + p] = tail

    def chunk_keys(i):
        return jnp.concatenate([keys[order[i * per + p]] for p in range(per)], axis=0)

    load_q.wait()
    q = q_ref[...]

    def score(i, m):
        s = nt_dot(q, chunk_keys(i))
        scores[i] = s
        for c in range(per):
            m = jnp.maximum(m, s[:, c * BLOCK : (c + 1) * BLOCK])
        return m

    wide = lax.fori_loop(0, chunks, score, jnp.full((n, BLOCK), -jnp.inf, jnp.float32))
    m = jnp.max(wide, axis=1, keepdims=True)
    if fresh:
        state[...] = jnp.zeros(state.shape, jnp.float32)
        kept = 0.0
    else:
        load_state.wait()
        old = state[:, feature : feature + 1]
        m = jnp.maximum(m, old)
        shrink = jnp.exp2((old - m) * rate)
        kept = state[:, feature + 1 : feature + 2] * shrink
        state[:, :feature] = state[:, :feature] * shrink
    for p in range(1, per):
        @pl.when(((chunks - 1) * per + p >= live) & (chunks > 0))
        def _(p=p):
            scores[chunks - 1, :, p * BLOCK : (p + 1) * BLOCK] = jnp.full((n, BLOCK), -jnp.inf, jnp.float32)

    def weigh(i, l):
        e = jnp.exp2((scores[i] - m) * rate)
        state[:, :feature] += jnp.dot(e.astype(jnp.bfloat16), chunk_keys(i), preferred_element_type=jnp.float32)
        for c in range(per):
            l = l + e[:, c * BLOCK : (c + 1) * BLOCK]
        return l

    l = lax.fori_loop(0, chunks, weigh, jnp.zeros((n, BLOCK), jnp.float32))
    total = jnp.sum(l, axis=1, keepdims=True) + kept
    lane = lax.broadcasted_iota(jnp.int32, (n, LANES), 1)
    state[:, feature:] = jnp.where(lane == 0, m, jnp.where(lane == 1, total, state[:, feature:]))


def hard_part(rate, q, states, blocks, name):
    n, feature = q.shape
    slots = blocks.shape[0]
    f32 = jnp.float32
    keys = slots * BLOCK
    return pl.pallas_call(
        functools.partial(hard_kernel, rate, not states),
        out_shape=jax.ShapeDtypeStruct((n, feature + LANES), f32),
        in_specs=[whole(pl.ANY)] * (2 + len(states)),
        out_specs=whole(),
        scratch_shapes=[
            pltpu.VMEM(q.shape, q.dtype),
            pltpu.VMEM(blocks.shape, blocks.dtype),
            pltpu.VMEM((keys // CHUNK, n, CHUNK), f32),
            pltpu.SMEM((slots + CHUNK // BLOCK,), jnp.int32),
            pltpu.SemaphoreType.DMA((3,)),
        ],
        compiler_params=pltpu.CompilerParams(vmem_limit_bytes=HARD_GRANT),
        cost_estimate=pl.CostEstimate(flops=2 * n * keys * feature, bytes_accessed=2 * keys * feature, transcendentals=n * keys // 2),
        name=name,
    )(q, *states, blocks)


def rtl_kernel(rate, scale, tiles, k_ref, *refs):
    n_refs, s_refs = refs[:tiles], refs[tiles : 2 * tiles]
    base_ref, out_ref = refs[2 * tiles :]
    k = k_ref[...]
    total = -base_ref[...].astype(jnp.float32) if tiles == 1 else base_ref[...]
    for n_ref, s_ref in zip(n_refs, s_refs):
        rows = n_ref[...]
        s = nt_dot(k, rows)
        w = jnp.exp2((s - s_ref[0:1, :]) * rate) * s_ref[1:2, :]
        total += jnp.dot(w.astype(jnp.bfloat16), rows, preferred_element_type=jnp.float32)
    out_ref[...] = total if tiles == 1 else total * scale


def rtl_part(rate, scale, k, nets, stats, base, rows=256):
    n, feature = k.shape
    tiles = len(nets)
    block = pl.BlockSpec((rows, feature), lambda i: (i, 0))
    full = pl.BlockSpec((n, feature), lambda i: (0, 0), pipeline_mode=pl.Buffered(1))
    stat = pl.BlockSpec((8, n), lambda i: (0, 0), pipeline_mode=pl.Buffered(1))
    return pl.pallas_call(
        functools.partial(rtl_kernel, rate, scale, tiles),
        grid=(n // rows,),
        out_shape=jax.ShapeDtypeStruct((n, feature), jnp.float32),
        in_specs=[block] + [full] * tiles + [stat] * tiles + [block],
        out_specs=block,
        compiler_params=pltpu.CompilerParams(vmem_limit_bytes=VMEM_LIMIT),
        cost_estimate=pl.CostEstimate(flops=4 * n * tiles * n * feature, bytes_accessed=(tiles + 3) * n * feature * 2, transcendentals=tiles * n * n),
        name="rtl_own" if tiles == 1 else "rtl_others",
    )(k, *nets, *stats, base)


def body(netlist, rtl, hard_target, hard_block):
    queries = netlist[0]
    own_keys = rtl[0]
    feature = queries.shape[1]
    scale = 3.0 / math.sqrt(feature)
    rate = scale * math.log2(math.e)
    groups = lax.axis_size("dp")
    targets = hard_target[0, 0, :, 0]
    picks = hard_block[0, 0]
    columns = [[g for g in range(groups) if (g // 2) % 2 == x] for x in range(2)]
    places = groups // 2

    def spread(packed):
        return lax.all_to_all(packed, "dp", split_axis=0, concat_axis=0, axis_index_groups=columns, tiled=True)

    at = jnp.full((1,), lax.axis_index("dp"), jnp.int32)
    packed, mail = pack_own(at, targets, picks, own_keys, places)
    first = spread(packed)
    mail = lax.ppermute(mail, "dp", [(g, g ^ 2) for g in range(groups)])
    rtl1 = passed_along(own_keys, "loop", 1)
    mail, rtl1, back = lax.optimization_barrier((mail, rtl1, queries))
    second = spread(pack_far(at, mail, places, targets.shape[0]))
    rtl2 = passed_along(rtl1, "loop", 1)
    net1 = passed_along(back, "loop", -1)

    state = cycle_part(rate, scale, queries, [own_keys, rtl1])
    state = hard_part(rate, queries, [state], first, "hard_first")
    net1, state = lax.optimization_barrier((net1, state))
    net2 = passed_along(net1, "loop", -1)
    state = cycle_part(rate, scale, queries, [rtl2], [state])
    others = hard_part(rate, queries, [], second, "hard_second")
    grad, loss, stats = cycle_part(rate, scale, queries, [], [state, others], own_keys)
    stats1 = passed_along(stats, "loop", -1)
    stats2 = passed_along(stats, "loop", -2)
    begun = rtl_part(rate, scale, own_keys, [queries], [stats], queries)
    rtl_grad = rtl_part(rate, scale, own_keys, [net1, net2], [stats1, stats2], begun)
    return (loss, grad[None], rtl_grad[None])


def solution(mesh):
    return jax.shard_map(
        body,
        mesh=mesh,
        in_specs=(
            P("dp", "loop", None),
            P("dp", "loop", None),
            P("dp", "loop", None, None),
            P("dp", "loop", None),
        ),
        out_specs=(P("dp", "loop"), P("dp", "loop", None), P("dp", "loop", None)),
        check_vma=False,
    )
```

```python
import functools
import math

import jax
import jax.numpy as jnp
from jax import lax
from jax.experimental import pallas as pl
from jax.experimental.pallas import tpu as pltpu
from jax.sharding import PartitionSpec as P

BLOCK = 128
CAP = 2
CHUNK = 512
VMEM_LIMIT = 20 * 1024 * 1024
BIG_GRANT = 60 * 1024 * 1024
FAR_GRANT = 64_000_000
HARD_GRANT = 32 * 1024 * 1024
ABSENT = 1024.0
LANES = 128


def passed_along(block, axis, distance):
    devices = range(lax.axis_size(axis))
    route = [((i - distance) % len(devices), i) for i in devices]
    return lax.ppermute(block, axis, route)


def nt_dot(a, b):
    return lax.dot_general(a, b, (((1,), (1,)), ((), ())), preferred_element_type=jnp.float32)


def whole(space=pltpu.VMEM):
    return pl.BlockSpec(memory_space=space)


def shared(slots, entries, out, tile, place, used, seen, mark, sems, mark_sems, column, target_of, pick_of):
    mark[...] = jnp.full(mark.shape, ABSENT, mark.dtype)
    for s in range(slots):
        used[s] = 0
        seen[s] = 0
    for j in range(entries):
        t = target_of(j)
        rank = seen[t]
        seen[t] = rank + 1
        slot = ((t >> 2) * 2 + (t & 1)) * CAP + jnp.minimum(rank, CAP - 1)
        place[j] = jnp.where(((t >> 1) & 1) == column, slot, -1)

        @pl.when(place[j] >= 0)
        def _(j=j):
            used[place[j]] = 1
            pltpu.make_async_copy(tile.at[pl.ds(pl.multiple_of(pick_of(j) * BLOCK, BLOCK), BLOCK)], out.at[place[j]], sems.at[j]).start()

    rows, lanes = mark.shape
    for s in range(slots):
        @pl.when(used[s] == 0)
        def _(s=s):
            pltpu.make_async_copy(mark, out.at[s, pl.ds(0, rows), pl.ds(0, lanes)], mark_sems.at[s]).start()

    def finish():
        for j in range(entries):
            @pl.when(place[j] >= 0)
            def _(j=j):
                pltpu.make_async_copy(tile.at[pl.ds(pl.multiple_of(pick_of(j) * BLOCK, BLOCK), BLOCK)], out.at[place[j]], sems.at[j]).wait()

        for s in range(slots):
            @pl.when(used[s] == 0)
            def _(s=s):
                pltpu.make_async_copy(mark, out.at[s, pl.ds(0, rows), pl.ds(0, lanes)], mark_sems.at[s]).wait()

    return finish


def own_kernel(entries, me, targets, picks, rtl, out, mail, target_s, pick_s, tile, head, place, used, seen, mark, sems, mark_sems, in_sems):
    lists = [pltpu.make_async_copy(targets, target_s, in_sems.at[0]), pltpu.make_async_copy(picks, pick_s, in_sems.at[1])]
    load = pltpu.make_async_copy(rtl, tile, in_sems.at[2])
    for copy in lists + [load]:
        copy.start()
    for copy in lists:
        copy.wait()
    load.wait()
    size = tile.shape[0]
    store = pltpu.make_async_copy(tile, mail.at[pl.ds(0, size)], in_sems.at[3])
    store.start()
    column = (me[0] >> 1) & 1
    finish = shared(out.shape[0], entries, out, tile, place, used, seen, mark, sems, mark_sems, column, lambda j: target_s[j], lambda j: pick_s[j])
    lane = lax.broadcasted_iota(jnp.int32, head.shape, 1)
    line = jnp.zeros(head.shape, jnp.int32)
    for j in range(entries):
        line = jnp.where(lane == j, target_s[j], line)
        line = jnp.where(lane == entries + j, pick_s[j], line)
    head[...] = line.astype(jnp.float32).astype(head.dtype)
    rows, lanes = head.shape
    note = pltpu.make_async_copy(head, mail.at[pl.ds(size, rows), pl.ds(0, lanes)], in_sems.at[4])
    note.start()
    finish()
    store.wait()
    note.wait()


def pack_own(me, targets, picks, tile, places):
    entries = targets.shape[0]
    rows, feature = tile.shape
    slots = places * CAP
    hbm = whole(pltpu.HBM)
    return pl.pallas_call(
        functools.partial(own_kernel, entries),
        out_shape=(jax.ShapeDtypeStruct((slots, BLOCK, feature), tile.dtype), jax.ShapeDtypeStruct((rows + 16, feature), tile.dtype)),
        in_specs=[whole(pltpu.SMEM), hbm, hbm, hbm],
        out_specs=(hbm, hbm),
        scratch_shapes=[
            pltpu.SMEM((entries,), jnp.int32),
            pltpu.SMEM((entries,), jnp.int32),
            pltpu.VMEM(tile.shape, tile.dtype),
            pltpu.VMEM((16, 128), tile.dtype),
            pltpu.SMEM((entries,), jnp.int32),
            pltpu.SMEM((slots,), jnp.int32),
            pltpu.SMEM((slots,), jnp.int32),
            pltpu.VMEM((16, 128), tile.dtype),
            pltpu.SemaphoreType.DMA((entries,)),
            pltpu.SemaphoreType.DMA((slots,)),
            pltpu.SemaphoreType.DMA((5,)),
        ],
        compiler_params=pltpu.CompilerParams(vmem_limit_bytes=BIG_GRANT),
        name="pack_own",
    )(me, targets, picks, tile)


def far_kernel(entries, me, mail, out, list_v, list_s, tile, head, place, used, seen, mark, sems, mark_sems, in_sems):
    size = tile.shape[0]
    rows, lanes = head.shape
    note = pltpu.make_async_copy(mail.at[pl.ds(size, rows), pl.ds(0, lanes)], head, in_sems.at[0])
    load = pltpu.make_async_copy(mail.at[pl.ds(0, size)], tile, in_sems.at[1])
    note.start()
    load.start()
    note.wait()
    list_v[...] = head[...].astype(jnp.float32)[:8].astype(jnp.int32)
    down = pltpu.make_async_copy(list_v, list_s, in_sems.at[2])
    down.start()
    down.wait()
    load.wait()
    column = (me[0] >> 1) & 1
    shared(out.shape[0], entries, out, tile, place, used, seen, mark, sems, mark_sems, column, lambda j: list_s[0, j], lambda j: list_s[0, entries + j])()


def pack_far(me, mail, places, entries):
    rows, feature = mail.shape
    slots = places * CAP
    hbm = whole(pltpu.HBM)
    return pl.pallas_call(
        functools.partial(far_kernel, entries),
        out_shape=jax.ShapeDtypeStruct((slots, BLOCK, feature), mail.dtype),
        in_specs=[whole(pltpu.SMEM), hbm],
        out_specs=hbm,
        scratch_shapes=[
            pltpu.VMEM((8, 128), jnp.int32),
            pltpu.SMEM((8, 128), jnp.int32),
            pltpu.VMEM((rows - 16, feature), mail.dtype),
            pltpu.VMEM((16, 128), mail.dtype),
            pltpu.SMEM((entries,), jnp.int32),
            pltpu.SMEM((slots,), jnp.int32),
            pltpu.SMEM((slots,), jnp.int32),
            pltpu.VMEM((16, 128), mail.dtype),
            pltpu.SemaphoreType.DMA((entries,)),
            pltpu.SemaphoreType.DMA((slots,)),
            pltpu.SemaphoreType.DMA((3,)),
        ],
        compiler_params=pltpu.CompilerParams(vmem_limit_bytes=FAR_GRANT),
        name="pack_far",
    )(me, mail)


def cycle_kernel(rate, scale, tiles, given, end, q_ref, *refs):
    q = q_ref[...]
    rows, feature = q.shape
    first = pl.multiple_of(pl.program_id(0) * rows, rows)
    keys = [ref[...] for ref in refs[:tiles]]
    scores = [nt_dot(q, k) for k in keys]
    states = refs[tiles : tiles + given]
    peaks = [jnp.max(s, axis=1, keepdims=True) for s in scores] + [state[:, feature : feature + 1] for state in states]
    m = functools.reduce(jnp.maximum, peaks)
    l = jnp.zeros((rows, 1), jnp.float32)
    num = jnp.zeros((rows, feature), jnp.float32)
    for s, k in zip(scores, keys):
        e = jnp.exp2((s - m) * rate)
        l += jnp.sum(e, axis=1, keepdims=True)
        num += jnp.dot(e.astype(jnp.bfloat16), k, preferred_element_type=jnp.float32)
    for state in states:
        shrink = jnp.exp2((state[:, feature : feature + 1] - m) * rate)
        l += state[:, feature + 1 : feature + 2] * shrink
        num += state[:, :feature] * shrink
    lane = lax.broadcasted_iota(jnp.int32, (rows, LANES), 1)
    if not end:
        state_ref = refs[-1]
        if given:
            positive = states[0][:, feature + 2 : feature + 3]
        else:
            own = refs[0][pl.ds(first, rows), :].astype(jnp.float32)
            positive = jnp.sum(q.astype(jnp.float32) * own, axis=1, keepdims=True)
        state_ref[:, :feature] = num
        state_ref[:, feature:] = jnp.where(lane == 0, m, jnp.where(lane == 1, l, positive))
        return
    positive = states[0][:, feature + 2 : feature + 3]
    own_ref, grad_ref, loss_ref, stats_ref = refs[tiles + given :]
    inverse = 1.0 / l
    grad_ref[...] = (num * inverse - own_ref[...].astype(jnp.float32)) * scale
    loss = (m - positive) * scale + jnp.log(l)
    table = jnp.where(lane == 0, m, jnp.where(lane == 1, inverse, loss))
    flipped = table.T
    stats_ref[...] = flipped[:8]
    loss_ref[...] = flipped[2:3]


def cycle_part(rate, scale, q, keys, states=(), own=None, rows=256):
    n, feature = q.shape
    f32 = jnp.float32
    tiles = len(keys)
    block = pl.BlockSpec((rows, feature), lambda i: (i, 0))
    wide = pl.BlockSpec((rows, feature + LANES), lambda i: (i, 0))
    full = pl.BlockSpec((n, feature), lambda i: (0, 0), pipeline_mode=pl.Buffered(1))
    end = own is not None
    args, specs = [q, *keys, *states], [block] + [full] * tiles + [wide] * len(states)
    shapes, outs = jax.ShapeDtypeStruct((n, feature + LANES), f32), wide
    if end:
        args, specs = args + [own], specs + [block]
        shapes = (jax.ShapeDtypeStruct((n, feature), f32), jax.ShapeDtypeStruct((1, n), f32), jax.ShapeDtypeStruct((8, n), f32))
        outs = (block, pl.BlockSpec((1, rows), lambda i: (0, i)), pl.BlockSpec((8, rows), lambda i: (0, i)))
    return pl.pallas_call(
        functools.partial(cycle_kernel, rate, scale, tiles, len(states), end),
        grid=(n // rows,),
        out_shape=shapes,
        in_specs=specs,
        out_specs=outs,
        compiler_params=pltpu.CompilerParams(vmem_limit_bytes=VMEM_LIMIT),
        cost_estimate=pl.CostEstimate(flops=4 * n * tiles * n * feature, bytes_accessed=8 * n * feature, transcendentals=tiles * n * n),
        name="cycle_last" if end else "cycle_more" if states else "cycle_own",
    )(*args)


def hard_kernel(rate, fresh, q_hbm, *refs):
    state_in = None if fresh else refs[0]
    blocks, state, q_ref, keys, scores, order, sems = refs[-7:]
    n, feature = q_ref.shape
    slots = blocks.shape[0]
    per = CHUNK // BLOCK
    load_keys = pltpu.make_async_copy(blocks, keys, sems.at[0])
    load_q = pltpu.make_async_copy(q_hbm, q_ref, sems.at[1])
    load_keys.start()
    load_q.start()
    if not fresh:
        load_state = pltpu.make_async_copy(state_in, state, sems.at[2])
        load_state.start()
    load_keys.wait()
    there = [(jnp.max(keys[s, :16, :128].astype(jnp.float32)) < ABSENT / 2).astype(jnp.int32) for s in range(slots)]
    live = jnp.int32(0)
    for s in range(slots):
        order[live] = s
        live += there[s]
    chunks = (live + per - 1) // per
    tail = order[jnp.maximum(live - 1, 0)]
    for p in range(per - 1):
        order[live + p] = tail

    def chunk_keys(i):
        return jnp.concatenate([keys[order[i * per + p]] for p in range(per)], axis=0)

    load_q.wait()
    q = q_ref[...]

    def score(i, m):
        s = nt_dot(q, chunk_keys(i))
        scores[i] = s
        for c in range(per):
            m = jnp.maximum(m, s[:, c * BLOCK : (c + 1) * BLOCK])
        return m

    wide = lax.fori_loop(0, chunks, score, jnp.full((n, BLOCK), -jnp.inf, jnp.float32))
    m = jnp.max(wide, axis=1, keepdims=True)
    if fresh:
        state[...] = jnp.zeros(state.shape, jnp.float32)
        kept = 0.0
    else:
        load_state.wait()
        old = state[:, feature : feature + 1]
        m = jnp.maximum(m, old)
        shrink = jnp.exp2((old - m) * rate)
        kept = state[:, feature + 1 : feature + 2] * shrink
        state[:, :feature] = state[:, :feature] * shrink
    for p in range(1, per):
        @pl.when(((chunks - 1) * per + p >= live) & (chunks > 0))
        def _(p=p):
            scores[chunks - 1, :, p * BLOCK : (p + 1) * BLOCK] = jnp.full((n, BLOCK), -jnp.inf, jnp.float32)

    def weigh(i, l):
        e = jnp.exp2((scores[i] - m) * rate)
        state[:, :feature] += jnp.dot(e.astype(jnp.bfloat16), chunk_keys(i), preferred_element_type=jnp.float32)
        for c in range(per):
            l = l + e[:, c * BLOCK : (c + 1) * BLOCK]
        return l

    l = lax.fori_loop(0, chunks, weigh, jnp.zeros((n, BLOCK), jnp.float32))
    total = jnp.sum(l, axis=1, keepdims=True) + kept
    lane = lax.broadcasted_iota(jnp.int32, (n, LANES), 1)
    state[:, feature:] = jnp.where(lane == 0, m, jnp.where(lane == 1, total, state[:, feature:]))


def hard_part(rate, q, states, blocks, name):
    n, feature = q.shape
    slots = blocks.shape[0]
    f32 = jnp.float32
    keys = slots * BLOCK
    return pl.pallas_call(
        functools.partial(hard_kernel, rate, not states),
        out_shape=jax.ShapeDtypeStruct((n, feature + LANES), f32),
        in_specs=[whole(pl.ANY)] * (2 + len(states)),
        out_specs=whole(),
        scratch_shapes=[
            pltpu.VMEM(q.shape, q.dtype),
            pltpu.VMEM(blocks.shape, blocks.dtype),
            pltpu.VMEM((keys // CHUNK, n, CHUNK), f32),
            pltpu.SMEM((slots + CHUNK // BLOCK,), jnp.int32),
            pltpu.SemaphoreType.DMA((3,)),
        ],
        compiler_params=pltpu.CompilerParams(vmem_limit_bytes=HARD_GRANT),
        cost_estimate=pl.CostEstimate(flops=2 * n * keys * feature, bytes_accessed=2 * keys * feature, transcendentals=n * keys // 2),
        name=name,
    )(q, *states, blocks)


def final_kernel(rate, scale, q_hbm, own_hbm, state_ref, blocks, grad, loss_ref, stats_ref, q_ref, own_ref, num, keys, scores, order, sems, out_sems):
    n, feature = q_ref.shape
    slots = blocks.shape[0]
    per = CHUNK // BLOCK
    load_keys = pltpu.make_async_copy(blocks, keys, sems.at[0])
    load_q = pltpu.make_async_copy(q_hbm, q_ref, sems.at[1])
    load_own = pltpu.make_async_copy(own_hbm, own_ref, sems.at[2])
    load_keys.start()
    load_q.start()
    load_own.start()
    old = state_ref[:, feature : feature + 1]
    load_keys.wait()
    there = [(jnp.max(keys[s, :16, :128].astype(jnp.float32)) < ABSENT / 2).astype(jnp.int32) for s in range(slots)]
    live = jnp.int32(0)
    for s in range(slots):
        order[live] = s
        live += there[s]
    chunks = (live + per - 1) // per
    tail = order[jnp.maximum(live - 1, 0)]
    for p in range(per - 1):
        order[live + p] = tail

    def chunk_keys(i):
        return jnp.concatenate([keys[order[i * per + p]] for p in range(per)], axis=0)

    load_q.wait()
    q = q_ref[...]

    def score(i, m):
        s = nt_dot(q, chunk_keys(i))
        scores[i] = s
        for c in range(per):
            m = jnp.maximum(m, s[:, c * BLOCK : (c + 1) * BLOCK])
        return m

    wide = lax.fori_loop(0, chunks, score, jnp.full((n, BLOCK), -jnp.inf, jnp.float32))
    m = jnp.maximum(jnp.max(wide, axis=1, keepdims=True), old)
    shrink = jnp.exp2((old - m) * rate)
    kept = state_ref[:, feature + 1 : feature + 2] * shrink
    num[...] = state_ref[:, :feature] * shrink
    for p in range(1, per):
        @pl.when(((chunks - 1) * per + p >= live) & (chunks > 0))
        def _(p=p):
            scores[chunks - 1, :, p * BLOCK : (p + 1) * BLOCK] = jnp.full((n, BLOCK), -jnp.inf, jnp.float32)

    def weigh(i, l):
        e = jnp.exp2((scores[i] - m) * rate)
        num[...] += jnp.dot(e.astype(jnp.bfloat16), chunk_keys(i), preferred_element_type=jnp.float32)
        for c in range(per):
            l = l + e[:, c * BLOCK : (c + 1) * BLOCK]
        return l

    l = lax.fori_loop(0, chunks, weigh, jnp.zeros((n, BLOCK), jnp.float32))
    total = jnp.sum(l, axis=1, keepdims=True) + kept
    inverse = 1.0 / total
    load_own.wait()
    pieces = out_sems.shape[0]
    piece = n // pieces
    saves = []
    for r in range(pieces):
        part = pl.ds(r * piece, piece)
        gain = inverse[r * piece : (r + 1) * piece]
        num[part, :] = (num[part, :] * gain - own_ref[part, :].astype(jnp.float32)) * scale
        saves.append(pltpu.make_async_copy(num.at[part], grad.at[part], out_sems.at[r]))
        saves[-1].start()
    positive = state_ref[:, feature + 2 : feature + 3]
    loss = (m - positive) * scale + jnp.log(total)
    lane = lax.broadcasted_iota(jnp.int32, (n, LANES), 1)
    table = jnp.where(lane == 0, m, jnp.where(lane == 1, inverse, loss))
    flipped = table.T
    stats_ref[...] = flipped[:8]
    loss_ref[...] = flipped[2:3]
    for save in saves:
        save.wait()


def final_part(rate, scale, q, own, state, blocks):
    n, feature = q.shape
    slots = blocks.shape[0]
    f32 = jnp.float32
    keys = slots * BLOCK
    return pl.pallas_call(
        functools.partial(final_kernel, rate, scale),
        out_shape=(jax.ShapeDtypeStruct((n, feature), f32), jax.ShapeDtypeStruct((1, n), f32), jax.ShapeDtypeStruct((8, n), f32)),
        in_specs=[whole(pl.ANY), whole(pl.ANY), whole(), whole(pl.ANY)],
        out_specs=(whole(pl.ANY), whole(), whole()),
        scratch_shapes=[
            pltpu.VMEM(q.shape, q.dtype),
            pltpu.VMEM(own.shape, own.dtype),
            pltpu.VMEM((n, feature), f32),
            pltpu.VMEM(blocks.shape, blocks.dtype),
            pltpu.VMEM((keys // CHUNK, n, CHUNK), f32),
            pltpu.SMEM((slots + CHUNK // BLOCK,), jnp.int32),
            pltpu.SemaphoreType.DMA((3,)),
            pltpu.SemaphoreType.DMA((4,)),
        ],
        compiler_params=pltpu.CompilerParams(vmem_limit_bytes=HARD_GRANT),
        cost_estimate=pl.CostEstimate(flops=2 * n * keys * feature, bytes_accessed=2 * keys * feature, transcendentals=n * keys // 2),
        name="hard_last",
    )(q, own, state, blocks)


def rtl_kernel(rate, scale, tiles, k_ref, *refs):
    n_refs, s_refs = refs[:tiles], refs[tiles : 2 * tiles]
    base_ref, out_ref = refs[2 * tiles :]
    k = k_ref[...]
    total = -base_ref[...].astype(jnp.float32) if tiles == 1 else base_ref[...]
    for n_ref, s_ref in zip(n_refs, s_refs):
        rows = n_ref[...]
        s = nt_dot(k, rows)
        w = jnp.exp2((s - s_ref[0:1, :]) * rate) * s_ref[1:2, :]
        total += jnp.dot(w.astype(jnp.bfloat16), rows, preferred_element_type=jnp.float32)
    out_ref[...] = total if tiles == 1 else total * scale


def rtl_part(rate, scale, k, nets, stats, base, rows=256):
    n, feature = k.shape
    tiles = len(nets)
    block = pl.BlockSpec((rows, feature), lambda i: (i, 0))
    full = pl.BlockSpec((n, feature), lambda i: (0, 0), pipeline_mode=pl.Buffered(1))
    stat = pl.BlockSpec((8, n), lambda i: (0, 0), pipeline_mode=pl.Buffered(1))
    return pl.pallas_call(
        functools.partial(rtl_kernel, rate, scale, tiles),
        grid=(n // rows,),
        out_shape=jax.ShapeDtypeStruct((n, feature), jnp.float32),
        in_specs=[block] + [full] * tiles + [stat] * tiles + [block],
        out_specs=block,
        compiler_params=pltpu.CompilerParams(vmem_limit_bytes=VMEM_LIMIT),
        cost_estimate=pl.CostEstimate(flops=4 * n * tiles * n * feature, bytes_accessed=(tiles + 3) * n * feature * 2, transcendentals=tiles * n * n),
        name="rtl_own" if tiles == 1 else "rtl_others",
    )(k, *nets, *stats, base)


def body(netlist, rtl, hard_target, hard_block):
    queries = netlist[0]
    own_keys = rtl[0]
    feature = queries.shape[1]
    scale = 3.0 / math.sqrt(feature)
    rate = scale * math.log2(math.e)
    groups = lax.axis_size("dp")
    targets = hard_target[0, 0, :, 0]
    picks = hard_block[0, 0]
    columns = [[g for g in range(groups) if (g // 2) % 2 == x] for x in range(2)]
    places = groups // 2

    def spread(packed):
        return lax.all_to_all(packed, "dp", split_axis=0, concat_axis=0, axis_index_groups=columns, tiled=True)

    at = jnp.full((1,), lax.axis_index("dp"), jnp.int32)
    packed, mail = pack_own(at, targets, picks, own_keys, places)
    first = spread(packed)
    mail = lax.ppermute(mail, "dp", [(g, g ^ 2) for g in range(groups)])
    rtl1 = passed_along(own_keys, "loop", 1)
    mail, rtl1, back = lax.optimization_barrier((mail, rtl1, queries))
    second = spread(pack_far(at, mail, places, targets.shape[0]))
    rtl2 = passed_along(rtl1, "loop", 1)
    net1 = passed_along(back, "loop", -1)

    state = cycle_part(rate, scale, queries, [own_keys, rtl1])
    state = hard_part(rate, queries, [state], first, "hard_first")
    net1, state = lax.optimization_barrier((net1, state))
    net2 = passed_along(net1, "loop", -1)
    state = cycle_part(rate, scale, queries, [rtl2], [state])
    grad, loss, stats = final_part(rate, scale, queries, own_keys, state, second)
    stats1 = passed_along(stats, "loop", -1)
    stats2 = passed_along(stats, "loop", -2)
    begun = rtl_part(rate, scale, own_keys, [queries], [stats], queries)
    rtl_grad = rtl_part(rate, scale, own_keys, [net1, net2], [stats1, stats2], begun)
    return (loss, grad[None], rtl_grad[None])


def solution(mesh):
    return jax.shard_map(
        body,
        mesh=mesh,
        in_specs=(
            P("dp", "loop", None),
            P("dp", "loop", None),
            P("dp", "loop", None, None),
            P("dp", "loop", None),
        ),
        out_specs=(P("dp", "loop"), P("dp", "loop", None), P("dp", "loop", None)),
        check_vma=False,
    )
```

```python
import functools
import math

import jax
import jax.numpy as jnp
from jax import lax
from jax.experimental import pallas as pl
from jax.experimental.pallas import tpu as pltpu
from jax.sharding import PartitionSpec as P

BLOCK = 128
CAP = 2
CHUNK = 512
VMEM_LIMIT = 20 * 1024 * 1024
BIG_GRANT = 60 * 1024 * 1024
FAR_GRANT = 64_000_000
HARD_GRANT = 32 * 1024 * 1024
ABSENT = 1024.0
LANES = 128


def passed_along(block, axis, distance):
    devices = range(lax.axis_size(axis))
    route = [((i - distance) % len(devices), i) for i in devices]
    return lax.ppermute(block, axis, route)


def nt_dot(a, b):
    return lax.dot_general(a, b, (((1,), (1,)), ((), ())), preferred_element_type=jnp.float32)


def whole(space=pltpu.VMEM):
    return pl.BlockSpec(memory_space=space)


def shared(slots, entries, out, tile, place, used, seen, mark, sems, mark_sems, column, target_of, pick_of):
    mark[...] = jnp.full(mark.shape, ABSENT, mark.dtype)
    for s in range(slots):
        used[s] = 0
        seen[s] = 0
    for j in range(entries):
        t = target_of(j)
        rank = seen[t]
        seen[t] = rank + 1
        slot = ((t >> 2) * 2 + (t & 1)) * CAP + jnp.minimum(rank, CAP - 1)
        place[j] = jnp.where(((t >> 1) & 1) == column, slot, -1)

        @pl.when(place[j] >= 0)
        def _(j=j):
            used[place[j]] = 1
            pltpu.make_async_copy(tile.at[pl.ds(pl.multiple_of(pick_of(j) * BLOCK, BLOCK), BLOCK)], out.at[place[j]], sems.at[j]).start()

    rows, lanes = mark.shape
    for s in range(slots):
        @pl.when(used[s] == 0)
        def _(s=s):
            pltpu.make_async_copy(mark, out.at[s, pl.ds(0, rows), pl.ds(0, lanes)], mark_sems.at[s]).start()

    def finish():
        for j in range(entries):
            @pl.when(place[j] >= 0)
            def _(j=j):
                pltpu.make_async_copy(tile.at[pl.ds(pl.multiple_of(pick_of(j) * BLOCK, BLOCK), BLOCK)], out.at[place[j]], sems.at[j]).wait()

        for s in range(slots):
            @pl.when(used[s] == 0)
            def _(s=s):
                pltpu.make_async_copy(mark, out.at[s, pl.ds(0, rows), pl.ds(0, lanes)], mark_sems.at[s]).wait()

    return finish


def own_kernel(entries, me, targets, picks, rtl, out, mail, target_s, pick_s, tile, head, place, used, seen, mark, sems, mark_sems, in_sems):
    lists = [pltpu.make_async_copy(targets, target_s, in_sems.at[0]), pltpu.make_async_copy(picks, pick_s, in_sems.at[1])]
    load = pltpu.make_async_copy(rtl, tile, in_sems.at[2])
    for copy in lists + [load]:
        copy.start()
    for copy in lists:
        copy.wait()
    load.wait()
    size = tile.shape[0]
    store = pltpu.make_async_copy(tile, mail.at[pl.ds(0, size)], in_sems.at[3])
    store.start()
    column = (me[0] >> 1) & 1
    finish = shared(out.shape[0], entries, out, tile, place, used, seen, mark, sems, mark_sems, column, lambda j: target_s[j], lambda j: pick_s[j])
    lane = lax.broadcasted_iota(jnp.int32, head.shape, 1)
    line = jnp.zeros(head.shape, jnp.int32)
    for j in range(entries):
        line = jnp.where(lane == j, target_s[j], line)
        line = jnp.where(lane == entries + j, pick_s[j], line)
    head[...] = line.astype(jnp.float32).astype(head.dtype)
    rows, lanes = head.shape
    note = pltpu.make_async_copy(head, mail.at[pl.ds(size, rows), pl.ds(0, lanes)], in_sems.at[4])
    note.start()
    finish()
    store.wait()
    note.wait()


def pack_own(me, targets, picks, tile, places):
    entries = targets.shape[0]
    rows, feature = tile.shape
    slots = places * CAP
    hbm = whole(pltpu.HBM)
    return pl.pallas_call(
        functools.partial(own_kernel, entries),
        out_shape=(jax.ShapeDtypeStruct((slots, BLOCK, feature), tile.dtype), jax.ShapeDtypeStruct((rows + 16, feature), tile.dtype)),
        in_specs=[whole(pltpu.SMEM), hbm, hbm, hbm],
        out_specs=(hbm, hbm),
        scratch_shapes=[
            pltpu.SMEM((entries,), jnp.int32),
            pltpu.SMEM((entries,), jnp.int32),
            pltpu.VMEM(tile.shape, tile.dtype),
            pltpu.VMEM((16, 128), tile.dtype),
            pltpu.SMEM((entries,), jnp.int32),
            pltpu.SMEM((slots,), jnp.int32),
            pltpu.SMEM((slots,), jnp.int32),
            pltpu.VMEM((16, 128), tile.dtype),
            pltpu.SemaphoreType.DMA((entries,)),
            pltpu.SemaphoreType.DMA((slots,)),
            pltpu.SemaphoreType.DMA((5,)),
        ],
        compiler_params=pltpu.CompilerParams(vmem_limit_bytes=BIG_GRANT),
        name="pack_own",
    )(me, targets, picks, tile)


def far_kernel(entries, me, mail, out, list_v, list_s, tile, head, place, used, seen, mark, sems, mark_sems, in_sems):
    size = tile.shape[0]
    rows, lanes = head.shape
    note = pltpu.make_async_copy(mail.at[pl.ds(size, rows), pl.ds(0, lanes)], head, in_sems.at[0])
    load = pltpu.make_async_copy(mail.at[pl.ds(0, size)], tile, in_sems.at[1])
    note.start()
    load.start()
    note.wait()
    list_v[...] = head[...].astype(jnp.float32)[:8].astype(jnp.int32)
    down = pltpu.make_async_copy(list_v, list_s, in_sems.at[2])
    down.start()
    down.wait()
    load.wait()
    column = (me[0] >> 1) & 1
    shared(out.shape[0], entries, out, tile, place, used, seen, mark, sems, mark_sems, column, lambda j: list_s[0, j], lambda j: list_s[0, entries + j])()


def pack_far(me, mail, places, entries):
    rows, feature = mail.shape
    slots = places * CAP
    hbm = whole(pltpu.HBM)
    return pl.pallas_call(
        functools.partial(far_kernel, entries),
        out_shape=jax.ShapeDtypeStruct((slots, BLOCK, feature), mail.dtype),
        in_specs=[whole(pltpu.SMEM), hbm],
        out_specs=hbm,
        scratch_shapes=[
            pltpu.VMEM((8, 128), jnp.int32),
            pltpu.SMEM((8, 128), jnp.int32),
            pltpu.VMEM((rows - 16, feature), mail.dtype),
            pltpu.VMEM((16, 128), mail.dtype),
            pltpu.SMEM((entries,), jnp.int32),
            pltpu.SMEM((slots,), jnp.int32),
            pltpu.SMEM((slots,), jnp.int32),
            pltpu.VMEM((16, 128), mail.dtype),
            pltpu.SemaphoreType.DMA((entries,)),
            pltpu.SemaphoreType.DMA((slots,)),
            pltpu.SemaphoreType.DMA((3,)),
        ],
        compiler_params=pltpu.CompilerParams(vmem_limit_bytes=FAR_GRANT),
        name="pack_far",
    )(me, mail)


def cycle_kernel(rate, scale, tiles, given, end, q_ref, *refs):
    q = q_ref[...]
    rows, feature = q.shape
    first = pl.multiple_of(pl.program_id(0) * rows, rows)
    keys = [ref[...] for ref in refs[:tiles]]
    scores = [nt_dot(q, k) for k in keys]
    states = refs[tiles : tiles + given]
    peaks = [jnp.max(s, axis=1, keepdims=True) for s in scores] + [state[:, feature : feature + 1] for state in states]
    m = functools.reduce(jnp.maximum, peaks)
    l = jnp.zeros((rows, 1), jnp.float32)
    num = jnp.zeros((rows, feature), jnp.float32)
    for s, k in zip(scores, keys):
        e = jnp.exp2((s - m) * rate)
        l += jnp.sum(e, axis=1, keepdims=True)
        num += jnp.dot(e.astype(jnp.bfloat16), k, preferred_element_type=jnp.float32)
    for state in states:
        shrink = jnp.exp2((state[:, feature : feature + 1] - m) * rate)
        l += state[:, feature + 1 : feature + 2] * shrink
        num += state[:, :feature] * shrink
    lane = lax.broadcasted_iota(jnp.int32, (rows, LANES), 1)
    if not end:
        state_ref = refs[-1]
        if given:
            positive = states[0][:, feature + 2 : feature + 3]
        else:
            own = refs[0][pl.ds(first, rows), :].astype(jnp.float32)
            positive = jnp.sum(q.astype(jnp.float32) * own, axis=1, keepdims=True)
        state_ref[:, :feature] = num
        state_ref[:, feature:] = jnp.where(lane == 0, m, jnp.where(lane == 1, l, positive))
        return
    positive = states[0][:, feature + 2 : feature + 3]
    own_ref, grad_ref, loss_ref, stats_ref = refs[tiles + given :]
    inverse = 1.0 / l
    grad_ref[...] = (num * inverse - own_ref[...].astype(jnp.float32)) * scale
    loss = (m - positive) * scale + jnp.log(l)
    table = jnp.where(lane == 0, m, jnp.where(lane == 1, inverse, loss))
    flipped = table.T
    stats_ref[...] = flipped[:8]
    loss_ref[...] = flipped[2:3]


def cycle_part(rate, scale, q, keys, states=(), own=None, rows=256):
    n, feature = q.shape
    f32 = jnp.float32
    tiles = len(keys)
    block = pl.BlockSpec((rows, feature), lambda i: (i, 0))
    wide = pl.BlockSpec((rows, feature + LANES), lambda i: (i, 0))
    full = pl.BlockSpec((n, feature), lambda i: (0, 0), pipeline_mode=pl.Buffered(1))
    end = own is not None
    args, specs = [q, *keys, *states], [block] + [full] * tiles + [wide] * len(states)
    shapes, outs = jax.ShapeDtypeStruct((n, feature + LANES), f32), wide
    if end:
        args, specs = args + [own], specs + [block]
        shapes = (jax.ShapeDtypeStruct((n, feature), f32), jax.ShapeDtypeStruct((1, n), f32), jax.ShapeDtypeStruct((8, n), f32))
        outs = (block, pl.BlockSpec((1, rows), lambda i: (0, i)), pl.BlockSpec((8, rows), lambda i: (0, i)))
    return pl.pallas_call(
        functools.partial(cycle_kernel, rate, scale, tiles, len(states), end),
        grid=(n // rows,),
        out_shape=shapes,
        in_specs=specs,
        out_specs=outs,
        compiler_params=pltpu.CompilerParams(vmem_limit_bytes=VMEM_LIMIT),
        cost_estimate=pl.CostEstimate(flops=4 * n * tiles * n * feature, bytes_accessed=8 * n * feature, transcendentals=tiles * n * n),
        name="cycle_last" if end else "cycle_more" if states else "cycle_own",
    )(*args)


def hard_kernel(rate, fresh, q_hbm, *refs):
    state_in = None if fresh else refs[0]
    blocks, state, q_ref, keys, scores, order, sems = refs[-7:]
    n, feature = q_ref.shape
    slots = blocks.shape[0]
    per = CHUNK // BLOCK
    load_keys = pltpu.make_async_copy(blocks, keys, sems.at[0])
    load_q = pltpu.make_async_copy(q_hbm, q_ref, sems.at[1])
    load_keys.start()
    load_q.start()
    if not fresh:
        load_state = pltpu.make_async_copy(state_in, state, sems.at[2])
        load_state.start()
    load_keys.wait()
    there = [(jnp.max(keys[s, :16, :128].astype(jnp.float32)) < ABSENT / 2).astype(jnp.int32) for s in range(slots)]
    live = jnp.int32(0)
    for s in range(slots):
        order[live] = s
        live += there[s]
    chunks = (live + per - 1) // per
    tail = order[jnp.maximum(live - 1, 0)]
    for p in range(per - 1):
        order[live + p] = tail

    def chunk_keys(i):
        return jnp.concatenate([keys[order[i * per + p]] for p in range(per)], axis=0)

    load_q.wait()
    q = q_ref[...]

    def score(i, m):
        s = nt_dot(q, chunk_keys(i))
        scores[i] = s
        for c in range(per):
            m = jnp.maximum(m, s[:, c * BLOCK : (c + 1) * BLOCK])
        return m

    wide = lax.fori_loop(0, chunks, score, jnp.full((n, BLOCK), -jnp.inf, jnp.float32))
    m = jnp.max(wide, axis=1, keepdims=True)
    if fresh:
        state[...] = jnp.zeros(state.shape, jnp.float32)
        kept = 0.0
    else:
        load_state.wait()
        old = state[:, feature : feature + 1]
        m = jnp.maximum(m, old)
        shrink = jnp.exp2((old - m) * rate)
        kept = state[:, feature + 1 : feature + 2] * shrink
        state[:, :feature] = state[:, :feature] * shrink
    for p in range(1, per):
        @pl.when(((chunks - 1) * per + p >= live) & (chunks > 0))
        def _(p=p):
            scores[chunks - 1, :, p * BLOCK : (p + 1) * BLOCK] = jnp.full((n, BLOCK), -jnp.inf, jnp.float32)

    def weigh(i, l):
        e = jnp.exp2((scores[i] - m) * rate)
        state[:, :feature] += jnp.dot(e.astype(jnp.bfloat16), chunk_keys(i), preferred_element_type=jnp.float32)
        for c in range(per):
            l = l + e[:, c * BLOCK : (c + 1) * BLOCK]
        return l

    l = lax.fori_loop(0, chunks, weigh, jnp.zeros((n, BLOCK), jnp.float32))
    total = jnp.sum(l, axis=1, keepdims=True) + kept
    lane = lax.broadcasted_iota(jnp.int32, (n, LANES), 1)
    state[:, feature:] = jnp.where(lane == 0, m, jnp.where(lane == 1, total, state[:, feature:]))


def hard_part(rate, q, states, blocks, name):
    n, feature = q.shape
    slots = blocks.shape[0]
    f32 = jnp.float32
    keys = slots * BLOCK
    return pl.pallas_call(
        functools.partial(hard_kernel, rate, not states),
        out_shape=jax.ShapeDtypeStruct((n, feature + LANES), f32),
        in_specs=[whole(pl.ANY)] * (2 + len(states)),
        out_specs=whole(),
        scratch_shapes=[
            pltpu.VMEM(q.shape, q.dtype),
            pltpu.VMEM(blocks.shape, blocks.dtype),
            pltpu.VMEM((keys // CHUNK, n, CHUNK), f32),
            pltpu.SMEM((slots + CHUNK // BLOCK,), jnp.int32),
            pltpu.SemaphoreType.DMA((3,)),
        ],
        compiler_params=pltpu.CompilerParams(vmem_limit_bytes=HARD_GRANT),
        cost_estimate=pl.CostEstimate(flops=2 * n * keys * feature, bytes_accessed=2 * keys * feature, transcendentals=n * keys // 2),
        name=name,
    )(q, *states, blocks)


def rtl_kernel(rate, scale, tiles, k_ref, *refs):
    n_refs, s_refs = refs[:tiles], refs[tiles : 2 * tiles]
    base_ref, out_ref = refs[2 * tiles :]
    k = k_ref[...]
    total = -base_ref[...].astype(jnp.float32) if tiles == 1 else base_ref[...]
    for n_ref, s_ref in zip(n_refs, s_refs):
        rows = n_ref[...]
        s = nt_dot(k, rows)
        w = jnp.exp2((s - s_ref[0:1, :]) * rate) * s_ref[1:2, :]
        total += jnp.dot(w.astype(jnp.bfloat16), rows, preferred_element_type=jnp.float32)
    out_ref[...] = total if tiles == 1 else total * scale


def rtl_part(rate, scale, k, nets, stats, base, rows=256):
    n, feature = k.shape
    tiles = len(nets)
    block = pl.BlockSpec((rows, feature), lambda i: (i, 0))
    full = pl.BlockSpec((n, feature), lambda i: (0, 0), pipeline_mode=pl.Buffered(1))
    stat = pl.BlockSpec((8, n), lambda i: (0, 0), pipeline_mode=pl.Buffered(1))
    return pl.pallas_call(
        functools.partial(rtl_kernel, rate, scale, tiles),
        grid=(n // rows,),
        out_shape=jax.ShapeDtypeStruct((n, feature), jnp.float32),
        in_specs=[block] + [full] * tiles + [stat] * tiles + [block],
        out_specs=block,
        compiler_params=pltpu.CompilerParams(vmem_limit_bytes=VMEM_LIMIT),
        cost_estimate=pl.CostEstimate(flops=4 * n * tiles * n * feature, bytes_accessed=(tiles + 3) * n * feature * 2, transcendentals=tiles * n * n),
        name="rtl_own" if tiles == 1 else "rtl_others",
    )(k, *nets, *stats, base)


def body(netlist, rtl, hard_target, hard_block):
    queries = netlist[0]
    own_keys = rtl[0]
    feature = queries.shape[1]
    scale = 3.0 / math.sqrt(feature)
    rate = scale * math.log2(math.e)
    groups = lax.axis_size("dp")
    targets = hard_target[0, 0, :, 0]
    picks = hard_block[0, 0]
    columns = [[g for g in range(groups) if (g // 2) % 2 == x] for x in range(2)]
    places = groups // 2

    def spread(packed):
        return lax.all_to_all(packed, "dp", split_axis=0, concat_axis=0, axis_index_groups=columns, tiled=True)

    at = jnp.full((1,), lax.axis_index("dp"), jnp.int32)
    packed, mail = pack_own(at, targets, picks, own_keys, places)
    first = spread(packed)
    mail = lax.ppermute(mail, "dp", [(g, g ^ 2) for g in range(groups)])
    rtl1 = passed_along(own_keys, "loop", 1)
    mail, rtl1, back = lax.optimization_barrier((mail, rtl1, queries))
    second = spread(pack_far(at, mail, places, targets.shape[0]))
    rtl2 = passed_along(rtl1, "loop", 1)
    net1 = passed_along(back, "loop", -1)

    state = cycle_part(rate, scale, queries, [own_keys, rtl1])
    state = hard_part(rate, queries, [state], first, "hard_first")
    net1, state = lax.optimization_barrier((net1, state))
    net2 = passed_along(net1, "loop", -1)
    state = cycle_part(rate, scale, queries, [rtl2], [state])
    others = hard_part(rate, queries, [], second, "hard_second")
    grad, loss, stats = cycle_part(rate, scale, queries, [], [state, others], own_keys)
    stats1 = passed_along(stats, "loop", -1)
    stats2 = passed_along(stats, "loop", -2)
    begun = rtl_part(rate, scale, own_keys, [queries], [stats], queries)
    net1, begun = lax.optimization_barrier((net1, begun))
    net1 = jnp.where(at < 0, queries, net1)
    rtl_grad = rtl_part(rate, scale, own_keys, [net1, net2], [stats1, stats2], begun)
    return (loss, grad[None], rtl_grad[None])


def solution(mesh):
    return jax.shard_map(
        body,
        mesh=mesh,
        in_specs=(
            P("dp", "loop", None),
            P("dp", "loop", None),
            P("dp", "loop", None, None),
            P("dp", "loop", None),
        ),
        out_specs=(P("dp", "loop"), P("dp", "loop", None), P("dp", "loop", None)),
        check_vma=False,
    )
```

```python
import functools
import math

import jax
import jax.numpy as jnp
from jax import lax
from jax.experimental import pallas as pl
from jax.experimental.pallas import tpu as pltpu
from jax.sharding import PartitionSpec as P

BLOCK = 128
CAP = 2
CHUNK = 512
VMEM_LIMIT = 20 * 1024 * 1024
BIG_GRANT = 60 * 1024 * 1024
FAR_GRANT = 40_000_000
HARD_GRANT = 32 * 1024 * 1024
ABSENT = 1024.0
LANES = 128


def passed_along(block, axis, distance):
    devices = range(lax.axis_size(axis))
    route = [((i - distance) % len(devices), i) for i in devices]
    return lax.ppermute(block, axis, route)


def nt_dot(a, b):
    return lax.dot_general(a, b, (((1,), (1,)), ((), ())), preferred_element_type=jnp.float32)


def whole(space=pltpu.VMEM):
    return pl.BlockSpec(memory_space=space)


def shared(slots, entries, out, tile, place, used, seen, mark, sems, mark_sems, column, target_of, pick_of):
    mark[...] = jnp.full(mark.shape, ABSENT, mark.dtype)
    for s in range(slots):
        used[s] = 0
        seen[s] = 0
    for j in range(entries):
        t = target_of(j)
        rank = seen[t]
        seen[t] = rank + 1
        slot = ((t >> 2) * 2 + (t & 1)) * CAP + jnp.minimum(rank, CAP - 1)
        place[j] = jnp.where(((t >> 1) & 1) == column, slot, -1)

        @pl.when(place[j] >= 0)
        def _(j=j):
            used[place[j]] = 1
            pltpu.make_async_copy(tile.at[pl.ds(pl.multiple_of(pick_of(j) * BLOCK, BLOCK), BLOCK)], out.at[place[j]], sems.at[j]).start()

    rows, lanes = mark.shape
    for s in range(slots):
        @pl.when(used[s] == 0)
        def _(s=s):
            pltpu.make_async_copy(mark, out.at[s, pl.ds(0, rows), pl.ds(0, lanes)], mark_sems.at[s]).start()

    def finish():
        for j in range(entries):
            @pl.when(place[j] >= 0)
            def _(j=j):
                pltpu.make_async_copy(tile.at[pl.ds(pl.multiple_of(pick_of(j) * BLOCK, BLOCK), BLOCK)], out.at[place[j]], sems.at[j]).wait()

        for s in range(slots):
            @pl.when(used[s] == 0)
            def _(s=s):
                pltpu.make_async_copy(mark, out.at[s, pl.ds(0, rows), pl.ds(0, lanes)], mark_sems.at[s]).wait()

    return finish


def own_kernel(entries, me, targets, picks, rtl, out, mail, target_s, pick_s, tile, head, place, used, seen, mark, sems, mark_sems, in_sems):
    lists = [pltpu.make_async_copy(targets, target_s, in_sems.at[0]), pltpu.make_async_copy(picks, pick_s, in_sems.at[1])]
    load = pltpu.make_async_copy(rtl, tile, in_sems.at[2])
    for copy in lists + [load]:
        copy.start()
    for copy in lists:
        copy.wait()
    load.wait()
    size = tile.shape[0]
    store = pltpu.make_async_copy(tile, mail.at[pl.ds(0, size)], in_sems.at[3])
    store.start()
    column = (me[0] >> 1) & 1
    finish = shared(out.shape[0], entries, out, tile, place, used, seen, mark, sems, mark_sems, column, lambda j: target_s[j], lambda j: pick_s[j])
    lane = lax.broadcasted_iota(jnp.int32, head.shape, 1)
    line = jnp.zeros(head.shape, jnp.int32)
    for j in range(entries):
        line = jnp.where(lane == j, target_s[j], line)
        line = jnp.where(lane == entries + j, pick_s[j], line)
    head[...] = line.astype(jnp.float32).astype(head.dtype)
    rows, lanes = head.shape
    note = pltpu.make_async_copy(head, mail.at[pl.ds(size, rows), pl.ds(0, lanes)], in_sems.at[4])
    note.start()
    finish()
    store.wait()
    note.wait()


def pack_own(me, targets, picks, tile, places):
    entries = targets.shape[0]
    rows, feature = tile.shape
    slots = places * CAP
    hbm = whole(pltpu.HBM)
    return pl.pallas_call(
        functools.partial(own_kernel, entries),
        out_shape=(jax.ShapeDtypeStruct((slots, BLOCK, feature), tile.dtype), jax.ShapeDtypeStruct((rows + 16, feature), tile.dtype)),
        in_specs=[whole(pltpu.SMEM), hbm, hbm, hbm],
        out_specs=(hbm, hbm),
        scratch_shapes=[
            pltpu.SMEM((entries,), jnp.int32),
            pltpu.SMEM((entries,), jnp.int32),
            pltpu.VMEM(tile.shape, tile.dtype),
            pltpu.VMEM((16, 128), tile.dtype),
            pltpu.SMEM((entries,), jnp.int32),
            pltpu.SMEM((slots,), jnp.int32),
            pltpu.SMEM((slots,), jnp.int32),
            pltpu.VMEM((16, 128), tile.dtype),
            pltpu.SemaphoreType.DMA((entries,)),
            pltpu.SemaphoreType.DMA((slots,)),
            pltpu.SemaphoreType.DMA((5,)),
        ],
        compiler_params=pltpu.CompilerParams(vmem_limit_bytes=BIG_GRANT),
        name="pack_own",
    )(me, targets, picks, tile)


def far_kernel(entries, me, mail, out, list_v, list_s, place, used, seen, mark, sems, mark_sems, in_sems):
    size = mail.shape[0] - 16
    list_v[...] = mail[size : size + 8, :128].astype(jnp.float32).astype(jnp.int32)
    down = pltpu.make_async_copy(list_v, list_s, in_sems.at[0])
    down.start()
    down.wait()
    column = (me[0] >> 1) & 1
    shared(out.shape[0], entries, out, mail, place, used, seen, mark, sems, mark_sems, column, lambda j: list_s[0, j], lambda j: list_s[0, entries + j])()


def pack_far(me, mail, places, entries):
    rows, feature = mail.shape
    slots = places * CAP
    return pl.pallas_call(
        functools.partial(far_kernel, entries),
        out_shape=jax.ShapeDtypeStruct((slots, BLOCK, feature), mail.dtype),
        in_specs=[whole(pltpu.SMEM), whole()],
        out_specs=whole(pltpu.HBM),
        scratch_shapes=[
            pltpu.VMEM((8, 128), jnp.int32),
            pltpu.SMEM((8, 128), jnp.int32),
            pltpu.SMEM((entries,), jnp.int32),
            pltpu.SMEM((slots,), jnp.int32),
            pltpu.SMEM((slots,), jnp.int32),
            pltpu.VMEM((16, 128), mail.dtype),
            pltpu.SemaphoreType.DMA((entries,)),
            pltpu.SemaphoreType.DMA((slots,)),
            pltpu.SemaphoreType.DMA((1,)),
        ],
        compiler_params=pltpu.CompilerParams(vmem_limit_bytes=FAR_GRANT),
        name="pack_far",
    )(me, mail)


def cycle_kernel(rate, scale, tiles, given, end, q_ref, *refs):
    q = q_ref[...]
    rows, feature = q.shape
    first = pl.multiple_of(pl.program_id(0) * rows, rows)
    keys = [ref[...] for ref in refs[:tiles]]
    scores = [nt_dot(q, k) for k in keys]
    states = refs[tiles : tiles + given]
    peaks = [jnp.max(s, axis=1, keepdims=True) for s in scores] + [state[:, feature : feature + 1] for state in states]
    m = functools.reduce(jnp.maximum, peaks)
    l = jnp.zeros((rows, 1), jnp.float32)
    num = jnp.zeros((rows, feature), jnp.float32)
    for s, k in zip(scores, keys):
        e = jnp.exp2((s - m) * rate)
        l += jnp.sum(e, axis=1, keepdims=True)
        num += jnp.dot(e.astype(jnp.bfloat16), k, preferred_element_type=jnp.float32)
    for state in states:
        shrink = jnp.exp2((state[:, feature : feature + 1] - m) * rate)
        l += state[:, feature + 1 : feature + 2] * shrink
        num += state[:, :feature] * shrink
    lane = lax.broadcasted_iota(jnp.int32, (rows, LANES), 1)
    if not end:
        state_ref = refs[-1]
        if given:
            positive = states[0][:, feature + 2 : feature + 3]
        else:
            own = refs[0][pl.ds(first, rows), :].astype(jnp.float32)
            positive = jnp.sum(q.astype(jnp.float32) * own, axis=1, keepdims=True)
        state_ref[:, :feature] = num
        state_ref[:, feature:] = jnp.where(lane == 0, m, jnp.where(lane == 1, l, positive))
        return
    positive = states[0][:, feature + 2 : feature + 3]
    own_ref, grad_ref, loss_ref, stats_ref = refs[tiles + given :]
    inverse = 1.0 / l
    grad_ref[...] = (num * inverse - own_ref[...].astype(jnp.float32)) * scale
    loss = (m - positive) * scale + jnp.log(l)
    table = jnp.where(lane == 0, m, jnp.where(lane == 1, inverse, loss))
    flipped = table.T
    stats_ref[...] = flipped[:8]
    loss_ref[...] = flipped[2:3]


def cycle_part(rate, scale, q, keys, states=(), own=None, rows=256):
    n, feature = q.shape
    f32 = jnp.float32
    tiles = len(keys)
    block = pl.BlockSpec((rows, feature), lambda i: (i, 0))
    wide = pl.BlockSpec((rows, feature + LANES), lambda i: (i, 0))
    full = pl.BlockSpec((n, feature), lambda i: (0, 0), pipeline_mode=pl.Buffered(1))
    end = own is not None
    args, specs = [q, *keys, *states], [block] + [full] * tiles + [wide] * len(states)
    shapes, outs = jax.ShapeDtypeStruct((n, feature + LANES), f32), wide
    if end:
        args, specs = args + [own], specs + [block]
        shapes = (jax.ShapeDtypeStruct((n, feature), f32), jax.ShapeDtypeStruct((1, n), f32), jax.ShapeDtypeStruct((8, n), f32))
        outs = (block, pl.BlockSpec((1, rows), lambda i: (0, i)), pl.BlockSpec((8, rows), lambda i: (0, i)))
    return pl.pallas_call(
        functools.partial(cycle_kernel, rate, scale, tiles, len(states), end),
        grid=(n // rows,),
        out_shape=shapes,
        in_specs=specs,
        out_specs=outs,
        compiler_params=pltpu.CompilerParams(vmem_limit_bytes=VMEM_LIMIT),
        cost_estimate=pl.CostEstimate(flops=4 * n * tiles * n * feature, bytes_accessed=8 * n * feature, transcendentals=tiles * n * n),
        name="cycle_last" if end else "cycle_more" if states else "cycle_own",
    )(*args)


def hard_kernel(rate, fresh, q_hbm, *refs):
    state_in = None if fresh else refs[0]
    blocks, state, q_ref, keys, scores, order, sems = refs[-7:]
    n, feature = q_ref.shape
    slots = blocks.shape[0]
    per = CHUNK // BLOCK
    load_keys = pltpu.make_async_copy(blocks, keys, sems.at[0])
    load_q = pltpu.make_async_copy(q_hbm, q_ref, sems.at[1])
    load_keys.start()
    load_q.start()
    if not fresh:
        load_state = pltpu.make_async_copy(state_in, state, sems.at[2])
        load_state.start()
    load_keys.wait()
    there = [(jnp.max(keys[s, :16, :128].astype(jnp.float32)) < ABSENT / 2).astype(jnp.int32) for s in range(slots)]
    live = jnp.int32(0)
    for s in range(slots):
        order[live] = s
        live += there[s]
    chunks = (live + per - 1) // per
    tail = order[jnp.maximum(live - 1, 0)]
    for p in range(per - 1):
        order[live + p] = tail

    def chunk_keys(i):
        return jnp.concatenate([keys[order[i * per + p]] for p in range(per)], axis=0)

    load_q.wait()
    q = q_ref[...]

    def score(i, m):
        s = nt_dot(q, chunk_keys(i))
        scores[i] = s
        for c in range(per):
            m = jnp.maximum(m, s[:, c * BLOCK : (c + 1) * BLOCK])
        return m

    wide = lax.fori_loop(0, chunks, score, jnp.full((n, BLOCK), -jnp.inf, jnp.float32))
    m = jnp.max(wide, axis=1, keepdims=True)
    if fresh:
        state[...] = jnp.zeros(state.shape, jnp.float32)
        kept = 0.0
    else:
        load_state.wait()
        old = state[:, feature : feature + 1]
        m = jnp.maximum(m, old)
        shrink = jnp.exp2((old - m) * rate)
        kept = state[:, feature + 1 : feature + 2] * shrink
        state[:, :feature] = state[:, :feature] * shrink
    for p in range(1, per):
        @pl.when(((chunks - 1) * per + p >= live) & (chunks > 0))
        def _(p=p):
            scores[chunks - 1, :, p * BLOCK : (p + 1) * BLOCK] = jnp.full((n, BLOCK), -jnp.inf, jnp.float32)

    def weigh(i, l):
        e = jnp.exp2((scores[i] - m) * rate)
        state[:, :feature] += jnp.dot(e.astype(jnp.bfloat16), chunk_keys(i), preferred_element_type=jnp.float32)
        for c in range(per):
            l = l + e[:, c * BLOCK : (c + 1) * BLOCK]
        return l

    l = lax.fori_loop(0, chunks, weigh, jnp.zeros((n, BLOCK), jnp.float32))
    total = jnp.sum(l, axis=1, keepdims=True) + kept
    lane = lax.broadcasted_iota(jnp.int32, (n, LANES), 1)
    state[:, feature:] = jnp.where(lane == 0, m, jnp.where(lane == 1, total, state[:, feature:]))


def hard_part(rate, q, states, blocks, name):
    n, feature = q.shape
    slots = blocks.shape[0]
    f32 = jnp.float32
    keys = slots * BLOCK
    return pl.pallas_call(
        functools.partial(hard_kernel, rate, not states),
        out_shape=jax.ShapeDtypeStruct((n, feature + LANES), f32),
        in_specs=[whole(pl.ANY)] * (2 + len(states)),
        out_specs=whole(),
        scratch_shapes=[
            pltpu.VMEM(q.shape, q.dtype),
            pltpu.VMEM(blocks.shape, blocks.dtype),
            pltpu.VMEM((keys // CHUNK, n, CHUNK), f32),
            pltpu.SMEM((slots + CHUNK // BLOCK,), jnp.int32),
            pltpu.SemaphoreType.DMA((3,)),
        ],
        compiler_params=pltpu.CompilerParams(vmem_limit_bytes=HARD_GRANT),
        cost_estimate=pl.CostEstimate(flops=2 * n * keys * feature, bytes_accessed=2 * keys * feature, transcendentals=n * keys // 2),
        name=name,
    )(q, *states, blocks)


def rtl_kernel(rate, scale, tiles, k_ref, *refs):
    n_refs, s_refs = refs[:tiles], refs[tiles : 2 * tiles]
    base_ref, out_ref = refs[2 * tiles :]
    k = k_ref[...]
    total = -base_ref[...].astype(jnp.float32) if tiles == 1 else base_ref[...]
    for n_ref, s_ref in zip(n_refs, s_refs):
        rows = n_ref[...]
        s = nt_dot(k, rows)
        w = jnp.exp2((s - s_ref[0:1, :]) * rate) * s_ref[1:2, :]
        total += jnp.dot(w.astype(jnp.bfloat16), rows, preferred_element_type=jnp.float32)
    out_ref[...] = total if tiles == 1 else total * scale


def rtl_part(rate, scale, k, nets, stats, base, rows=256):
    n, feature = k.shape
    tiles = len(nets)
    block = pl.BlockSpec((rows, feature), lambda i: (i, 0))
    full = pl.BlockSpec((n, feature), lambda i: (0, 0), pipeline_mode=pl.Buffered(1))
    stat = pl.BlockSpec((8, n), lambda i: (0, 0), pipeline_mode=pl.Buffered(1))
    return pl.pallas_call(
        functools.partial(rtl_kernel, rate, scale, tiles),
        grid=(n // rows,),
        out_shape=jax.ShapeDtypeStruct((n, feature), jnp.float32),
        in_specs=[block] + [full] * tiles + [stat] * tiles + [block],
        out_specs=block,
        compiler_params=pltpu.CompilerParams(vmem_limit_bytes=VMEM_LIMIT),
        cost_estimate=pl.CostEstimate(flops=4 * n * tiles * n * feature, bytes_accessed=(tiles + 3) * n * feature * 2, transcendentals=tiles * n * n),
        name="rtl_own" if tiles == 1 else "rtl_others",
    )(k, *nets, *stats, base)


def body(netlist, rtl, hard_target, hard_block):
    queries = netlist[0]
    own_keys = rtl[0]
    feature = queries.shape[1]
    scale = 3.0 / math.sqrt(feature)
    rate = scale * math.log2(math.e)
    groups = lax.axis_size("dp")
    targets = hard_target[0, 0, :, 0]
    picks = hard_block[0, 0]
    columns = [[g for g in range(groups) if (g // 2) % 2 == x] for x in range(2)]
    places = groups // 2

    def spread(packed):
        return lax.all_to_all(packed, "dp", split_axis=0, concat_axis=0, axis_index_groups=columns, tiled=True)

    at = jnp.full((1,), lax.axis_index("dp"), jnp.int32)
    packed, mail = pack_own(at, targets, picks, own_keys, places)
    first = spread(packed)
    mail = lax.ppermute(mail, "dp", [(g, g ^ 2) for g in range(groups)])
    rtl1 = passed_along(own_keys, "loop", 1)
    mail, rtl1, back = lax.optimization_barrier((mail, rtl1, queries))
    second = spread(pack_far(at, mail, places, targets.shape[0]))
    rtl2 = passed_along(rtl1, "loop", 1)
    net1 = passed_along(back, "loop", -1)

    state = cycle_part(rate, scale, queries, [own_keys, rtl1])
    state = hard_part(rate, queries, [state], first, "hard_first")
    net1, state = lax.optimization_barrier((net1, state))
    net2 = passed_along(net1, "loop", -1)
    state = cycle_part(rate, scale, queries, [rtl2], [state])
    others = hard_part(rate, queries, [], second, "hard_second")
    grad, loss, stats = cycle_part(rate, scale, queries, [], [state, others], own_keys)
    stats1 = passed_along(stats, "loop", -1)
    stats2 = passed_along(stats, "loop", -2)
    begun = rtl_part(rate, scale, own_keys, [queries], [stats], queries)
    net1, begun = lax.optimization_barrier((net1, begun))
    net1 = jnp.where(at < 0, queries, net1)
    rtl_grad = rtl_part(rate, scale, own_keys, [net1, net2], [stats1, stats2], begun)
    return (loss, grad[None], rtl_grad[None])


def solution(mesh):
    return jax.shard_map(
        body,
        mesh=mesh,
        in_specs=(
            P("dp", "loop", None),
            P("dp", "loop", None),
            P("dp", "loop", None, None),
            P("dp", "loop", None),
        ),
        out_specs=(P("dp", "loop"), P("dp", "loop", None), P("dp", "loop", None)),
        check_vma=False,
    )
```
